32 devices in a mesh: groups: 2 (over y), slab: 4 (over z), pencil: 2 (over x), comp: 2 (over core).
Axes of the slice: x: 2, y: 2, z: 4, core: 2. Of those that a mesh axis runs over, the one named last changes fastest.
Arguments:
- u_start: float32 [3, 64, 64, 512], P(None, ('groups', 'slab'), 'pencil', 'comp'), parts along dimension 1, may hold values from -6 to 6
- toughness: float32 [64, 64, 512], P(('groups', 'slab'), 'pencil', 'comp'), parts along dimension 0, may hold values from 0.3 to 1.5
- crack_label: int32 [64, 64, 512], P(('groups', 'slab'), 'pencil', 'comp'), parts along dimension 0, may hold values from 0 to 2
- obs_weight: bfloat16 [32, 64, 2, 4096], P('slab', 'pencil', 'comp'), may hold values from -0.75 to 0.75
- sensor_cell: int32 [4096], replicated, may hold values from 0 to 4095
Outputs:
- moved: float32 [3, 64, 64, 512], P(None, ('groups', 'slab'), 'pencil', 'comp'), parts along dimension 1
- damage: float32 [64, 64, 512], P(('groups', 'slab'), 'pencil', 'comp'), parts along dimension 0
- readings: float32 [3, 8192], P(None, 'groups'), parts along dimension 1
The draws below stay inside these ranges and needn't reach their ends.
There are 2 independent parts, one for each index of `groups`. The reference program is written for one: setup_inputs(seed, part) draws one part's arguments, and reference() takes and returns one part's arrays. A program takes and returns all parts, laid end to end along the dimension named above; an argument that names none is the same for every part. Nothing has to cross between parts.
Inputs may be any that keep to these rules, and one draw needn't show every extreme that they name: `sensor_cell`: numbers cell blocks as (64 z + y) * 2 + h. `crack_label`: 0 intact, 1 partly cracked, 2 cracked.
All inputs are finite; a program needn't handle non-finite values.
Results may differ from the reference program's by a relative error of at most 0.003.
Values sent between devices are 32-bit elements; how exact they have to be, the bound alone decides.
No kernel may reach another device: no remote copies, remote signals or barrier semaphores. Data moves between devices by JAX's collectives and lax.ppermute only.
A program may use at most 128 MiB of HBM per device.

```python
import math
import jax
import jax.numpy as jnp

CX = 256
SENSORS = 4096
NZ = 32
NY = 64
NX = 512
BLOCKS = 4096
N_COMP = 2


def set_ends(array, rng, least, largest):
    longest = array.shape.index(max(array.shape))
    spots = []
    for shift in (0, 1):
        where = [jax.random.randint(jax.random.fold_in(rng, axis), (), 0, length) for axis, length in enumerate(array.shape)]
        where[longest] = (where[longest] + shift) % array.shape[longest]
        spots.append(tuple(where))
    return array.at[spots[0]].set(least).at[spots[1]].set(largest)


def steps_of(key, extent, cuts, low, largest):
    def one(dim, shards_of):
        heights = jax.random.uniform(jax.random.fold_in(jax.random.fold_in(key, 6), dim), (shards_of,), jnp.float32, low / len(cuts), largest / len(cuts))
        return jnp.repeat(jnp.exp(heights), extent[dim] // shards_of).reshape((-1,) + (1,) * (len(extent) - dim - 1))

    gain = one(*cuts[0])
    for cut in cuts[1:]:
        gain = gain * one(*cut)
    return gain


def normal_values(stream_key, extent, width, limit, cuts=(), held_as=jnp.bfloat16):
    loudness = steps_of(stream_key, extent, cuts, -0.22, 0.18) if cuts else 1.0
    array = jax.random.normal(stream_key, extent, jnp.float32) * width * loudness
    return jnp.minimum(jnp.maximum(array, -limit), limit).astype(held_as)


def setup_inputs(seed: int = 0, part: int = 0) -> dict:
    key_list = jax.random.split(jax.random.key(seed), 6)
    part_splits = jax.random.split(jax.random.fold_in(key_list[5], part), 6)
    u_start = normal_values(part_splits[0], (3, NZ, NY, NX), 1.0, 6.0, ((1, 4), (2, 2), (3, 2)), jnp.float32)
    toughness = jnp.clip(jnp.exp(math.log(1.5) - 1.60943787 * jax.random.uniform(part_splits[1], (NZ, NY, NX), jnp.float32) ** steps_of(part_splits[1], (NZ, NY, NX), ((0, 4), (1, 2), (2, 2)), -0.2, 0.2)), 0.3, 1.5)
    crack_label = set_ends(jax.random.randint(part_splits[2], (NZ, NY, NX), 0, 3), jax.random.fold_in(part_splits[2], 1), 0, 2).astype(jnp.int32)
    obs_weight = normal_values(key_list[3], (NZ, NY, N_COMP, SENSORS), (BLOCKS // 64) ** -0.5, 0.75, ((0, 4), (1, 2), (2, 2)))
    sensor_cell = set_ends(jax.random.randint(key_list[4], (SENSORS,), 0, BLOCKS), jax.random.fold_in(key_list[4], 1), 0, BLOCKS - 1).astype(jnp.int32)
    return dict(u_start=u_start, toughness=toughness, crack_label=crack_label, obs_weight=obs_weight, sensor_cell=sensor_cell)


SHEAR_MODULUS = 1.0
LAME_FIRST = 1.5
RESIDUAL_STIFF = 0.001
TIME_DISP = 0.15
TIME_DAMAGE = 0.08
LENGTH_SCALE = 1.0
DAMAGE_LEVEL = 0.45
POINT_GAIN = 8.0


def central(source, spatial):
    if spatial == 0:
        return 0.5 * (source[..., 2:, 1:-1, 1:-1] - source[..., :-2, 1:-1, 1:-1])
    if spatial == 1:
        return 0.5 * (source[..., 1:-1, 2:, 1:-1] - source[..., 1:-1, :-2, 1:-1])
    return 0.5 * (source[..., 1:-1, 1:-1, 2:] - source[..., 1:-1, 1:-1, :-2])


def shrink(source):
    return source[..., 1:-1, 1:-1, 1:-1]


def laplace(source):
    return (source[2:, 1:-1, 1:-1] + source[:-2, 1:-1, 1:-1] + source[1:-1, 2:, 1:-1]
            + source[1:-1, :-2, 1:-1] + source[1:-1, 1:-1, 2:] + source[1:-1, 1:-1, :-2]
            - 6.0 * source[1:-1, 1:-1, 1:-1])


def entry_key(first, second):
    return (min(first, second), max(first, second))


def rotate(matrix, first, second):
    other = 3 - first - second
    diag_first = matrix[(first, first)]
    diag_second = matrix[(second, second)]
    coupling = matrix[(first, second)]
    angle = 0.5 * jnp.arctan2(2.0 * coupling, diag_second - diag_first)
    cosine = jnp.cos(angle)
    sine = jnp.sin(angle)
    side_first = matrix[entry_key(other, first)]
    side_second = matrix[entry_key(other, second)]
    result = dict(matrix)
    result[(first, first)] = cosine * cosine * diag_first - 2.0 * cosine * sine * coupling + sine * sine * diag_second
    result[(second, second)] = sine * sine * diag_first + 2.0 * cosine * sine * coupling + cosine * cosine * diag_second
    result[(first, second)] = jnp.zeros_like(coupling)
    result[entry_key(other, first)] = cosine * side_first - sine * side_second
    result[entry_key(other, second)] = sine * side_first + cosine * side_second
    return result


def eigenvalues(matrix):
    for sweep_index in range(5):
        for first, second in ((0, 1), (0, 2), (1, 2)):
            matrix = rotate(matrix, first, second)
    return [matrix[(0, 0)], matrix[(1, 1)], matrix[(2, 2)]]


def advance(padded_disp, padded_damage, toughness):
    gradient = [[central(padded_disp[component], direction) for direction in range(3)] for component in range(3)]
    strain = {}
    for first in range(3):
        for second in range(first, 3):
            strain[(first, second)] = 0.5 * (gradient[first][second] + gradient[second][first])
    trace_full = strain[(0, 0)] + strain[(1, 1)] + strain[(2, 2)]
    damage_mid = shrink(padded_damage)
    degrade = (1.0 - damage_mid) ** 2 + RESIDUAL_STIFF
    divergence = []
    for component in range(3):
        total_force = 0.0
        for direction in range(3):
            stress = 2.0 * SHEAR_MODULUS * strain[entry_key(component, direction)]
            if component == direction:
                stress = stress + LAME_FIRST * trace_full
            total_force = total_force + central(degrade * stress, direction)
        divergence.append(total_force)
    moved = shrink(shrink(padded_disp)) + TIME_DISP * jnp.stack(divergence)
    inner = {key_pair: shrink(entry_value) for key_pair, entry_value in strain.items()}
    trace_inner = shrink(trace_full)
    energy = 0.5 * LAME_FIRST * jnp.maximum(trace_inner, 0.0) ** 2
    for eigen_value in eigenvalues(inner):
        energy = energy + SHEAR_MODULUS * jnp.maximum(eigen_value, 0.0) ** 2
    damage_core = shrink(damage_mid)
    damage = damage_core + TIME_DAMAGE * (2.0 * (1.0 - damage_core) * energy
                                          - toughness / LENGTH_SCALE * damage_core
                                          + toughness * LENGTH_SCALE * laplace(damage_mid))
    return moved, damage


def reference(u_start, toughness, crack_label, obs_weight, sensor_cell):
    damage = DAMAGE_LEVEL * crack_label.astype(jnp.float32)
    moved = u_start
    for repeat in range(2):
        padded_disp = jnp.pad(moved, ((0, 0), (2, 2), (2, 2), (2, 2)))
        padded_damage = jnp.pad(damage, 2)
        moved, damage = advance(padded_disp, padded_damage, toughness)
    pooled = jnp.mean(moved.reshape(3, NZ, NY, N_COMP, CX), axis=-1)
    pooled = pooled.reshape(3, NZ * NY * N_COMP).astype(jnp.bfloat16)
    dense = jnp.dot(pooled, obs_weight.reshape(NZ * NY * N_COMP, SENSORS), preferred_element_type=jnp.float32)
    point = pooled.astype(jnp.float32)[:, sensor_cell]
    readings = dense + POINT_GAIN * point
    return moved, damage, readings
```

```python
import functools

import jax
import jax.numpy as jnp
from jax import lax
from jax.experimental import pallas as pl
from jax.experimental.pallas import tpu as pltpu
from jax.sharding import PartitionSpec as P

SHEAR_MODULUS = 1.0
LAME_FIRST = 1.5
RESIDUAL_STIFF = 0.001
TIME_DISP = 0.15
TIME_DAMAGE = 0.08
DAMAGE_LEVEL = 0.45
POINT_GAIN = 8.0
LANES = 128
SUB = 8
COS_THIRD = (
    0.5000000037331834,
    0.5773496613984853,
    -0.11109449276880777,
    0.05327935086024303,
    -0.031925412185213546,
    0.01960032102518762,
    -0.010237508432464154,
    0.003654119632233793,
    -0.0006260453394989179,
)
F32 = jnp.float32
VMEM = pl.BlockSpec(memory_space=pltpu.VMEM)


def positive_square_sum(m00, m11, m22, m01, m02, m12):
    mean = (m00 + m11 + m22) * (1.0 / 3.0)
    b00, b11, b22 = m00 - mean, m11 - mean, m22 - mean
    s01, s02, s12 = m01 * m01, m02 * m02, m12 * m12
    p2 = (b00 * b00 + b11 * b11 + b22 * b22) * (1.0 / 6.0) + (s01 + s02 + s12) * (1.0 / 3.0)
    det = b00 * (b11 * b22 - s12) + 2.0 * (m01 * m02) * m12 - b11 * s02 - b22 * s01
    mean2 = mean * mean
    whole = mean * (mean2 - 3.0 * p2) + det
    up = whole >= 0.0
    safe = jnp.maximum(p2, 1e-24)
    inv = lax.rsqrt(safe)
    p = safe * inv
    half = 0.25 * (det * inv) * (inv * inv)
    half = jnp.where(up, half, -half) + 0.5
    half = jnp.minimum(jnp.maximum(half, 0.0), 1.0)
    t = jnp.sqrt(half)
    c = jnp.full_like(t, COS_THIRD[-1])
    for value in COS_THIRD[-2::-1]:
        c = c * t + value
    pc = p * c
    lead = jnp.where(up, mean, -mean)
    largest = lead + 2.0 * pc
    square = largest * largest
    norm = 6.0 * p2 + 3.0 * mean2
    rest = lead - pc
    return jnp.where(
        up, jnp.where(rest > 0.0, norm, square), jnp.where(rest < 0.0, norm - square, 0.0)
    )


def emit_payloads(merged, py, u, d, zup, zdn, ys, dgs):
    _, Z, Y, X = u.shape
    for c in range(3):
        zup[2 * c : 2 * c + 2] = u[c, Z - 2 : Z]
        zdn[2 * c : 2 * c + 2] = u[c, 0:2]
    zup[6] = d[Z - 1]
    zdn[6] = d[0]

    def rows(side, c, layer, zs):
        row = Y - 2 + layer if side > 0 else layer
        return u[c, zs, row, :]

    def pick(fn):
        if merged:
            first = py == 0
            return [jnp.where(first, fn(1), fn(-1))]
        return [fn(1), fn(-1)]

    full = slice(0, Z)
    for c in range(3):
        for layer in range(2):
            for ref, value in zip(ys, pick(lambda s: rows(s, c, layer, full))):
                ref[2 * c + layer] = value
    for ref, value in zip(ys, pick(lambda s: d[:, Y - 1 if s > 0 else 0, :])):
        ref[6] = value
    n = len(ys)
    for k, zs in enumerate((slice(Z - 1, Z), slice(0, 1))):
        for c in range(3):
            for j, value in enumerate(
                pick(lambda s: rows(s, c, 1 if s > 0 else 0, zs))
            ):
                dgs[k * n + j][c : c + 1, :] = value


def payload_shapes(Z, Y, X, n):
    return (
        [jax.ShapeDtypeStruct((7, Y, X), F32)] * 2
        + [jax.ShapeDtypeStruct((7, Z, X), F32)] * n
        + [jax.ShapeDtypeStruct((SUB, X), F32)] * (2 * n)
    )


def pack_kernel(merged, n, u, label, d0, zup, zdn, *rest):
    d0[...] = DAMAGE_LEVEL * label[...].astype(F32)
    emit_payloads(merged, lax.axis_index("pencil"), u, d0, zup, zdn, rest[:n], rest[n:])


def xpack_kernel(merged, u, d, zlo, zhi, ylo, yhi, out):
    _, Z, Y, X = u.shape
    left = lax.axis_index("comp") == 0
    lane = lax.broadcasted_iota(jnp.int32, (Y, LANES), 1)
    slot = jnp.where(left, (lane + 2) // 2 % (LANES // 2), lane // 2)

    def side(ref, *at):
        return jnp.where(left, ref[at + (slice(X - LANES, X),)], ref[at + (slice(0, LANES),)])

    acc = jnp.zeros((Y, LANES), F32)
    entry = 0
    for c in range(3):
        for z in range(-1, Z + 1):
            if z < 0:
                tile = side(zlo, 2 * c + 1, slice(None))
            elif z == Z:
                tile = side(zhi, 2 * c, slice(None))
            else:
                tile = side(u, c, z, slice(None))
            acc = jnp.where(slot == entry, pltpu.roll(tile, 2 * entry, 1), acc)
            entry += 1
    for z in range(Z):
        acc = jnp.where(slot == entry, pltpu.roll(side(d, z, slice(None)), 2 * entry, 1), acc)
        entry += 1
    out[0:Y, :] = jnp.where(left, pltpu.roll(acc, 2, 1), acc)
    acc = jnp.zeros((Z, LANES), F32)
    entry = 0
    for ref, layer in ((ylo, 1), (yhi, 0)):
        for c in range(3):
            tile = side(ref, 2 * c + layer, slice(None))
            acc = jnp.where(slot[0:Z] == entry, pltpu.roll(tile, 2 * entry, 1), acc)
            entry += 1
    out[Y : Y + Z, :] = jnp.where(left, pltpu.roll(acc, 2, 1), acc)


def gather_blocks(merged, refs, U, D):
    u, d, zlo, zhi, ylo, yhi, dgs, xh = refs
    _, Z, Y, X = u.shape
    H = SUB
    py = lax.axis_index("pencil")
    left = lax.axis_index("comp") == 0
    lo_ok = py != 0 if merged else None
    hi_ok = py == 0 if merged else None

    def keep(ok, value):
        return value if ok is None else jnp.where(ok, value, 0.0)

    lane = lax.broadcasted_iota(jnp.int32, (Y, LANES), 1)
    inside = jnp.where(left, lane, LANES - 1 - lane) < 2
    packet = xh[0:Y, :]
    packet = jnp.where(left, packet, pltpu.roll(packet, LANES - 2, 1))
    edge = xh[Y : Y + Z, :]
    edge = jnp.where(left, edge, pltpu.roll(edge, LANES - 2, 1))

    def column(source, entry):
        shift = (LANES - 2 * entry) % LANES
        moved = pltpu.roll(source, shift, 1) if shift else source
        return jnp.where(inside[0 : source.shape[0]], moved, 0.0)

    entry = 0
    for c in range(3):
        U[c, 2 : Z + 2, H : H + Y, 0:X] = u[c]
        U[c, 0:2, H : H + Y, 0:X] = zlo[2 * c : 2 * c + 2]
        U[c, Z + 2 : Z + 4, H : H + Y, 0:X] = zhi[2 * c : 2 * c + 2]
        for z in range(-1, Z + 1):
            U[c, z + 2, H : H + Y, X : X + LANES] = column(packet, entry)
            entry += 1
        for layer in range(2):
            low = keep(lo_ok, ylo[2 * c + layer])
            high = keep(hi_ok, yhi[2 * c + layer])
            for z in range(Z):
                U[c, z + 2, H - 2 + layer : H - 1 + layer, 0:X] = low[z : z + 1]
                U[c, z + 2, H + Y + layer : H + Y + layer + 1, 0:X] = high[z : z + 1]
        low, high = keep(lo_ok, column(edge, c)), keep(hi_ok, column(edge, 3 + c))
        for z in range(Z):
            U[c, z + 2, H - 1 : H, X : X + LANES] = low[z : z + 1]
            U[c, z + 2, H + Y : H + Y + 1, X : X + LANES] = high[z : z + 1]
        n = len(dgs) // 2
        for k, zi in ((0, 1), (1, Z + 2)):
            from_low = dgs[k * n][c : c + 1, :]
            from_high = dgs[k * n + n - 1][c : c + 1, :]
            U[c, zi, H - 1 : H, 0:X] = keep(lo_ok, from_low)
            U[c, zi, H + Y : H + Y + 1, 0:X] = keep(hi_ok, from_high)
    D[1 : Z + 1, H : H + Y, 0:X] = d[...]
    D[0, H : H + Y, 0:X] = zlo[6]
    D[Z + 1, H : H + Y, 0:X] = zhi[6]
    low, high = keep(lo_ok, ylo[6]), keep(hi_ok, yhi[6])
    for z in range(Z):
        D[z + 1, H : H + Y, X : X + LANES] = column(packet, entry)
        D[z + 1, H - 1 : H, 0:X] = low[z : z + 1]
        D[z + 1, H + Y : H + Y + 1, 0:X] = high[z : z + 1]
        entry += 1


def ahead(value):
    return pltpu.roll(value, value.shape[-1] - 1, value.ndim - 1)


def behind(value):
    return pltpu.roll(value, 1, value.ndim - 1)


def step_kernel(merged, n, last, *refs):
    u, d, tough, zlo, zhi = refs[:5]
    rest = list(refs[5:])
    take = lambda k: [rest.pop(0) for _ in range(k)]
    ys, dgs, (xh,) = take(n), take(2 * n), take(1)
    if last:
        weight, sensor = take(2)
    moved, damage = take(2)
    if last:
        (part,) = take(1)
    else:
        zup, zdn, *out = take(2 + 3 * n)
    U, D, S = take(3)
    _, Z, Y, X = u.shape
    H = SUB
    gather_blocks(merged, (u, d, zlo, zhi, ys[0], ys[-1], dgs, xh), U, D)
    zz, zy, zx, yy, yx, xx = range(6)
    tiles = Y // SUB

    def gradients(zi, r):
        at = slice(r, r + SUB)
        gz, gy, gx = [], [], []
        for c in range(3):
            gz.append(U[c, zi + 1, at, :] - U[c, zi - 1, at, :])
            gy.append(U[c, zi, r + 1 : r + SUB + 1, :] - U[c, zi, r - 1 : r + SUB - 1, :])
            mid = U[c, zi, at, :]
            gx.append(ahead(mid) - behind(mid))
        return gz, gy, gx

    def stiffness(zi, r):
        keep = 1.0 - D[zi - 1, r : r + SUB, :]
        return 0.5 * (keep * keep + RESIDUAL_STIFF)

    def put(key, zi, r, value, width):
        S[key, zi - 1, r : r + SUB, 0:width] = value[:, 0:width]

    def z_face(zi):
        for t in range(1, tiles + 1):
            r = t * SUB
            gz, gy, gx = gradients(zi, r)
            h = stiffness(zi, r)
            total = LAME_FIRST * (gz[0] + gy[1] + gx[2])
            put(zz, zi, r, h * (total + 2.0 * gz[0]), X)
            put(zy, zi, r, h * (gy[0] + gz[1]), X)
            put(zx, zi, r, h * (gx[0] + gz[2]), X)

    z_face(1)
    z_face(Z + 2)

    @pl.loop(2, Z + 2)
    def _(zi):
        for t in (0, tiles + 1):
            r = t * SUB
            at = slice(r, r + SUB)
            row = H - 1 if t == 0 else H + Y
            one = slice(row, row + 1)
            gz, gy, gx = [], [], []
            for c in range(3):
                gz.append(U[c, zi + 1, one, :] - U[c, zi - 1, one, :])
                gy.append(U[c, zi, row + 1 : row + 2, :] - U[c, zi, row - 1 : row, :])
                mid = U[c, zi, one, :]
                gx.append(ahead(mid) - behind(mid))
            keep = 1.0 - D[zi - 1, one, :]
            h = 0.5 * (keep * keep + RESIDUAL_STIFF)
            total = LAME_FIRST * (gz[0] + gy[1] + gx[2])
            for key, value in (
                (zy, gy[0] + gz[1]),
                (yy, total + 2.0 * gy[1]),
                (yx, gx[1] + gy[2]),
            ):
                S[key, zi - 1, one, 0:X] = (h * value)[:, 0:X]
        for t in range(1, tiles + 1):
            r = t * SUB
            gz, gy, gx = gradients(zi, r)
            h = stiffness(zi, r)
            trace = gz[0] + gy[1] + gx[2]
            total = LAME_FIRST * trace
            mzy, mzx, myx = gy[0] + gz[1], gx[0] + gz[2], gx[1] + gy[2]
            put(zz, zi, r, h * (total + 2.0 * gz[0]), X)
            put(yy, zi, r, h * (total + 2.0 * gy[1]), X)
            put(zy, zi, r, h * mzy, X)
            put(zx, zi, r, h * mzx, X + LANES)
            put(yx, zi, r, h * myx, X + LANES)
            put(xx, zi, r, h * (total + 2.0 * gx[2]), X + LANES)
            cut = lambda value: value[:, 0:X]
            squares = positive_square_sum(
                cut(gz[0]), cut(gy[1]), cut(gx[2]), 0.5 * cut(mzy), 0.5 * cut(mzx), 0.5 * cut(myx)
            )
            grow = jnp.maximum(cut(trace), 0.0)
            energy = (0.25 * 0.5 * LAME_FIRST) * (grow * grow) + (0.25 * SHEAR_MODULUS) * squares
            at = slice(r, r + SUB)
            mid = D[zi - 1, at, :]
            core = cut(mid)
            lap = (
                D[zi, at, 0:X]
                + D[zi - 2, at, 0:X]
                + D[zi - 1, r + 1 : r + SUB + 1, 0:X]
                + D[zi - 1, r - 1 : r + SUB - 1, 0:X]
                + cut(ahead(mid) + behind(mid))
                - 6.0 * core
            )
            own = slice((t - 1) * SUB, t * SUB)
            tgh = tough[zi - 2, own, :]
            damage[zi - 2, own, :] = core + TIME_DAMAGE * (
                2.0 * (1.0 - core) * energy + tgh * (lap - core)
            )

    pairs = ((zz, zy, zx), (zy, yy, yx), (zx, yx, xx))
    if last:
        pooled = rest[0]

    @pl.loop(2, Z + 2)
    def _(zi):
        for t in range(1, tiles + 1):
            r = t * SUB
            at = slice(r, r + SUB)
            own = slice((t - 1) * SUB, t * SUB)
            sums = []
            for c in range(3):
                kz, ky, kx = pairs[c]
                mid = S[kx, zi - 1, at, :]
                force = (
                    S[kz, zi, at, 0:X]
                    - S[kz, zi - 2, at, 0:X]
                    + S[ky, zi - 1, r + 1 : r + SUB + 1, 0:X]
                    - S[ky, zi - 1, r - 1 : r + SUB - 1, 0:X]
                    + (ahead(mid) - behind(mid))[:, 0:X]
                )
                new = u[c, zi - 2, own, :] + (0.5 * TIME_DISP) * force
                moved[c, zi - 2, own, :] = new
                if last:
                    sums.append(jnp.sum(new, axis=-1, keepdims=True))
            if last:
                lane = lax.broadcasted_iota(jnp.int32, (SUB, LANES), 1)
                value = jnp.where(lane == 0, sums[0], jnp.where(lane == 1, sums[1], sums[2]))
                start = pl.multiple_of((zi - 2) * Y + (t - 1) * SUB, SUB)
                pooled[pl.ds(start, SUB), :] = value

    if last:
        means = (pooled[...] * (1.0 / X)).T[0:SUB].astype(jnp.bfloat16)
        blocks = Z * Y
        count = lax.axis_size("comp")
        spread = Y * lax.axis_size("pencil")
        index = lax.broadcasted_iota(jnp.int32, (blocks, 1), 0)
        plane = lax.axis_index("slab") * Z + index // Y
        row = lax.axis_index("pencil") * Y + index % Y
        ids = (plane * spread + row) * count + lax.axis_index("comp")
        chunk = 8 * LANES
        S8 = lax.broadcasted_iota(jnp.int32, (SUB, LANES), 0)
        for k in range(sensor.shape[1] // chunk):
            cols = slice(k * chunk, (k + 1) * chunk)
            picks = jnp.where(ids == sensor[:, cols], POINT_GAIN, 0.0).astype(jnp.bfloat16)
            value = jnp.dot(means, weight[:, cols], preferred_element_type=F32)
            value = value + jnp.dot(means, picks, preferred_element_type=F32)
            for c in range(3):
                tile = jnp.zeros((SUB, LANES), F32)
                for j in range(8):
                    tile = jnp.where(
                        S8 == j, value[c : c + 1, j * LANES : (j + 1) * LANES], tile
                    )
                part[c, k] = tile
    else:
        emit_payloads(
            merged, lax.axis_index("pencil"), moved, damage, zup, zdn, out[:n], out[n:]
        )


def finish_kernel(count, *refs):
    out = refs[-1]
    total = refs[0][...]
    for ref in refs[1:-1]:
        total = total + ref[...]
    for c in range(3):
        for k in range(total.shape[1]):
            for j in range(SUB):
                start = (k * SUB + j) * LANES
                out[c : c + 1, start : start + LANES] = total[c, k, j : j + 1, :]


def call(kernel, outs, *args, scratch=(), name=None):
    many = isinstance(outs, (list, tuple))
    return pl.pallas_call(
        kernel,
        out_shape=outs,
        in_specs=[VMEM] * len(args),
        out_specs=[VMEM] * len(outs) if many else VMEM,
        scratch_shapes=list(scratch),
        compiler_params=pltpu.CompilerParams(vmem_limit_bytes=48 * 1024 * 1024),
        name=name,
    )(*args)


def up_pairs(count):
    return [(i, i + 1) for i in range(count - 1)]


def down_pairs(count):
    return [(i + 1, i) for i in range(count - 1)]


def exchange(zup, zdn, ys, dgs):
    slabs, pencils = lax.axis_size("slab"), lax.axis_size("pencil")
    n = len(ys)
    zlo = lax.ppermute(zup, "slab", up_pairs(slabs))
    zhi = lax.ppermute(zdn, "slab", down_pairs(slabs))
    swap = up_pairs(pencils) + down_pairs(pencils)
    y_pairs = [swap] if n == 1 else [up_pairs(pencils), down_pairs(pencils)]
    new_ys = [lax.ppermute(y, "pencil", pairs) for y, pairs in zip(ys, y_pairs)]
    new_dgs = []
    for k, z_pairs in enumerate((up_pairs(slabs), down_pairs(slabs))):
        for j, pairs in enumerate(y_pairs):
            joint = [
                (za * pencils + ya, zb * pencils + yb) for za, zb in z_pairs for ya, yb in pairs
            ]
            new_dgs.append(lax.ppermute(dgs[k * n + j], ("slab", "pencil"), joint))
    return zlo, zhi, new_ys, new_dgs


def all_sum(value):
    for axis in ("comp", "pencil"):
        count = lax.axis_size(axis)
        bit = 1
        while bit < count:
            value = value + lax.ppermute(value, axis, [(i, i ^ bit) for i in range(count)])
            bit *= 2
    count = lax.axis_size("slab")
    bit = 1
    while count // bit > 4:
        value = value + lax.ppermute(value, "slab", [(i, i ^ bit) for i in range(count)])
        bit *= 2
    terms = [value]
    for k in range(1, count // bit):
        terms.append(lax.ppermute(value, "slab", [(i, i ^ (k * bit)) for i in range(count)]))
    return terms


def local(u_start, toughness, crack_label, obs_weight, sensor_cell):
    Z, Y, X = toughness.shape
    pencils = lax.axis_size("pencil")
    merged = pencils == 2
    n = 1 if merged else 2
    shape = jax.ShapeDtypeStruct
    field, vector = shape((Z, Y, X), F32), shape((3, Z, Y, X), F32)
    payloads = payload_shapes(Z, Y, X, n)
    swap = [(0, 1), (1, 0)]
    d, *out = call(
        functools.partial(pack_kernel, merged, n),
        [field] + payloads,
        u_start,
        crack_label,
        name="pack",
    )
    moved = u_start
    scratch = [
        pltpu.VMEM((3, Z + 4, Y + 2 * SUB, X + LANES), F32),
        pltpu.VMEM((Z + 2, Y + 2 * SUB, X + LANES), F32),
        pltpu.VMEM((6, Z + 2, Y + 2 * SUB, X + LANES), F32),
    ]
    sensors = sensor_cell.shape[0]
    for repeat in range(2):
        last = repeat == 1
        zlo, zhi, ys, dgs = exchange(out[0], out[1], out[2 : 2 + n], out[2 + n :])
        packet = call(
            functools.partial(xpack_kernel, merged),
            shape((Y + Z, LANES), F32),
            moved,
            d,
            zlo,
            zhi,
            ys[0],
            ys[-1],
            name="xpack",
        )
        xh = lax.ppermute(packet, "comp", swap)
        args = [moved, d, toughness, zlo, zhi, *ys, *dgs, xh]
        if last:
            args += [
                obs_weight.reshape(Z * Y, sensors),
                sensor_cell.reshape(1, sensors),
            ]
            moved, d, part = call(
                functools.partial(step_kernel, merged, n, True),
                [vector, field, shape((3, sensors // (SUB * LANES), SUB, LANES), F32)],
                *args,
                scratch=scratch + [pltpu.VMEM((Z * Y, LANES), F32)],
                name="step2",
            )
        else:
            moved, d, *out = call(
                functools.partial(step_kernel, merged, n, False),
                [vector, field] + payloads,
                *args,
                scratch=scratch,
                name="step1",
            )
    terms = all_sum(part)
    readings = call(
        functools.partial(finish_kernel, len(terms)),
        shape((3, sensors), F32),
        *terms,
        name="finish",
    )
    return moved, d, readings


def solution(mesh):
    return jax.shard_map(
        local,
        mesh=mesh,
        in_specs=(
            P(None, ("groups", "slab"), "pencil", "comp"),
            P(("groups", "slab"), "pencil", "comp"),
            P(("groups", "slab"), "pencil", "comp"),
            P("slab", "pencil", "comp", None),
            P(),
        ),
        out_specs=(
            P(None, ("groups", "slab"), "pencil", "comp"),
            P(("groups", "slab"), "pencil", "comp"),
            P(None, "groups"),
        ),
        check_vma=False,
    )
```

```python
import functools

import jax
import jax.numpy as jnp
from jax import lax
from jax.experimental import pallas as pl
from jax.experimental.pallas import tpu as pltpu
from jax.sharding import PartitionSpec as P

SHEAR_MODULUS = 1.0
LAME_FIRST = 1.5
RESIDUAL_STIFF = 0.001
TIME_DISP = 0.15
TIME_DAMAGE = 0.08
DAMAGE_LEVEL = 0.45
POINT_GAIN = 8.0
LANES = 128
SUB = 8
COS_THIRD = (
    0.5000000037331834,
    0.5773496613984853,
    -0.11109449276880777,
    0.05327935086024303,
    -0.031925412185213546,
    0.01960032102518762,
    -0.010237508432464154,
    0.003654119632233793,
    -0.0006260453394989179,
)
F32 = jnp.float32
VMEM = pl.BlockSpec(memory_space=pltpu.VMEM)


def positive_square_sum(m00, m11, m22, m01, m02, m12):
    mean = (m00 + m11 + m22) * (1.0 / 3.0)
    b00, b11, b22 = m00 - mean, m11 - mean, m22 - mean
    s01, s02, s12 = m01 * m01, m02 * m02, m12 * m12
    p2 = (b00 * b00 + b11 * b11 + b22 * b22) * (1.0 / 6.0) + (s01 + s02 + s12) * (1.0 / 3.0)
    det = b00 * (b11 * b22 - s12) + 2.0 * (m01 * m02) * m12 - b11 * s02 - b22 * s01
    mean2 = mean * mean
    whole = mean * (mean2 - 3.0 * p2) + det
    up = whole >= 0.0
    safe = jnp.maximum(p2, 1e-24)
    inv = lax.rsqrt(safe)
    p = safe * inv
    half = 0.25 * (det * inv) * (inv * inv)
    half = jnp.where(up, half, -half) + 0.5
    half = jnp.minimum(jnp.maximum(half, 0.0), 1.0)
    t = jnp.sqrt(half)
    c = jnp.full_like(t, COS_THIRD[-1])
    for value in COS_THIRD[-2::-1]:
        c = c * t + value
    pc = p * c
    lead = jnp.where(up, mean, -mean)
    largest = lead + 2.0 * pc
    square = largest * largest
    norm = 6.0 * p2 + 3.0 * mean2
    rest = lead - pc
    return jnp.where(
        up, jnp.where(rest > 0.0, norm, square), jnp.where(rest < 0.0, norm - square, 0.0)
    )


def emit_payloads(merged, py, u, d, zup, zdn, ys, dgs):
    _, Z, Y, X = u.shape
    for c in range(3):
        zup[2 * c : 2 * c + 2] = u[c, Z - 2 : Z]
        zdn[2 * c : 2 * c + 2] = u[c, 0:2]
    zup[6] = d[Z - 1]
    zdn[6] = d[0]

    def rows(side, c, layer, zs):
        row = Y - 2 + layer if side > 0 else layer
        return u[c, zs, row, :]

    def pick(fn):
        if merged:
            first = py == 0
            return [jnp.where(first, fn(1), fn(-1))]
        return [fn(1), fn(-1)]

    full = slice(0, Z)
    for c in range(3):
        for layer in range(2):
            for ref, value in zip(ys, pick(lambda s: rows(s, c, layer, full))):
                ref[2 * c + layer] = value
    for ref, value in zip(ys, pick(lambda s: d[:, Y - 1 if s > 0 else 0, :])):
        ref[6] = value
    n = len(ys)
    for k, zs in enumerate((slice(Z - 1, Z), slice(0, 1))):
        for c in range(3):
            for j, value in enumerate(
                pick(lambda s: rows(s, c, 1 if s > 0 else 0, zs))
            ):
                dgs[k * n + j][c : c + 1, :] = value


def payload_shapes(Z, Y, X, n):
    return (
        [jax.ShapeDtypeStruct((7, Y, X), F32)] * 2
        + [jax.ShapeDtypeStruct((7, Z, X), F32)] * n
        + [jax.ShapeDtypeStruct((SUB, X), F32)] * (2 * n)
    )


def pack_kernel(merged, n, u, label, d0, zup, zdn, *rest):
    d0[...] = DAMAGE_LEVEL * label[...].astype(F32)
    emit_payloads(merged, lax.axis_index("pencil"), u, d0, zup, zdn, rest[:n], rest[n:])


def xpack_kernel(merged, u, d, zlo, zhi, ylo, yhi, *rest):
    out = rest[-1]
    _, Z, Y, X = u.shape
    left = lax.axis_index("comp") == 0
    lane = lax.broadcasted_iota(jnp.int32, (Y, LANES), 1)
    slot = jnp.where(left, (lane + 2) // 2 % (LANES // 2), lane // 2)

    def side(ref, *at):
        return jnp.where(left, ref[at + (slice(X - LANES, X),)], ref[at + (slice(0, LANES),)])

    acc = jnp.zeros((Y, LANES), F32)
    entry = 0
    for c in range(3):
        for z in range(-1, Z + 1):
            if z < 0:
                tile = side(zlo, 2 * c + 1, slice(None))
            elif z == Z:
                tile = side(zhi, 2 * c, slice(None))
            else:
                tile = side(u, c, z, slice(None))
            acc = jnp.where(slot == entry, pltpu.roll(tile, 2 * entry, 1), acc)
            entry += 1
    for z in range(Z):
        acc = jnp.where(slot == entry, pltpu.roll(side(d, z, slice(None)), 2 * entry, 1), acc)
        entry += 1
    out[0:Y, :] = jnp.where(left, pltpu.roll(acc, 2, 1), acc)
    acc = jnp.zeros((Z, LANES), F32)
    entry = 0
    for ref, layer in ((ylo, 1), (yhi, 0)):
        for c in range(3):
            tile = side(ref, 2 * c + layer, slice(None))
            acc = jnp.where(slot[0:Z] == entry, pltpu.roll(tile, 2 * entry, 1), acc)
            entry += 1
    out[Y : Y + Z, :] = jnp.where(left, pltpu.roll(acc, 2, 1), acc)


def gather_blocks(merged, refs, U, D):
    u, d, zlo, zhi, ylo, yhi, dgs, xh = refs
    _, Z, Y, X = u.shape
    H = SUB
    py = lax.axis_index("pencil")
    left = lax.axis_index("comp") == 0
    lo_ok = py != 0 if merged else None
    hi_ok = py == 0 if merged else None

    def keep(ok, value):
        return value if ok is None else jnp.where(ok, value, 0.0)

    lane = lax.broadcasted_iota(jnp.int32, (Y, LANES), 1)
    inside = jnp.where(left, lane, LANES - 1 - lane) < 2
    packet = xh[0:Y, :]
    packet = jnp.where(left, packet, pltpu.roll(packet, LANES - 2, 1))
    edge = xh[Y : Y + Z, :]
    edge = jnp.where(left, edge, pltpu.roll(edge, LANES - 2, 1))

    def column(source, entry):
        shift = (LANES - 2 * entry) % LANES
        moved = pltpu.roll(source, shift, 1) if shift else source
        return jnp.where(inside[0 : source.shape[0]], moved, 0.0)

    entry = 0
    for c in range(3):
        U[c, 2 : Z + 2, H : H + Y, 0:X] = u[c]
        U[c, 0:2, H : H + Y, 0:X] = zlo[2 * c : 2 * c + 2]
        U[c, Z + 2 : Z + 4, H : H + Y, 0:X] = zhi[2 * c : 2 * c + 2]
        for z in range(-1, Z + 1):
            U[c, z + 2, H : H + Y, X : X + LANES] = column(packet, entry)
            entry += 1
        for layer in range(2):
            low = keep(lo_ok, ylo[2 * c + layer])
            high = keep(hi_ok, yhi[2 * c + layer])
            for z in range(Z):
                U[c, z + 2, H - 2 + layer : H - 1 + layer, 0:X] = low[z : z + 1]
                U[c, z + 2, H + Y + layer : H + Y + layer + 1, 0:X] = high[z : z + 1]
        low, high = keep(lo_ok, column(edge, c)), keep(hi_ok, column(edge, 3 + c))
        for z in range(Z):
            U[c, z + 2, H - 1 : H, X : X + LANES] = low[z : z + 1]
            U[c, z + 2, H + Y : H + Y + 1, X : X + LANES] = high[z : z + 1]
        n = len(dgs) // 2
        for k, zi in ((0, 1), (1, Z + 2)):
            from_low = dgs[k * n][c : c + 1, :]
            from_high = dgs[k * n + n - 1][c : c + 1, :]
            U[c, zi, H - 1 : H, 0:X] = keep(lo_ok, from_low)
            U[c, zi, H + Y : H + Y + 1, 0:X] = keep(hi_ok, from_high)
    D[1 : Z + 1, H : H + Y, 0:X] = d[...]
    D[0, H : H + Y, 0:X] = zlo[6]
    D[Z + 1, H : H + Y, 0:X] = zhi[6]
    low, high = keep(lo_ok, ylo[6]), keep(hi_ok, yhi[6])
    for z in range(Z):
        D[z + 1, H : H + Y, X : X + LANES] = column(packet, entry)
        D[z + 1, H - 1 : H, 0:X] = low[z : z + 1]
        D[z + 1, H + Y : H + Y + 1, 0:X] = high[z : z + 1]
        entry += 1


def ahead(value):
    return pltpu.roll(value, value.shape[-1] - 1, value.ndim - 1)


def behind(value):
    return pltpu.roll(value, 1, value.ndim - 1)


def step_kernel(merged, n, last, *refs):
    u, d, tough, zlo, zhi = refs[:5]
    rest = list(refs[5:])
    take = lambda k: [rest.pop(0) for _ in range(k)]
    ys, dgs, (xh,) = take(n), take(2 * n), take(1)
    if last:
        weight, sensor = take(2)
    moved, damage = take(2)
    if last:
        (part,) = take(1)
    else:
        zup, zdn, *out = take(2 + 3 * n)
    U, D, S = take(3)
    _, Z, Y, X = u.shape
    H = SUB
    gather_blocks(merged, (u, d, zlo, zhi, ys[0], ys[-1], dgs, xh), U, D)
    zz, zy, zx, yy, yx, xx = range(6)
    tiles = Y // SUB

    def gradients(zi, r):
        at = slice(r, r + SUB)
        gz, gy, gx = [], [], []
        for c in range(3):
            gz.append(U[c, zi + 1, at, :] - U[c, zi - 1, at, :])
            gy.append(U[c, zi, r + 1 : r + SUB + 1, :] - U[c, zi, r - 1 : r + SUB - 1, :])
            mid = U[c, zi, at, :]
            gx.append(ahead(mid) - behind(mid))
        return gz, gy, gx

    def stiffness(zi, r):
        keep = 1.0 - D[zi - 1, r : r + SUB, :]
        return 0.5 * (keep * keep + RESIDUAL_STIFF)

    def put(key, zi, r, value, width):
        S[key, zi - 1, r : r + SUB, 0:width] = value[:, 0:width]

    def z_face(zi):
        for t in range(1, tiles + 1):
            r = t * SUB
            gz, gy, gx = gradients(zi, r)
            h = stiffness(zi, r)
            total = LAME_FIRST * (gz[0] + gy[1] + gx[2])
            put(zz, zi, r, h * (total + 2.0 * gz[0]), X)
            put(zy, zi, r, h * (gy[0] + gz[1]), X)
            put(zx, zi, r, h * (gx[0] + gz[2]), X)

    z_face(1)
    z_face(Z + 2)

    @pl.loop(2, Z + 2)
    def _(zi):
        for t in (0, tiles + 1):
            r = t * SUB
            at = slice(r, r + SUB)
            row = H - 1 if t == 0 else H + Y
            one = slice(row, row + 1)
            gz, gy, gx = [], [], []
            for c in range(3):
                gz.append(U[c, zi + 1, one, :] - U[c, zi - 1, one, :])
                gy.append(U[c, zi, row + 1 : row + 2, :] - U[c, zi, row - 1 : row, :])
                mid = U[c, zi, one, :]
                gx.append(ahead(mid) - behind(mid))
            keep = 1.0 - D[zi - 1, one, :]
            h = 0.5 * (keep * keep + RESIDUAL_STIFF)
            total = LAME_FIRST * (gz[0] + gy[1] + gx[2])
            for key, value in (
                (zy, gy[0] + gz[1]),
                (yy, total + 2.0 * gy[1]),
                (yx, gx[1] + gy[2]),
            ):
                S[key, zi - 1, one, 0:X] = (h * value)[:, 0:X]
        for t in range(1, tiles + 1):
            r = t * SUB
            gz, gy, gx = gradients(zi, r)
            h = stiffness(zi, r)
            trace = gz[0] + gy[1] + gx[2]
            total = LAME_FIRST * trace
            mzy, mzx, myx = gy[0] + gz[1], gx[0] + gz[2], gx[1] + gy[2]
            put(zz, zi, r, h * (total + 2.0 * gz[0]), X)
            put(yy, zi, r, h * (total + 2.0 * gy[1]), X)
            put(zy, zi, r, h * mzy, X)
            put(zx, zi, r, h * mzx, X + LANES)
            put(yx, zi, r, h * myx, X + LANES)
            put(xx, zi, r, h * (total + 2.0 * gx[2]), X + LANES)
            cut = lambda value: value[:, 0:X]
            squares = positive_square_sum(
                cut(gz[0]), cut(gy[1]), cut(gx[2]), 0.5 * cut(mzy), 0.5 * cut(mzx), 0.5 * cut(myx)
            )
            grow = jnp.maximum(cut(trace), 0.0)
            energy = (0.25 * 0.5 * LAME_FIRST) * (grow * grow) + (0.25 * SHEAR_MODULUS) * squares
            at = slice(r, r + SUB)
            mid = D[zi - 1, at, :]
            core = cut(mid)
            lap = (
                D[zi, at, 0:X]
                + D[zi - 2, at, 0:X]
                + D[zi - 1, r + 1 : r + SUB + 1, 0:X]
                + D[zi - 1, r - 1 : r + SUB - 1, 0:X]
                + cut(ahead(mid) + behind(mid))
                - 6.0 * core
            )
            own = slice((t - 1) * SUB, t * SUB)
            tgh = tough[zi - 2, own, :]
            damage[zi - 2, own, :] = core + TIME_DAMAGE * (
                2.0 * (1.0 - core) * energy + tgh * (lap - core)
            )

    pairs = ((zz, zy, zx), (zy, yy, yx), (zx, yx, xx))
    if last:
        pooled = rest[0]

    @pl.loop(2, Z + 2)
    def _(zi):
        for t in range(1, tiles + 1):
            r = t * SUB
            at = slice(r, r + SUB)
            own = slice((t - 1) * SUB, t * SUB)
            sums = []
            for c in range(3):
                kz, ky, kx = pairs[c]
                mid = S[kx, zi - 1, at, :]
                force = (
                    S[kz, zi, at, 0:X]
                    - S[kz, zi - 2, at, 0:X]
                    + S[ky, zi - 1, r + 1 : r + SUB + 1, 0:X]
                    - S[ky, zi - 1, r - 1 : r + SUB - 1, 0:X]
                    + (ahead(mid) - behind(mid))[:, 0:X]
                )
                new = u[c, zi - 2, own, :] + (0.5 * TIME_DISP) * force
                moved[c, zi - 2, own, :] = new
                if last:
                    sums.append(jnp.sum(new, axis=-1, keepdims=True))
            if last:
                lane = lax.broadcasted_iota(jnp.int32, (SUB, LANES), 1)
                value = jnp.where(lane == 0, sums[0], jnp.where(lane == 1, sums[1], sums[2]))
                start = pl.multiple_of((zi - 2) * Y + (t - 1) * SUB, SUB)
                pooled[pl.ds(start, SUB), :] = value

    if last:
        means = (pooled[...] * (1.0 / X)).T[0:SUB].astype(jnp.bfloat16)
        blocks = Z * Y
        count = lax.axis_size("comp")
        spread = Y * lax.axis_size("pencil")
        index = lax.broadcasted_iota(jnp.int32, (blocks, 1), 0)
        plane = lax.axis_index("slab") * Z + index // Y
        row = lax.axis_index("pencil") * Y + index % Y
        ids = (plane * spread + row) * count + lax.axis_index("comp")
        chunk = 8 * LANES
        S8 = lax.broadcasted_iota(jnp.int32, (SUB, LANES), 0)
        for k in range(sensor.shape[1] // chunk):
            cols = slice(k * chunk, (k + 1) * chunk)
            picks = jnp.where(ids == sensor[:, cols], POINT_GAIN, 0.0).astype(jnp.bfloat16)
            value = jnp.dot(means, weight[:, cols], preferred_element_type=F32)
            value = value + jnp.dot(means, picks, preferred_element_type=F32)
            for c in range(3):
                tile = jnp.zeros((SUB, LANES), F32)
                for j in range(8):
                    tile = jnp.where(
                        S8 == j, value[c : c + 1, j * LANES : (j + 1) * LANES], tile
                    )
                part[c, k] = tile
    else:
        emit_payloads(
            merged, lax.axis_index("pencil"), moved, damage, zup, zdn, out[:n], out[n:]
        )


def finish_kernel(count, *refs):
    out = refs[-1]
    total = refs[0][...]
    for ref in refs[1:-1]:
        total = total + ref[...]
    for c in range(3):
        for k in range(total.shape[1]):
            for j in range(SUB):
                start = (k * SUB + j) * LANES
                out[c : c + 1, start : start + LANES] = total[c, k, j : j + 1, :]


def call(kernel, outs, *args, scratch=(), name=None):
    many = isinstance(outs, (list, tuple))
    return pl.pallas_call(
        kernel,
        out_shape=outs,
        in_specs=[VMEM] * len(args),
        out_specs=[VMEM] * len(outs) if many else VMEM,
        scratch_shapes=list(scratch),
        compiler_params=pltpu.CompilerParams(vmem_limit_bytes=48 * 1024 * 1024),
        name=name,
    )(*args)


def up_pairs(count):
    return [(i, i + 1) for i in range(count - 1)]


def down_pairs(count):
    return [(i + 1, i) for i in range(count - 1)]


def exchange(zup, zdn, ys, dgs):
    slabs, pencils = lax.axis_size("slab"), lax.axis_size("pencil")
    n = len(ys)
    zlo = lax.ppermute(zup, "slab", up_pairs(slabs))
    zhi = lax.ppermute(zdn, "slab", down_pairs(slabs))
    swap = up_pairs(pencils) + down_pairs(pencils)
    y_pairs = [swap] if n == 1 else [up_pairs(pencils), down_pairs(pencils)]
    new_ys = [lax.ppermute(y, "pencil", pairs) for y, pairs in zip(ys, y_pairs)]
    new_dgs = []
    for k, z_pairs in enumerate((up_pairs(slabs), down_pairs(slabs))):
        for j, pairs in enumerate(y_pairs):
            joint = [
                (za * pencils + ya, zb * pencils + yb) for za, zb in z_pairs for ya, yb in pairs
            ]
            new_dgs.append(lax.ppermute(dgs[k * n + j], ("slab", "pencil"), joint))
    return zlo, zhi, new_ys, new_dgs


def all_sum(value):
    for axis in ("comp", "pencil"):
        count = lax.axis_size(axis)
        bit = 1
        while bit < count:
            value = value + lax.ppermute(value, axis, [(i, i ^ bit) for i in range(count)])
            bit *= 2
    count = lax.axis_size("slab")
    bit = 1
    while count // bit > 4:
        value = value + lax.ppermute(value, "slab", [(i, i ^ bit) for i in range(count)])
        bit *= 2
    terms = [value]
    for k in range(1, count // bit):
        terms.append(lax.ppermute(value, "slab", [(i, i ^ (k * bit)) for i in range(count)]))
    return terms


def local(u_start, toughness, crack_label, obs_weight, sensor_cell):
    Z, Y, X = toughness.shape
    pencils = lax.axis_size("pencil")
    merged = pencils == 2
    n = 1 if merged else 2
    shape = jax.ShapeDtypeStruct
    field, vector = shape((Z, Y, X), F32), shape((3, Z, Y, X), F32)
    payloads = payload_shapes(Z, Y, X, n)
    swap = [(0, 1), (1, 0)]
    d, *out = call(
        functools.partial(pack_kernel, merged, n),
        [field] + payloads,
        u_start,
        crack_label,
        name="pack",
    )
    moved = u_start
    scratch = [
        pltpu.VMEM((3, Z + 4, Y + 2 * SUB, X + LANES), F32),
        pltpu.VMEM((Z + 2, Y + 2 * SUB, X + LANES), F32),
        pltpu.VMEM((6, Z + 2, Y + 2 * SUB, X + LANES), F32),
    ]
    sensors = sensor_cell.shape[0]
    for repeat in range(2):
        last = repeat == 1
        zlo, zhi, ys, dgs = exchange(out[0], out[1], out[2 : 2 + n], out[2 + n :])
        packet = call(
            functools.partial(xpack_kernel, merged),
            shape((Y + Z, LANES), F32),
            moved,
            d,
            zlo,
            zhi,
            ys[0],
            ys[-1],
            *dgs,
            name="xpack",
        )
        xh = lax.ppermute(packet, "comp", swap)
        args = [moved, d, toughness, zlo, zhi, *ys, *dgs, xh]
        if last:
            args += [
                obs_weight.reshape(Z * Y, sensors),
                sensor_cell.reshape(1, sensors),
            ]
            moved, d, part = call(
                functools.partial(step_kernel, merged, n, True),
                [vector, field, shape((3, sensors // (SUB * LANES), SUB, LANES), F32)],
                *args,
                scratch=scratch + [pltpu.VMEM((Z * Y, LANES), F32)],
                name="step2",
            )
        else:
            moved, d, *out = call(
                functools.partial(step_kernel, merged, n, False),
                [vector, field] + payloads,
                *args,
                scratch=scratch,
                name="step1",
            )
    terms = all_sum(part)
    readings = call(
        functools.partial(finish_kernel, len(terms)),
        shape((3, sensors), F32),
        *terms,
        name="finish",
    )
    return moved, d, readings


def solution(mesh):
    return jax.shard_map(
        local,
        mesh=mesh,
        in_specs=(
            P(None, ("groups", "slab"), "pencil", "comp"),
            P(("groups", "slab"), "pencil", "comp"),
            P(("groups", "slab"), "pencil", "comp"),
            P("slab", "pencil", "comp", None),
            P(),
        ),
        out_specs=(
            P(None, ("groups", "slab"), "pencil", "comp"),
            P(("groups", "slab"), "pencil", "comp"),
            P(None, "groups"),
        ),
        check_vma=False,
    )
```

```python
import functools

import jax
import jax.numpy as jnp
from jax import lax
from jax.experimental import pallas as pl
from jax.experimental.pallas import tpu as pltpu
from jax.sharding import PartitionSpec as P

SHEAR_MODULUS = 1.0
LAME_FIRST = 1.5
RESIDUAL_STIFF = 0.001
TIME_DISP = 0.15
TIME_DAMAGE = 0.08
DAMAGE_LEVEL = 0.45
POINT_GAIN = 8.0
LANES = 128
SUB = 8
COS_THIRD = (
    0.5000000037331834,
    0.5773496613984853,
    -0.11109449276880777,
    0.05327935086024303,
    -0.031925412185213546,
    0.01960032102518762,
    -0.010237508432464154,
    0.003654119632233793,
    -0.0006260453394989179,
)
F32 = jnp.float32
VMEM_LIMIT = 24 * 1024 * 1024
VMEM = pl.BlockSpec(memory_space=pltpu.VMEM)


def positive_square_sum(m00, m11, m22, m01, m02, m12):
    mean = (m00 + m11 + m22) * (1.0 / 3.0)
    b00, b11, b22 = m00 - mean, m11 - mean, m22 - mean
    s01, s02, s12 = m01 * m01, m02 * m02, m12 * m12
    p2 = (b00 * b00 + b11 * b11 + b22 * b22) * (1.0 / 6.0) + (s01 + s02 + s12) * (1.0 / 3.0)
    det = b00 * (b11 * b22 - s12) + 2.0 * (m01 * m02) * m12 - b11 * s02 - b22 * s01
    mean2 = mean * mean
    whole = mean * (mean2 - 3.0 * p2) + det
    up = whole >= 0.0
    safe = jnp.maximum(p2, 1e-24)
    inv = lax.rsqrt(safe)
    p = safe * inv
    half = 0.25 * (det * inv) * (inv * inv)
    half = jnp.where(up, half, -half) + 0.5
    half = jnp.minimum(jnp.maximum(half, 0.0), 1.0)
    t = jnp.sqrt(half)
    c = jnp.full_like(t, COS_THIRD[-1])
    for value in COS_THIRD[-2::-1]:
        c = c * t + value
    pc = p * c
    lead = jnp.where(up, mean, -mean)
    largest = lead + 2.0 * pc
    square = largest * largest
    norm = 6.0 * p2 + 3.0 * mean2
    rest = lead - pc
    return jnp.where(
        up, jnp.where(rest > 0.0, norm, square), jnp.where(rest < 0.0, norm - square, 0.0)
    )


def sides(merged, fn):
    if merged:
        return [jnp.where(lax.axis_index("pencil") == 0, fn(1), fn(-1))]
    return [fn(1), fn(-1)]


def is_left():
    return lax.axis_index("comp") == 0


def put_columns(u, d, out):
    _, Z, Y, X = u.shape
    left = is_left()
    lane = lax.broadcasted_iota(jnp.int32, (Y, LANES), 1)
    slot = jnp.where(left, (lane + 2) // 2 % (LANES // 2), lane // 2)
    acc = jnp.zeros((Y, LANES), F32)
    entry = 0
    for c in range(4):
        for z in range(Z):
            ref = d.at[z] if c == 3 else u.at[c, z]
            tile = jnp.where(left, ref[:, X - LANES : X], ref[:, 0:LANES])
            turned = pltpu.roll(tile, 2 * entry, 1) if entry else tile
            acc = jnp.where(slot == entry, turned, acc)
            entry += 1
    out[...] = jnp.where(left, pltpu.roll(acc, 2, 1), acc)


def column_reader(packet):
    rows = packet.shape[0]
    left = is_left()
    lane = lax.broadcasted_iota(jnp.int32, (rows, LANES), 1)
    inside = jnp.where(left, lane, LANES - 1 - lane) < 2
    packet = jnp.where(left, packet, pltpu.roll(packet, LANES - 2, 1))

    def column(entry):
        shift = (LANES - 2 * entry) % LANES
        turned = pltpu.roll(packet, shift, 1) if shift else packet
        return jnp.where(inside, turned, 0.0)

    return column


def load_kernel(u_hbm, label_hbm, u, d, cols, label, sems):
    copies = [pltpu.make_async_copy(u_hbm.at[c], u.at[c], sems.at[c]) for c in range(3)]
    copies.append(pltpu.make_async_copy(label_hbm, label, sems.at[3]))
    for copy in copies:
        copy.start()
    copies[3].wait()
    d[...] = DAMAGE_LEVEL * label[...].astype(F32)
    for copy in copies[:3]:
        copy.wait()
    put_columns(u, d, cols)


def rows_kernel(merged, u, d, xh, *outs):
    _, Z, Y, X = u.shape
    for c in range(3):
        for layer in range(2):
            row = lambda s: u[c, :, Y - 2 + layer if s > 0 else layer, :]
            for ref, value in zip(outs, sides(merged, row)):
                ref[2 * c + layer] = value
    for ref, value in zip(outs, sides(merged, lambda s: d[:, Y - 1 if s > 0 else 0, :])):
        ref[6] = value
    corner = lambda s: xh[Y - 1 : Y, :] if s > 0 else xh[0:1, :]
    for ref, value in zip(outs, sides(merged, corner)):
        ref[7, 0:1, 0:LANES] = value


def planes_kernel(u, d, xh, ylo, yhi, zup, zdn):
    _, Z, Y, X = u.shape
    for out, near, first in ((zup, Z - 1, Z - 2), (zdn, 0, 0)):
        for c in range(3):
            out[2 * c : 2 * c + 2] = u[c, first : first + 2]
        out[6] = d[near]
        out[7, :, 0:LANES] = xh[...]
        at = 0
        for ref, layer in ((ylo, 1), (yhi, 0)):
            for c in range(3):
                for k in range(X // LANES):
                    out[7, at : at + 1, LANES : 2 * LANES] = ref[
                        2 * c + layer, near : near + 1, k * LANES : (k + 1) * LANES
                    ]
                    at += 1


def row_keepers(merged):
    if not merged:
        return (lambda value: value), (lambda value: value)
    py = lax.axis_index("pencil")
    return (
        lambda value: jnp.where(py != 0, value, 0.0),
        lambda value: jnp.where(py == 0, value, 0.0),
    )


def lay_out(merged, u, d, xh, ylo, yhi, U, D):
    _, Z, Y, X = u.shape
    H = SUB
    low_of, high_of = row_keepers(merged)
    column = column_reader(xh[...])
    low_corner = column_reader(low_of(ylo[7, 0:1, 0:LANES]))
    high_corner = column_reader(high_of(yhi[7, 0:1, 0:LANES]))
    for c in range(3):
        U[c, :, H : H + Y, 0:X] = u[c]
        for layer in range(2):
            low, high = low_of(ylo[2 * c + layer]), high_of(yhi[2 * c + layer])
            for z in range(Z):
                U[c, z, H - 2 + layer : H - 1 + layer, 0:X] = low[z : z + 1]
                U[c, z, H + Y + layer : H + Y + layer + 1, 0:X] = high[z : z + 1]
        for z in range(Z):
            entry = c * Z + z
            U[c, z, H : H + Y, X : X + LANES] = column(entry)
            U[c, z, H - 1 : H, X : X + LANES] = low_corner(entry)
            U[c, z, H + Y : H + Y + 1, X : X + LANES] = high_corner(entry)
    D[:, H : H + Y, 0:X] = d[...]
    low, high = low_of(ylo[6]), high_of(yhi[6])
    for z in range(Z):
        D[z, H - 1 : H, 0:X] = low[z : z + 1]
        D[z, H + Y : H + Y + 1, 0:X] = high[z : z + 1]
        D[z, H : H + Y, X : X + LANES] = column(3 * Z + z)


def lay_out_face(merged, zmsg, layers, entry_plane, Z, F):
    _, Y, X = zmsg.shape
    H = SUB
    low_of, high_of = row_keepers(merged)
    column = column_reader(zmsg[7, :, 0:LANES])
    far, near = layers
    halves = X // LANES
    for c in range(3):
        F[c, 0, H : H + Y, 0:X] = zmsg[2 * c + far]
        F[c, 1, H : H + Y, 0:X] = zmsg[2 * c + near]
        F[c, 1, H : H + Y, X : X + LANES] = column(c * Z + entry_plane)
        for k in range(halves):
            at = c * halves + k
            lanes = slice(k * LANES, (k + 1) * LANES)
            F[c, 1, H - 1 : H, lanes] = low_of(zmsg[7, at : at + 1, LANES : 2 * LANES])
            at += 3 * halves
            F[c, 1, H + Y : H + Y + 1, lanes] = high_of(zmsg[7, at : at + 1, LANES : 2 * LANES])


def ahead(value):
    return pltpu.roll(value, value.shape[-1] - 1, value.ndim - 1)


def behind(value):
    return pltpu.roll(value, 1, value.ndim - 1)


ZZ, ZY, ZX, YY, YX, XX = range(6)
PAIRS = ((ZZ, ZY, ZX), (ZY, YY, YX), (ZX, YX, XX))


def gradients(at, row, count):
    rows = slice(row, row + count)
    gz, gy, gx = [], [], []
    for c in range(3):
        mid = at(c, 0)
        gz.append(at(c, 1)[rows, :] - at(c, -1)[rows, :])
        gy.append(mid[row + 1 : row + count + 1, :] - mid[row - 1 : row + count - 1, :])
        value = mid[rows, :]
        gx.append(ahead(value) - behind(value))
    return gz, gy, gx


def stiffness(damage):
    keep = 1.0 - damage
    return 0.5 * (keep * keep + RESIDUAL_STIFF)


def energy_of(gz, gy, gx, X):
    cut = lambda value: value[:, 0:X]
    z0, y1, x2 = cut(gz[0]), cut(gy[1]), cut(gx[2])
    mzy = 0.5 * cut(gy[0] + gz[1])
    mzx = 0.5 * cut(gx[0] + gz[2])
    myx = 0.5 * cut(gx[1] + gy[2])
    squares = positive_square_sum(z0, y1, x2, mzy, mzx, myx)
    grow = jnp.maximum(z0 + y1 + x2, 0.0)
    return (0.25 * 0.5 * LAME_FIRST) * (grow * grow) + (0.25 * SHEAR_MODULUS) * squares


def new_damage(mid, below, above, t, energy, tough):
    X = tough.shape[-1]
    r = t * SUB
    value = mid[r : r + SUB, :]
    core = value[:, 0:X]
    lap = (
        below
        + above
        + mid[r + 1 : r + SUB + 1, 0:X]
        + mid[r - 1 : r + SUB - 1, 0:X]
        + (ahead(value) + behind(value))[:, 0:X]
        - 6.0 * core
    )
    return core + TIME_DAMAGE * (2.0 * (1.0 - core) * energy + tough * (lap - core))


def plane_stress(at, damage_plane, S, Y, X, then=None):
    H = SUB
    for row in (H - 1, H + Y):
        gz, gy, gx = gradients(at, row, 1)
        h = stiffness(damage_plane[row : row + 1, :])
        total = LAME_FIRST * (gz[0] + gy[1] + gx[2])
        for key, value in (
            (ZY, gy[0] + gz[1]),
            (YY, total + 2.0 * gy[1]),
            (YX, gx[1] + gy[2]),
        ):
            S[key, row : row + 1, 0:X] = (h * value)[:, 0:X]
    for t in range(1, Y // SUB + 1):
        rows = slice(t * SUB, t * SUB + SUB)
        gz, gy, gx = gradients(at, t * SUB, SUB)
        h = stiffness(damage_plane[rows, :])
        total = LAME_FIRST * (gz[0] + gy[1] + gx[2])
        S[ZZ, rows, 0:X] = (h * (total + 2.0 * gz[0]))[:, 0:X]
        S[YY, rows, 0:X] = (h * (total + 2.0 * gy[1]))[:, 0:X]
        S[ZY, rows, 0:X] = (h * (gy[0] + gz[1]))[:, 0:X]
        S[ZX, rows, :] = h * (gx[0] + gz[2])
        S[YX, rows, :] = h * (gx[1] + gy[2])
        S[XX, rows, :] = h * (total + 2.0 * gx[2])
        if then is not None:
            then(t, energy_of(gz, gy, gx, X))


def face_stress(at, damage, S, Y, X):
    for t in range(1, Y // SUB + 1):
        rows = slice(t * SUB, t * SUB + SUB)
        gz, gy, gx = gradients(at, t * SUB, SUB)
        h = stiffness(damage[(t - 1) * SUB : t * SUB, :])
        total = LAME_FIRST * (gz[0] + gy[1] + gx[2])
        for key, value in (
            (ZZ, total + 2.0 * gz[0]),
            (ZY, gy[0] + gz[1]),
            (ZX, gx[0] + gz[2]),
        ):
            S[key, rows, 0:X] = h * value[:, 0:X]


def plane_moved(below, mid, above, u_plane, t, X):
    r = t * SUB
    rows = slice(r, r + SUB)
    out = []
    for c in range(3):
        kz, ky, kx = PAIRS[c]
        value = mid[kx, rows, :]
        force = (
            above[kz, rows, 0:X]
            - below[kz, rows, 0:X]
            + mid[ky, r + 1 : r + SUB + 1, 0:X]
            - mid[ky, r - 1 : r + SUB - 1, 0:X]
            + (ahead(value) - behind(value))[:, 0:X]
        )
        out.append(u_plane(c)[(t - 1) * SUB : t * SUB, :] + (0.5 * TIME_DISP) * force)
    return out


def row_sums(new):
    lane = lax.broadcasted_iota(jnp.int32, (SUB, LANES), 1)
    sums = [jnp.sum(value, axis=-1, keepdims=True) for value in new]
    return jnp.where(lane == 0, sums[0], jnp.where(lane == 1, sums[1], sums[2]))


def means_of(pool, X):
    return (pool * (1.0 / X)).T[0:SUB].astype(jnp.bfloat16)


def inner_kernel(merged, last, *refs):
    rest = list(refs)
    take = lambda k: [rest.pop(0) for _ in range(k)]
    u, d, tough, xh, ylo, yhi = take(6)
    if last:
        weight, sensor = take(2)
    U, D, S, moved, damage = take(5)
    if last:
        part, edge_rows, pool = take(3)
    _, Z, Y, X = u.shape
    tiles = range(1, Y // SUB + 1)
    lay_out(merged, u, d, xh, ylo, yhi, U, D)

    @pl.loop(1, Z - 1)
    def _(z):
        def then(t, energy):
            rows = slice(t * SUB, t * SUB + SUB)
            own = slice((t - 1) * SUB, t * SUB)
            damage[z - 1, own, :] = new_damage(
                D.at[z], D[z - 1, rows, 0:X], D[z + 1, rows, 0:X], t, energy, tough[z, own, :]
            )

        plane_stress(lambda c, dz: U.at[c, z + dz], D.at[z], S.at[z - 1], Y, X, then)

    @pl.loop(2, Z - 2)
    def _(z):
        for t in tiles:
            own = slice((t - 1) * SUB, t * SUB)
            new = plane_moved(
                S.at[z - 2], S.at[z - 1], S.at[z], lambda c: u.at[c, z], t, X
            )
            for c in range(3):
                moved[c, z - 2, own, :] = new[c]
            if last:
                start = pl.multiple_of((z - 2) * Y + (t - 1) * SUB, SUB)
                pool[pl.ds(start, SUB), :] = row_sums(new)

    if last:
        means = means_of(pool[...], X)
        count = lax.axis_size("comp")
        spread = Y * lax.axis_size("pencil")
        index = lax.broadcasted_iota(jnp.int32, (Z * Y, 1), 0)
        plane = lax.axis_index("slab") * Z + index // Y
        row = lax.axis_index("pencil") * Y + index % Y
        ids = (plane * spread + row) * count + lax.axis_index("comp")
        chunk = 8 * LANES
        two, end = 2 * Y, (Z - 2) * Y
        edge_rows[0:two, :] = weight[0:two, :]
        edge_rows[two : 2 * two, :] = weight[end : end + two, :]
        for k in range(sensor.shape[1] // chunk):
            cols = slice(k * chunk, (k + 1) * chunk)
            picks = jnp.where(ids == sensor[:, cols], POINT_GAIN, 0.0).astype(jnp.bfloat16)
            edge_rows[2 * two : 3 * two, cols] = picks[0:two]
            edge_rows[3 * two : 4 * two, cols] = picks[end : end + two]
            value = jnp.dot(means, weight[two:end, cols], preferred_element_type=F32)
            part[:, cols] = value + jnp.dot(means, picks[two:end], preferred_element_type=F32)


def outer_kernel(merged, last, *refs):
    rest = list(refs)
    take = lambda k: [rest.pop(0) for _ in range(k)]
    u, d, zlo, zhi, U, D, S = take(7)
    if last:
        inner_part, edge_rows = take(2)
        moved, part = take(2)
    else:
        tough, inner_moved, inner_damage = take(3)
        moved, damage, cols = take(3)
    low, high, faces, first_s, last_s = take(5)
    if last:
        (pool,) = take(1)
    _, Z, Y, X = u.shape
    tiles = range(1, Y // SUB + 1)
    lay_out_face(merged, zlo, (0, 1), Z - 1, Z, low)
    lay_out_face(merged, zhi, (1, 0), 0, Z, high)

    def at_plane(z):
        def at(c, dz):
            k = z + dz
            if k < 0:
                return low.at[c, 2 + k]
            if k >= Z:
                return high.at[c, Z + 1 - k]
            return U.at[c, k]

        return at

    face_stress(at_plane(-1), zlo.at[6], faces.at[0], Y, X)
    face_stress(at_plane(Z), zhi.at[6], faces.at[1], Y, X)
    for z, out in ((0, first_s), (Z - 1, last_s)):
        then = None
        if not last:

            def then(t, energy, z=z):
                rows = slice(t * SUB, t * SUB + SUB)
                own = slice((t - 1) * SUB, t * SUB)
                below = zlo[6, own, :] if z == 0 else D[z - 1, rows, 0:X]
                above = D[z + 1, rows, 0:X] if z == 0 else zhi[6, own, :]
                damage[z, own, :] = new_damage(D.at[z], below, above, t, energy, tough[z, own, :])

        plane_stress(at_plane(z), D.at[z], out, Y, X, then)

    def stress(z):
        if z < 0:
            return faces.at[0]
        if z >= Z:
            return faces.at[1]
        if z == 0:
            return first_s
        if z == Z - 1:
            return last_s
        return S.at[z - 1]

    for k, z in enumerate((0, 1, Z - 2, Z - 1)):
        for t in tiles:
            own = slice((t - 1) * SUB, t * SUB)
            new = plane_moved(stress(z - 1), stress(z), stress(z + 1), lambda c: u.at[c, z], t, X)
            for c in range(3):
                moved[c, k if last else z, own, :] = new[c]
            if last:
                start = k * Y + (t - 1) * SUB
                pool[start : start + SUB, :] = row_sums(new)
    if last:
        means = means_of(pool[...], X)
        means = jnp.concatenate([means, means], axis=1)
        chunk = 8 * LANES
        sub = lax.broadcasted_iota(jnp.int32, (SUB, LANES), 0)
        for k in range(edge_rows.shape[1] // chunk):
            start = slice(k * chunk, (k + 1) * chunk)
            value = inner_part[:, start] + jnp.dot(
                means, edge_rows[:, start], preferred_element_type=F32
            )
            for c in range(3):
                tile = jnp.zeros((SUB, LANES), F32)
                for j in range(SUB):
                    piece = value[c : c + 1, j * LANES : (j + 1) * LANES]
                    tile = jnp.where(sub == j, piece, tile)
                part[c, k] = tile
    else:
        for c in range(3):
            moved[c, 2 : Z - 2] = inner_moved[c]
        damage[1 : Z - 1] = inner_damage[...]
        put_columns(moved, damage, cols)


def fields_kernel(u, D, U, zlo, zhi, tough, inner_moved, inner_damage, edge_moved, moved, damage):
    Z, Y, X = tough.shape
    for c in range(3):
        moved[c, 0:2] = edge_moved[c, 0:2]
        moved[c, 2 : Z - 2] = inner_moved[c]
        moved[c, Z - 2 : Z] = edge_moved[c, 2:4]
    damage[1 : Z - 1] = inner_damage[...]
    for z in (0, Z - 1):
        for t in range(1, Y // SUB + 1):
            r = t * SUB
            rows = slice(r, r + SUB)
            own = slice((t - 1) * SUB, t * SUB)
            gz, gy, gx = [], [], []
            for c in range(3):
                below = zlo[2 * c + 1, own, :] if z == 0 else U[c, z - 1, rows, 0:X]
                above = U[c, z + 1, rows, 0:X] if z == 0 else zhi[2 * c, own, :]
                gz.append(above - below)
                gy.append(U[c, z, r + 1 : r + SUB + 1, 0:X] - U[c, z, r - 1 : r + SUB - 1, 0:X])
                value = U[c, z, rows, :]
                gx.append((ahead(value) - behind(value))[:, 0:X])
            energy = energy_of(gz, gy, gx, X)
            below = zlo[6, own, :] if z == 0 else D[z - 1, rows, 0:X]
            above = D[z + 1, rows, 0:X] if z == 0 else zhi[6, own, :]
            damage[z, own, :] = new_damage(D.at[z], below, above, t, energy, tough[z, own, :])


def finish_kernel(count, *refs):
    out = refs[-1]
    total = refs[0][...]
    for ref in refs[1:-1]:
        total = total + ref[...]
    for c in range(3):
        for k in range(total.shape[1]):
            for j in range(SUB):
                start = (k * SUB + j) * LANES
                out[c : c + 1, start : start + LANES] = total[c, k, j : j + 1, :]


def call(kernel, outs, *args, scratch=(), name=None, in_specs=None, micros=1):
    many = isinstance(outs, (list, tuple))
    return pl.pallas_call(
        kernel,
        out_shape=outs,
        in_specs=in_specs or [VMEM] * len(args),
        out_specs=[VMEM] * len(outs) if many else VMEM,
        scratch_shapes=list(scratch),
        compiler_params=pltpu.CompilerParams(vmem_limit_bytes=VMEM_LIMIT),
        cost_estimate=pl.CostEstimate(
            flops=0, bytes_accessed=micros * 3_000_000, transcendentals=0
        ),
        name=name,
    )(*args)


def up_pairs(count):
    return [(i, i + 1) for i in range(count - 1)]


def down_pairs(count):
    return [(i + 1, i) for i in range(count - 1)]


def all_sum(value):
    for axis in ("comp", "pencil"):
        count = lax.axis_size(axis)
        bit = 1
        while bit < count:
            value = value + lax.ppermute(value, axis, [(i, i ^ bit) for i in range(count)])
            bit *= 2
    count = lax.axis_size("slab")
    bit = 1
    while count // bit > 4:
        value = value + lax.ppermute(value, "slab", [(i, i ^ bit) for i in range(count)])
        bit *= 2
    terms = [value]
    for k in range(1, count // bit):
        terms.append(lax.ppermute(value, "slab", [(i, i ^ (k * bit)) for i in range(count)]))
    return terms


def local(u_start, toughness, crack_label, obs_weight, sensor_cell):
    Z, Y, X = toughness.shape
    slabs, pencils = lax.axis_size("slab"), lax.axis_size("pencil")
    if lax.axis_size("comp") != 2 or Z < 6 or Z % SUB or 8 * Z > LANES:
        raise ValueError("unsupported block")
    merged = pencils == 2
    n = 1 if merged else 2
    shape = jax.ShapeDtypeStruct
    field, vector = shape((Z, Y, X), F32), shape((3, Z, Y, X), F32)
    columns = shape((Y, LANES), F32)
    sensors = sensor_cell.shape[0]
    rows, lanes = Y + 2 * SUB, X + LANES
    y_up, y_down = up_pairs(pencils), down_pairs(pencils)
    y_pairs = [y_up + y_down] if merged else [y_up, y_down]
    margins = [
        shape((3, Z, rows, lanes), F32),
        shape((Z, rows, lanes), F32),
        shape((6, Z - 2, rows, lanes), F32),
    ]
    margins[2] = shape((Z - 2, 6, rows, lanes), F32)
    scratch = [
        pltpu.VMEM((3, 2, rows, lanes), F32),
        pltpu.VMEM((3, 2, rows, lanes), F32),
        pltpu.VMEM((2, 3, rows, lanes), F32),
        pltpu.VMEM((6, rows, lanes), F32),
        pltpu.VMEM((6, rows, lanes), F32),
    ]
    inner_fields = [shape((3, Z - 4, Y, X), F32), shape((Z - 2, Y, X), F32)]
    moved, damage, cols = call(
        load_kernel,
        [vector, field, columns],
        u_start,
        crack_label,
        scratch=[pltpu.VMEM((Z, Y, X), jnp.int32), pltpu.SemaphoreType.DMA((4,))],
        in_specs=[pl.BlockSpec(memory_space=pltpu.HBM)] * 2,
        name="load",
    )
    for step in range(2):
        last = step == 1
        xh = lax.ppermute(cols, "comp", [(0, 1), (1, 0)])
        out = call(
            functools.partial(rows_kernel, merged),
            [shape((8, Z, X), F32)] * n,
            moved,
            damage,
            xh,
            name="rows",
        )
        ys = [lax.ppermute(y, "pencil", pairs) for y, pairs in zip(out, y_pairs)]
        zup, zdn = call(
            planes_kernel,
            [shape((8, Y, X), F32)] * 2,
            moved,
            damage,
            xh,
            ys[0],
            ys[-1],
            name="planes",
        )
        zlo = lax.ppermute(zup, "slab", up_pairs(slabs))
        zhi = lax.ppermute(zdn, "slab", down_pairs(slabs))
        args = [moved, damage, toughness, xh, ys[0], ys[-1]]
        outs = margins + inner_fields
        inner_scratch = []
        if last:
            args += [obs_weight.reshape(Z * Y, sensors), sensor_cell.reshape(1, sensors)]
            outs = outs + [shape((SUB, sensors), F32), shape((8 * Y, sensors), jnp.bfloat16)]
            inner_scratch = [pltpu.VMEM(((Z - 4) * Y, LANES), F32)]
        U, D, S, inner_moved, inner_damage, *more = call(
            functools.partial(inner_kernel, merged, last),
            outs,
            *args,
            scratch=inner_scratch,
            name="inner",
            micros=4,
        )
        if last:
            edge_moved, part = call(
                functools.partial(outer_kernel, merged, True),
                [shape((3, 4, Y, X), F32), shape((3, sensors // (SUB * LANES), SUB, LANES), F32)],
                moved,
                damage,
                zlo,
                zhi,
                U,
                D,
                S,
                *more,
                scratch=scratch + [pltpu.VMEM((4 * Y, LANES), F32)],
                name="outer2",
            )
            moved, damage = call(
                fields_kernel,
                [vector, field],
                moved,
                D,
                U,
                zlo,
                zhi,
                toughness,
                inner_moved,
                inner_damage,
                edge_moved,
                name="fields",
            )
        else:
            moved, damage, cols = call(
                functools.partial(outer_kernel, merged, False),
                [vector, field, columns],
                moved,
                damage,
                zlo,
                zhi,
                U,
                D,
                S,
                toughness,
                inner_moved,
                inner_damage,
                scratch=scratch,
                name="outer1",
            )
    terms = all_sum(part)
    readings = call(
        functools.partial(finish_kernel, len(terms)),
        shape((3, sensors), F32),
        *terms,
        name="finish",
    )
    return moved, damage, readings


def solution(mesh):
    return jax.shard_map(
        local,
        mesh=mesh,
        in_specs=(
            P(None, ("groups", "slab"), "pencil", "comp"),
            P(("groups", "slab"), "pencil", "comp"),
            P(("groups", "slab"), "pencil", "comp"),
            P("slab", "pencil", "comp", None),
            P(),
        ),
        out_specs=(
            P(None, ("groups", "slab"), "pencil", "comp"),
            P(("groups", "slab"), "pencil", "comp"),
            P(None, "groups"),
        ),
        check_vma=False,
    )
```

```python
import functools

import jax
import jax.numpy as jnp
from jax import lax
from jax.experimental import pallas as pl
from jax.experimental.pallas import tpu as pltpu
from jax.sharding import PartitionSpec as P

SHEAR_MODULUS = 1.0
LAME_FIRST = 1.5
RESIDUAL_STIFF = 0.001
TIME_DISP = 0.15
TIME_DAMAGE = 0.08
DAMAGE_LEVEL = 0.45
POINT_GAIN = 8.0
LANES = 128
SUB = 8
COS_THIRD = (
    0.5000000037331834,
    0.5773496613984853,
    -0.11109449276880777,
    0.05327935086024303,
    -0.031925412185213546,
    0.01960032102518762,
    -0.010237508432464154,
    0.003654119632233793,
    -0.0006260453394989179,
)
F32 = jnp.float32
VMEM_LIMIT = 24 * 1024 * 1024
VMEM = pl.BlockSpec(memory_space=pltpu.VMEM)


def positive_square_sum(m00, m11, m22, m01, m02, m12):
    mean = (m00 + m11 + m22) * (1.0 / 3.0)
    b00, b11, b22 = m00 - mean, m11 - mean, m22 - mean
    s01, s02, s12 = m01 * m01, m02 * m02, m12 * m12
    p2 = (b00 * b00 + b11 * b11 + b22 * b22) * (1.0 / 6.0) + (s01 + s02 + s12) * (1.0 / 3.0)
    det = b00 * (b11 * b22 - s12) + 2.0 * (m01 * m02) * m12 - b11 * s02 - b22 * s01
    mean2 = mean * mean
    whole = mean * (mean2 - 3.0 * p2) + det
    up = whole >= 0.0
    safe = jnp.maximum(p2, 1e-24)
    inv = lax.rsqrt(safe)
    p = safe * inv
    half = 0.25 * (det * inv) * (inv * inv)
    half = jnp.where(up, half, -half) + 0.5
    half = jnp.minimum(jnp.maximum(half, 0.0), 1.0)
    t = jnp.sqrt(half)
    c = jnp.full_like(t, COS_THIRD[-1])
    for value in COS_THIRD[-2::-1]:
        c = c * t + value
    pc = p * c
    lead = jnp.where(up, mean, -mean)
    largest = lead + 2.0 * pc
    square = largest * largest
    norm = 6.0 * p2 + 3.0 * mean2
    rest = lead - pc
    return jnp.where(
        up, jnp.where(rest > 0.0, norm, square), jnp.where(rest < 0.0, norm - square, 0.0)
    )


def sides(merged, fn):
    if merged:
        return [jnp.where(lax.axis_index("pencil") == 0, fn(1), fn(-1))]
    return [fn(1), fn(-1)]


def is_left():
    return lax.axis_index("comp") == 0


def pack_columns(tiles, out):
    Y = out.shape[0]
    left = is_left()
    lane = lax.broadcasted_iota(jnp.int32, (Y, LANES), 1)
    slot = jnp.where(left, (lane + 2) // 2 % (LANES // 2), lane // 2)
    acc = jnp.zeros((Y, LANES), F32)
    for entry, plane in enumerate(tiles):
        X = plane.shape[1]
        tile = jnp.where(left, plane[:, X - LANES : X], plane[:, 0:LANES])
        turned = pltpu.roll(tile, 2 * entry, 1) if entry else tile
        acc = jnp.where(slot == entry, turned, acc)
    out[...] = jnp.where(left, pltpu.roll(acc, 2, 1), acc)


def put_columns(u, d, out):
    Z = d.shape[0]
    pack_columns([u.at[c, z] for c in range(3) for z in range(Z)] + [d.at[z] for z in range(Z)], out)


def is_even():
    return lax.axis_index("slab") % 2 == 0


def put_planes(u, d, first, second):
    _, Z, Y, X = u.shape
    even = is_even()
    for c in range(3):
        up, down = u[c, Z - 2 : Z], u[c, 0:2]
        first[2 * c : 2 * c + 2] = jnp.where(even, up, down)
        second[2 * c : 2 * c + 2] = jnp.where(even, down, up)
    up, down = d[Z - 1], d[0]
    first[6] = jnp.where(even, up, down)
    second[6] = jnp.where(even, down, up)


def plane_readers(first, second):
    even = is_even()

    def low(*at):
        return jnp.where(even, second[at], first[at])

    def high(*at):
        return jnp.where(even, first[at], second[at])

    return low, high


def column_reader(packet):
    rows = packet.shape[0]
    left = is_left()
    lane = lax.broadcasted_iota(jnp.int32, (rows, LANES), 1)
    inside = jnp.where(left, lane, LANES - 1 - lane) < 2
    packet = jnp.where(left, packet, pltpu.roll(packet, LANES - 2, 1))

    def column(entry):
        shift = (LANES - 2 * entry) % LANES
        turned = pltpu.roll(packet, shift, 1) if shift else packet
        return jnp.where(inside, turned, 0.0)

    return column


def load_kernel(u_hbm, label_hbm, u, d, cols, first, second, label, sems):
    copies = [pltpu.make_async_copy(u_hbm.at[c], u.at[c], sems.at[c]) for c in range(3)]
    copies.append(pltpu.make_async_copy(label_hbm, label, sems.at[3]))
    for copy in copies:
        copy.start()
    copies[3].wait()
    d[...] = DAMAGE_LEVEL * label[...].astype(F32)
    for copy in copies[:3]:
        copy.wait()
    put_planes(u, d, first, second)
    put_columns(u, d, cols)


def rows_kernel(merged, u, d, xh, *outs):
    _, Z, Y, X = u.shape
    for c in range(3):
        for layer in range(2):
            row = lambda s: u[c, :, Y - 2 + layer if s > 0 else layer, :]
            for ref, value in zip(outs, sides(merged, row)):
                ref[2 * c + layer] = value
    for ref, value in zip(outs, sides(merged, lambda s: d[:, Y - 1 if s > 0 else 0, :])):
        ref[6] = value
    corner = lambda s: xh[Y - 1 : Y, :] if s > 0 else xh[0:1, :]
    for ref, value in zip(outs, sides(merged, corner)):
        ref[7, 0:1, 0:LANES] = value


def corners_kernel(merged, first, second, cols, *outs):
    _, Y, X = first.shape
    low, high = plane_readers(first, second)
    near = [low(2 * c + 1) for c in range(3)] + [high(2 * c) for c in range(3)]
    for k, plane in enumerate(near):
        edge = lambda s: plane[Y - 1 : Y, :] if s > 0 else plane[0:1, :]
        for ref, value in zip(outs, sides(merged, edge)):
            ref[k : k + 1, :] = value
    pack_columns(near, cols)


def row_keepers(merged):
    if not merged:
        return (lambda value: value), (lambda value: value)
    py = lax.axis_index("pencil")
    return (
        lambda value: jnp.where(py != 0, value, 0.0),
        lambda value: jnp.where(py == 0, value, 0.0),
    )


def lay_out(merged, u, d, xh, ylo, yhi, U, D):
    _, Z, Y, X = u.shape
    H = SUB
    low_of, high_of = row_keepers(merged)
    column = column_reader(xh[...])
    low_corner = column_reader(low_of(ylo[7, 0:1, 0:LANES]))
    high_corner = column_reader(high_of(yhi[7, 0:1, 0:LANES]))
    for c in range(3):
        U[c, :, H : H + Y, 0:X] = u[c]
        for layer in range(2):
            low, high = low_of(ylo[2 * c + layer]), high_of(yhi[2 * c + layer])
            for z in range(Z):
                U[c, z, H - 2 + layer : H - 1 + layer, 0:X] = low[z : z + 1]
                U[c, z, H + Y + layer : H + Y + layer + 1, 0:X] = high[z : z + 1]
        for z in range(Z):
            entry = c * Z + z
            U[c, z, H : H + Y, X : X + LANES] = column(entry)
            U[c, z, H - 1 : H, X : X + LANES] = low_corner(entry)
            U[c, z, H + Y : H + Y + 1, X : X + LANES] = high_corner(entry)
    D[:, H : H + Y, 0:X] = d[...]
    low, high = low_of(ylo[6]), high_of(yhi[6])
    for z in range(Z):
        D[z, H - 1 : H, 0:X] = low[z : z + 1]
        D[z, H + Y : H + Y + 1, 0:X] = high[z : z + 1]
        D[z, H : H + Y, X : X + LANES] = column(3 * Z + z)


def lay_out_face(merged, k, far, near, low_rows, high_rows, columns, F):
    Y, X = near(0).shape
    H = SUB
    low_of, high_of = row_keepers(merged)
    column = column_reader(columns[...])
    for c in range(3):
        F[c, 0, H : H + Y, 0:X] = far(c)
        F[c, 1, H : H + Y, 0:X] = near(c)
        F[c, 1, H : H + Y, X : X + LANES] = column(3 * k + c)
        row = 3 * k + c
        F[c, 1, H - 1 : H, 0:X] = low_of(low_rows[row : row + 1, :])
        F[c, 1, H + Y : H + Y + 1, 0:X] = high_of(high_rows[row : row + 1, :])


def ahead(value):
    return pltpu.roll(value, value.shape[-1] - 1, value.ndim - 1)


def behind(value):
    return pltpu.roll(value, 1, value.ndim - 1)


ZZ, ZY, ZX, YY, YX, XX = range(6)
PAIRS = ((ZZ, ZY, ZX), (ZY, YY, YX), (ZX, YX, XX))


def gradients(at, row, count):
    rows = slice(row, row + count)
    gz, gy, gx = [], [], []
    for c in range(3):
        mid = at(c, 0)
        gz.append(at(c, 1)[rows, :] - at(c, -1)[rows, :])
        gy.append(mid[row + 1 : row + count + 1, :] - mid[row - 1 : row + count - 1, :])
        value = mid[rows, :]
        gx.append(ahead(value) - behind(value))
    return gz, gy, gx


def stiffness(damage):
    keep = 1.0 - damage
    return 0.5 * (keep * keep + RESIDUAL_STIFF)


def energy_of(gz, gy, gx, X):
    cut = lambda value: value[:, 0:X]
    z0, y1, x2 = cut(gz[0]), cut(gy[1]), cut(gx[2])
    mzy = 0.5 * cut(gy[0] + gz[1])
    mzx = 0.5 * cut(gx[0] + gz[2])
    myx = 0.5 * cut(gx[1] + gy[2])
    squares = positive_square_sum(z0, y1, x2, mzy, mzx, myx)
    grow = jnp.maximum(z0 + y1 + x2, 0.0)
    return (0.25 * 0.5 * LAME_FIRST) * (grow * grow) + (0.25 * SHEAR_MODULUS) * squares


def new_damage(mid, below, above, t, energy, tough):
    X = tough.shape[-1]
    r = t * SUB
    value = mid[r : r + SUB, :]
    core = value[:, 0:X]
    lap = (
        below
        + above
        + mid[r + 1 : r + SUB + 1, 0:X]
        + mid[r - 1 : r + SUB - 1, 0:X]
        + (ahead(value) + behind(value))[:, 0:X]
        - 6.0 * core
    )
    return core + TIME_DAMAGE * (2.0 * (1.0 - core) * energy + tough * (lap - core))


def row_stress(at, damage_plane, S, Y, X):
    H = SUB
    for row in (H - 1, H + Y):
        gz, gy, gx = gradients(at, row, 1)
        h = stiffness(damage_plane[row : row + 1, :])
        total = LAME_FIRST * (gz[0] + gy[1] + gx[2])
        for key, value in (
            (ZY, gy[0] + gz[1]),
            (YY, total + 2.0 * gy[1]),
            (YX, gx[1] + gy[2]),
        ):
            S[key, row : row + 1, 0:X] = (h * value)[:, 0:X]


def plane_stress(at, damage_plane, S, Y, X, then=None):
    row_stress(at, damage_plane, S, Y, X)
    for t in range(1, Y // SUB + 1):
        rows = slice(t * SUB, t * SUB + SUB)
        gz, gy, gx = gradients(at, t * SUB, SUB)
        h = stiffness(damage_plane[rows, :])
        total = LAME_FIRST * (gz[0] + gy[1] + gx[2])
        S[ZZ, rows, 0:X] = (h * (total + 2.0 * gz[0]))[:, 0:X]
        S[YY, rows, 0:X] = (h * (total + 2.0 * gy[1]))[:, 0:X]
        S[ZY, rows, 0:X] = (h * (gy[0] + gz[1]))[:, 0:X]
        S[ZX, rows, :] = h * (gx[0] + gz[2])
        S[YX, rows, :] = h * (gx[1] + gy[2])
        S[XX, rows, :] = h * (total + 2.0 * gx[2])
        if then is not None:
            then(t, energy_of(gz, gy, gx, X))


def side_stress(at, damage_plane, S, Y, X):
    turn = LANES
    for t in range(1, Y // SUB + 1):
        r = t * SUB
        rows, out = slice(r, r + SUB), slice(X, X + LANES)
        gz, gy, gx = [], [], []
        for c in range(3):
            mid = at(c, 0)
            gz.append(at(c, 1)[rows, out] - at(c, -1)[rows, out])
            gy.append(mid[r + 1 : r + SUB + 1, out] - mid[r - 1 : r + SUB - 1, out])
            value = mid[rows, :]
            gx.append((ahead(value) - behind(value))[:, out])
        h = stiffness(damage_plane[rows, out])
        total = LAME_FIRST * (gz[0] + gy[1] + gx[2])
        S[ZX, rows, out] = h * (gx[0] + gz[2])
        S[YX, rows, out] = h * (gx[1] + gy[2])
        S[XX, rows, out] = h * (total + 2.0 * gx[2])


def face_stress(at, damage, S, Y, X):
    for t in range(1, Y // SUB + 1):
        rows = slice(t * SUB, t * SUB + SUB)
        gz, gy, gx = gradients(at, t * SUB, SUB)
        h = stiffness(damage(slice((t - 1) * SUB, t * SUB)))
        total = LAME_FIRST * (gz[0] + gy[1] + gx[2])
        for key, value in (
            (ZZ, total + 2.0 * gz[0]),
            (ZY, gy[0] + gz[1]),
            (ZX, gx[0] + gz[2]),
        ):
            S[key, rows, 0:X] = h * value[:, 0:X]


def plane_moved(below, mid, above, u_plane, t, X):
    r = t * SUB
    rows = slice(r, r + SUB)
    out = []
    for c in range(3):
        kz, ky, kx = PAIRS[c]
        value = mid[kx, rows, :]
        force = (
            above[kz, rows, 0:X]
            - below[kz, rows, 0:X]
            + mid[ky, r + 1 : r + SUB + 1, 0:X]
            - mid[ky, r - 1 : r + SUB - 1, 0:X]
            + (ahead(value) - behind(value))[:, 0:X]
        )
        out.append(u_plane(c)[(t - 1) * SUB : t * SUB, :] + (0.5 * TIME_DISP) * force)
    return out


def row_sums(new):
    lane = lax.broadcasted_iota(jnp.int32, (SUB, LANES), 1)
    sums = [jnp.sum(value, axis=-1, keepdims=True) for value in new]
    return jnp.where(lane == 0, sums[0], jnp.where(lane == 1, sums[1], sums[2]))


def means_of(pool, X):
    return (pool * (1.0 / X)).T[0:SUB].astype(jnp.bfloat16)


def inner_kernel(merged, last, *refs):
    rest = list(refs)
    take = lambda k: [rest.pop(0) for _ in range(k)]
    u, d, tough, xh, ylo, yhi = take(6)
    if last:
        weight, sensor = take(2)
    U, D, S, moved, damage = take(5)
    if last:
        part, edge_rows, pool = take(3)
    _, Z, Y, X = u.shape
    tiles = range(1, Y // SUB + 1)
    lay_out(merged, u, d, xh, ylo, yhi, U, D)

    @pl.loop(1, Z - 1)
    def _(z):
        def then(t, energy):
            rows = slice(t * SUB, t * SUB + SUB)
            own = slice((t - 1) * SUB, t * SUB)
            damage[z - 1, own, :] = new_damage(
                D.at[z], D[z - 1, rows, 0:X], D[z + 1, rows, 0:X], t, energy, tough[z, own, :]
            )

        plane_stress(lambda c, dz: U.at[c, z + dz], D.at[z], S.at[z - 1], Y, X, then)

    @pl.loop(2, Z - 2)
    def _(z):
        for t in tiles:
            own = slice((t - 1) * SUB, t * SUB)
            new = plane_moved(
                S.at[z - 2], S.at[z - 1], S.at[z], lambda c: u.at[c, z], t, X
            )
            for c in range(3):
                moved[c, z - 2, own, :] = new[c]
            if last:
                start = pl.multiple_of((z - 2) * Y + (t - 1) * SUB, SUB)
                pool[pl.ds(start, SUB), :] = row_sums(new)

    if last:
        means = means_of(pool[...], X)
        count = lax.axis_size("comp")
        spread = Y * lax.axis_size("pencil")
        index = lax.broadcasted_iota(jnp.int32, (Z * Y, 1), 0)
        plane = lax.axis_index("slab") * Z + index // Y
        row = lax.axis_index("pencil") * Y + index % Y
        ids = (plane * spread + row) * count + lax.axis_index("comp")
        chunk = 8 * LANES
        two, end = 2 * Y, (Z - 2) * Y
        edge_rows[0:two, :] = weight[0:two, :]
        edge_rows[two : 2 * two, :] = weight[end : end + two, :]
        for k in range(sensor.shape[1] // chunk):
            cols = slice(k * chunk, (k + 1) * chunk)
            picks = jnp.where(ids == sensor[:, cols], POINT_GAIN, 0.0).astype(jnp.bfloat16)
            edge_rows[2 * two : 3 * two, cols] = picks[0:two]
            edge_rows[3 * two : 4 * two, cols] = picks[end : end + two]
            value = jnp.dot(means, weight[two:end, cols], preferred_element_type=F32)
            part[:, cols] = value + jnp.dot(means, picks[two:end], preferred_element_type=F32)


def edge_kernel(U, D, tough, first, second, S, damage):
    Z, Y, X = tough.shape
    low, high = plane_readers(first, second)
    for k, z in enumerate((0, Z - 1)):
        for t in range(1, Y // SUB + 1):
            r = t * SUB
            rows = slice(r, r + SUB)
            own = slice((t - 1) * SUB, t * SUB)
            gz, gy, gx = [], [], []
            for c in range(3):
                below = low(2 * c + 1, own) if z == 0 else U[c, z - 1, rows, 0:X]
                above = U[c, z + 1, rows, 0:X] if z == 0 else high(2 * c, own)
                gz.append(above - below)
                gy.append(U[c, z, r + 1 : r + SUB + 1, 0:X] - U[c, z, r - 1 : r + SUB - 1, 0:X])
                value = U[c, z, rows, :]
                gx.append((ahead(value) - behind(value))[:, 0:X])
            h = stiffness(D[z, rows, 0:X])
            total = LAME_FIRST * (gz[0] + gy[1] + gx[2])
            S[k, ZZ, rows, 0:X] = h * (total + 2.0 * gz[0])
            S[k, YY, rows, 0:X] = h * (total + 2.0 * gy[1])
            S[k, XX, rows, 0:X] = h * (total + 2.0 * gx[2])
            S[k, ZY, rows, 0:X] = h * (gy[0] + gz[1])
            S[k, ZX, rows, 0:X] = h * (gx[0] + gz[2])
            S[k, YX, rows, 0:X] = h * (gx[1] + gy[2])
            energy = energy_of(gz, gy, gx, X)
            below = low(6, own) if z == 0 else D[z - 1, rows, 0:X]
            above = D[z + 1, rows, 0:X] if z == 0 else high(6, own)
            damage[k, own, :] = new_damage(D.at[z], below, above, t, energy, tough[z, own, :])


def outer_kernel(merged, last, *refs):
    rest = list(refs)
    take = lambda k: [rest.pop(0) for _ in range(k)]
    u, first, second, low_rows, high_rows, columns, U, D, S, E_in = take(10)
    if last:
        inner_part, edge_rows = take(2)
        E, moved, part = take(3)
    else:
        inner_moved, inner_damage, edge_damage = take(3)
        E, moved, damage, cols, to_first, to_second = take(6)
    del E_in
    low_face, high_face, faces = take(3)
    if last:
        (pool,) = take(1)
    _, Z, Y, X = u.shape
    tiles = range(1, Y // SUB + 1)
    low, high = plane_readers(first, second)
    lay_out_face(
        merged, 0, lambda c: low(2 * c), lambda c: low(2 * c + 1), low_rows, high_rows, columns, low_face
    )
    lay_out_face(
        merged, 1, lambda c: high(2 * c + 1), lambda c: high(2 * c), low_rows, high_rows, columns, high_face
    )

    def at_plane(z):
        def at(c, dz):
            k = z + dz
            if k < 0:
                return low_face.at[c, 2 + k]
            if k >= Z:
                return high_face.at[c, Z + 1 - k]
            return U.at[c, k]

        return at

    face_stress(at_plane(-1), lambda own: low(6, own), faces.at[0], Y, X)
    face_stress(at_plane(Z), lambda own: high(6, own), faces.at[1], Y, X)
    for k, z in enumerate((0, Z - 1)):
        row_stress(at_plane(z), D.at[z], E.at[k], Y, X)
        side_stress(at_plane(z), D.at[z], E.at[k], Y, X)

    def stress(z):
        if z < 0:
            return faces.at[0]
        if z >= Z:
            return faces.at[1]
        if z == 0:
            return E.at[0]
        if z == Z - 1:
            return E.at[1]
        return S.at[z - 1]

    for k, z in enumerate((0, 1, Z - 2, Z - 1)):
        for t in tiles:
            own = slice((t - 1) * SUB, t * SUB)
            new = plane_moved(stress(z - 1), stress(z), stress(z + 1), lambda c: u.at[c, z], t, X)
            for c in range(3):
                moved[c, k if last else z, own, :] = new[c]
            if last:
                start = k * Y + (t - 1) * SUB
                pool[start : start + SUB, :] = row_sums(new)
    if last:
        means = means_of(pool[...], X)
        means = jnp.concatenate([means, means], axis=1)
        chunk = 8 * LANES
        sub = lax.broadcasted_iota(jnp.int32, (SUB, LANES), 0)
        for k in range(edge_rows.shape[1] // chunk):
            start = slice(k * chunk, (k + 1) * chunk)
            value = inner_part[:, start] + jnp.dot(
                means, edge_rows[:, start], preferred_element_type=F32
            )
            for c in range(3):
                tile = jnp.zeros((SUB, LANES), F32)
                for j in range(SUB):
                    piece = value[c : c + 1, j * LANES : (j + 1) * LANES]
                    tile = jnp.where(sub == j, piece, tile)
                part[c, k] = tile
    else:
        for c in range(3):
            moved[c, 2 : Z - 2] = inner_moved[c]
        damage[0] = edge_damage[0]
        damage[1 : Z - 1] = inner_damage[...]
        damage[Z - 1] = edge_damage[1]
        put_planes(moved, damage, to_first, to_second)
        put_columns(moved, damage, cols)


def fields_kernel(inner_moved, edge_moved, inner_damage, edge_damage, moved, damage):
    Z = damage.shape[0]
    for c in range(3):
        moved[c, 0:2] = edge_moved[c, 0:2]
        moved[c, 2 : Z - 2] = inner_moved[c]
        moved[c, Z - 2 : Z] = edge_moved[c, 2:4]
    damage[0] = edge_damage[0]
    damage[1 : Z - 1] = inner_damage[...]
    damage[Z - 1] = edge_damage[1]


def finish_kernel(count, *refs):
    out = refs[-1]
    total = refs[0][...]
    for ref in refs[1:-1]:
        total = total + ref[...]
    for c in range(3):
        for k in range(total.shape[1]):
            for j in range(SUB):
                start = (k * SUB + j) * LANES
                out[c : c + 1, start : start + LANES] = total[c, k, j : j + 1, :]


def call(kernel, outs, *args, scratch=(), name=None, in_specs=None, micros=1, alias=None):
    many = isinstance(outs, (list, tuple))
    return pl.pallas_call(
        kernel,
        out_shape=outs,
        in_specs=in_specs or [VMEM] * len(args),
        out_specs=[VMEM] * len(outs) if many else VMEM,
        scratch_shapes=list(scratch),
        compiler_params=pltpu.CompilerParams(vmem_limit_bytes=VMEM_LIMIT),
        cost_estimate=pl.CostEstimate(
            flops=0, bytes_accessed=micros * 3_000_000, transcendentals=0
        ),
        input_output_aliases=alias or {},
        name=name,
    )(*args)


def up_pairs(count):
    return [(i, i + 1) for i in range(count - 1)]


def down_pairs(count):
    return [(i + 1, i) for i in range(count - 1)]


def all_sum(value):
    for axis in ("comp", "pencil"):
        count = lax.axis_size(axis)
        bit = 1
        while bit < count:
            value = value + lax.ppermute(value, axis, [(i, i ^ bit) for i in range(count)])
            bit *= 2
    count = lax.axis_size("slab")
    bit = 1
    while count // bit > 4:
        value = value + lax.ppermute(value, "slab", [(i, i ^ bit) for i in range(count)])
        bit *= 2
    terms = [value]
    for k in range(1, count // bit):
        terms.append(lax.ppermute(value, "slab", [(i, i ^ (k * bit)) for i in range(count)]))
    return terms


def local(u_start, toughness, crack_label, obs_weight, sensor_cell):
    Z, Y, X = toughness.shape
    slabs, pencils = lax.axis_size("slab"), lax.axis_size("pencil")
    if lax.axis_size("comp") != 2 or Z < 6 or Z % SUB or 8 * Z > LANES:
        raise ValueError("unsupported block")
    merged = pencils == 2
    n = 1 if merged else 2
    shape = jax.ShapeDtypeStruct
    field, vector = shape((Z, Y, X), F32), shape((3, Z, Y, X), F32)
    columns = shape((Y, LANES), F32)
    sensors = sensor_cell.shape[0]
    rows, lanes = Y + 2 * SUB, X + LANES
    y_up, y_down = up_pairs(pencils), down_pairs(pencils)
    y_pairs = [y_up + y_down] if merged else [y_up, y_down]
    margins = [
        shape((3, Z, rows, lanes), F32),
        shape((Z, rows, lanes), F32),
        shape((Z - 2, 6, rows, lanes), F32),
    ]
    scratch = [
        pltpu.VMEM((3, 2, rows, lanes), F32),
        pltpu.VMEM((3, 2, rows, lanes), F32),
        pltpu.VMEM((2, 3, rows, lanes), F32),
    ]
    edges = shape((2, 6, rows, lanes), F32)
    inner_fields = [shape((3, Z - 4, Y, X), F32), shape((Z - 2, Y, X), F32)]
    planes = shape((7, Y, X), F32)
    evens = [pair for pair in up_pairs(slabs) + down_pairs(slabs) if min(pair) % 2 == 0]
    odds = [pair for pair in up_pairs(slabs) + down_pairs(slabs) if min(pair) % 2 == 1]
    swap = [(0, 1), (1, 0)]
    moved, damage, cols, to_first, to_second = call(
        load_kernel,
        [vector, field, columns, planes, planes],
        u_start,
        crack_label,
        scratch=[pltpu.VMEM((Z, Y, X), jnp.int32), pltpu.SemaphoreType.DMA((4,))],
        in_specs=[pl.BlockSpec(memory_space=pltpu.HBM)] * 2,
        name="load",
    )
    for step in range(2):
        last = step == 1
        first = lax.ppermute(to_first, "slab", evens)
        second = lax.ppermute(to_second, "slab", odds)
        xh = lax.ppermute(cols, "comp", swap)
        out = call(
            functools.partial(rows_kernel, merged),
            [shape((8, Z, X), F32)] * n,
            moved,
            damage,
            xh,
            name="rows",
        )
        ys = [lax.ppermute(y, "pencil", pairs) for y, pairs in zip(out, y_pairs)]
        args = [moved, damage, toughness, xh, ys[0], ys[-1]]
        outs = margins + inner_fields
        inner_scratch = []
        if last:
            args += [obs_weight.reshape(Z * Y, sensors), sensor_cell.reshape(1, sensors)]
            outs = outs + [shape((SUB, sensors), F32), shape((8 * Y, sensors), jnp.bfloat16)]
            inner_scratch = [pltpu.VMEM(((Z - 4) * Y, LANES), F32)]
        U, D, S, inner_moved, inner_damage, *more = call(
            functools.partial(inner_kernel, merged, last),
            outs,
            *args,
            scratch=inner_scratch,
            name="inner",
            micros=4,
        )
        *corner_rows, corner_columns = call(
            lambda a, b, _, *rest: corners_kernel(merged, a, b, rest[-1], *rest[:-1]),
            [shape((SUB, X), F32)] * n + [columns],
            first,
            second,
            inner_damage,
            name="corners",
        )
        crows = [lax.ppermute(y, "pencil", pairs) for y, pairs in zip(corner_rows, y_pairs)]
        ccols = lax.ppermute(corner_columns, "comp", swap)
        E, edge_damage = call(
            edge_kernel,
            [edges, shape((2, Y, X), F32)],
            U,
            D,
            toughness,
            first,
            second,
            name="edge",
        )
        args = [moved, first, second, crows[0], crows[-1], ccols, U, D, S, E]
        if last:
            _, edge_moved, part = call(
                functools.partial(outer_kernel, merged, True),
                [
                    edges,
                    shape((3, 4, Y, X), F32),
                    shape((3, sensors // (SUB * LANES), SUB, LANES), F32),
                ],
                *args,
                *more,
                scratch=scratch + [pltpu.VMEM((4 * Y, LANES), F32)],
                name="outer2",
                alias={9: 0},
            )
            moved, damage = call(
                fields_kernel,
                [vector, field],
                inner_moved,
                edge_moved,
                inner_damage,
                edge_damage,
                name="fields",
            )
        else:
            _, moved, damage, cols, to_first, to_second = call(
                functools.partial(outer_kernel, merged, False),
                [edges, vector, field, columns, planes, planes],
                *args,
                inner_moved,
                inner_damage,
                edge_damage,
                scratch=scratch,
                name="outer1",
                alias={9: 0},
            )
    terms = all_sum(part)
    readings = call(
        functools.partial(finish_kernel, len(terms)),
        shape((3, sensors), F32),
        *terms,
        name="finish",
    )
    return moved, damage, readings


def solution(mesh):
    return jax.shard_map(
        local,
        mesh=mesh,
        in_specs=(
            P(None, ("groups", "slab"), "pencil", "comp"),
            P(("groups", "slab"), "pencil", "comp"),
            P(("groups", "slab"), "pencil", "comp"),
            P("slab", "pencil", "comp", None),
            P(),
        ),
        out_specs=(
            P(None, ("groups", "slab"), "pencil", "comp"),
            P(("groups", "slab"), "pencil", "comp"),
            P(None, "groups"),
        ),
        check_vma=False,
    )
```

```python
import functools

import jax
import jax.numpy as jnp
from jax import lax
from jax.experimental import pallas as pl
from jax.experimental.pallas import tpu as pltpu
from jax.sharding import PartitionSpec as P

SHEAR_MODULUS = 1.0
LAME_FIRST = 1.5
RESIDUAL_STIFF = 0.001
TIME_DISP = 0.15
TIME_DAMAGE = 0.08
DAMAGE_LEVEL = 0.45
POINT_GAIN = 8.0
LANES = 128
SUB = 8
COS_THIRD = (
    0.5000000037331834,
    0.5773496613984853,
    -0.11109449276880777,
    0.05327935086024303,
    -0.031925412185213546,
    0.01960032102518762,
    -0.010237508432464154,
    0.003654119632233793,
    -0.0006260453394989179,
)
F32 = jnp.float32
VMEM_LIMIT = 24 * 1024 * 1024
VMEM = pl.BlockSpec(memory_space=pltpu.VMEM)


def positive_square_sum(m00, m11, m22, m01, m02, m12):
    mean = (m00 + m11 + m22) * (1.0 / 3.0)
    b00, b11, b22 = m00 - mean, m11 - mean, m22 - mean
    s01, s02, s12 = m01 * m01, m02 * m02, m12 * m12
    p2 = (b00 * b00 + b11 * b11 + b22 * b22) * (1.0 / 6.0) + (s01 + s02 + s12) * (1.0 / 3.0)
    det = b00 * (b11 * b22 - s12) + 2.0 * (m01 * m02) * m12 - b11 * s02 - b22 * s01
    mean2 = mean * mean
    whole = mean * (mean2 - 3.0 * p2) + det
    up = whole >= 0.0
    safe = jnp.maximum(p2, 1e-24)
    inv = lax.rsqrt(safe)
    p = safe * inv
    half = 0.25 * (det * inv) * (inv * inv)
    half = jnp.where(up, half, -half) + 0.5
    half = jnp.minimum(jnp.maximum(half, 0.0), 1.0)
    t = jnp.sqrt(half)
    c = jnp.full_like(t, COS_THIRD[-1])
    for value in COS_THIRD[-2::-1]:
        c = c * t + value
    pc = p * c
    lead = jnp.where(up, mean, -mean)
    largest = lead + 2.0 * pc
    square = largest * largest
    norm = 6.0 * p2 + 3.0 * mean2
    rest = lead - pc
    return jnp.where(
        up, jnp.where(rest > 0.0, norm, square), jnp.where(rest < 0.0, norm - square, 0.0)
    )


def sides(merged, fn):
    if merged:
        return [jnp.where(lax.axis_index("pencil") == 0, fn(1), fn(-1))]
    return [fn(1), fn(-1)]


def is_left():
    return lax.axis_index("comp") == 0


def pack_columns(tiles, out):
    Y = out.shape[0]
    left = is_left()
    lane = lax.broadcasted_iota(jnp.int32, (Y, LANES), 1)
    slot = jnp.where(left, (lane + 2) // 2 % (LANES // 2), lane // 2)
    acc = jnp.zeros((Y, LANES), F32)
    for entry, plane in enumerate(tiles):
        X = plane.shape[1]
        tile = jnp.where(left, plane[:, X - LANES : X], plane[:, 0:LANES])
        turned = pltpu.roll(tile, 2 * entry, 1) if entry else tile
        acc = jnp.where(slot == entry, turned, acc)
    out[...] = jnp.where(left, pltpu.roll(acc, 2, 1), acc)


def put_columns(u, d, out):
    Z = d.shape[0]
    pack_columns([u.at[c, z] for c in range(3) for z in range(Z)] + [d.at[z] for z in range(Z)], out)


def is_even():
    return lax.axis_index("slab") % 2 == 0


def put_planes(u, d, first, second):
    _, Z, Y, X = u.shape
    even = is_even()
    for c in range(3):
        up, down = u[c, Z - 2 : Z], u[c, 0:2]
        first[2 * c : 2 * c + 2] = jnp.where(even, up, down)
        second[2 * c : 2 * c + 2] = jnp.where(even, down, up)
    up, down = d[Z - 1], d[0]
    first[6] = jnp.where(even, up, down)
    second[6] = jnp.where(even, down, up)


def plane_readers(first, second):
    even = is_even()

    def low(*at):
        return jnp.where(even, second[at], first[at])

    def high(*at):
        return jnp.where(even, first[at], second[at])

    return low, high


def column_reader(packet):
    rows = packet.shape[0]
    left = is_left()
    lane = lax.broadcasted_iota(jnp.int32, (rows, LANES), 1)
    inside = jnp.where(left, lane, LANES - 1 - lane) < 2
    packet = jnp.where(left, packet, pltpu.roll(packet, LANES - 2, 1))

    def column(entry):
        shift = (LANES - 2 * entry) % LANES
        turned = pltpu.roll(packet, shift, 1) if shift else packet
        return jnp.where(inside, turned, 0.0)

    return column


def load_kernel(u_hbm, label_hbm, u, d, cols, first, second, label, sems):
    copies = [pltpu.make_async_copy(u_hbm.at[c], u.at[c], sems.at[c]) for c in range(3)]
    copies.append(pltpu.make_async_copy(label_hbm, label, sems.at[3]))
    for copy in copies:
        copy.start()
    copies[3].wait()
    d[...] = DAMAGE_LEVEL * label[...].astype(F32)
    for copy in copies[:3]:
        copy.wait()
    put_planes(u, d, first, second)
    put_columns(u, d, cols)


def rows_kernel(merged, u, d, xh, *outs):
    _, Z, Y, X = u.shape
    for c in range(3):
        for layer in range(2):
            row = lambda s: u[c, :, Y - 2 + layer if s > 0 else layer, :]
            for ref, value in zip(outs, sides(merged, row)):
                ref[2 * c + layer] = value
    for ref, value in zip(outs, sides(merged, lambda s: d[:, Y - 1 if s > 0 else 0, :])):
        ref[6] = value
    corner = lambda s: xh[Y - 1 : Y, :] if s > 0 else xh[0:1, :]
    for ref, value in zip(outs, sides(merged, corner)):
        ref[7, 0:1, 0:LANES] = value


def corners_kernel(merged, first, second, cols, *outs):
    _, Y, X = first.shape
    low, high = plane_readers(first, second)
    near = [low(2 * c + 1) for c in range(3)] + [high(2 * c) for c in range(3)]
    for k, plane in enumerate(near):
        edge = lambda s: plane[Y - 1 : Y, :] if s > 0 else plane[0:1, :]
        for ref, value in zip(outs, sides(merged, edge)):
            ref[k : k + 1, :] = value
    pack_columns(near, cols)


def row_keepers(merged):
    if not merged:
        return (lambda value: value), (lambda value: value)
    py = lax.axis_index("pencil")
    return (
        lambda value: jnp.where(py != 0, value, 0.0),
        lambda value: jnp.where(py == 0, value, 0.0),
    )


def lay_out_columns(u, d, xh, U, D):
    _, Z, Y, X = u.shape
    H = SUB
    column = column_reader(xh[...])
    for c in range(3):
        U[c, :, H : H + Y, 0:X] = u[c]
        for z in range(Z):
            U[c, z, H : H + Y, X : X + LANES] = column(c * Z + z)
    D[:, H : H + Y, 0:X] = d[...]
    for z in range(Z):
        D[z, H : H + Y, X : X + LANES] = column(3 * Z + z)


def lay_out_rows(merged, ylo, yhi, U, D):
    Z, X = D.shape[0], ylo.shape[2]
    Y, H = D.shape[1] - 2 * SUB, SUB
    low_of, high_of = row_keepers(merged)
    low_corner = column_reader(low_of(ylo[7, 0:1, 0:LANES]))
    high_corner = column_reader(high_of(yhi[7, 0:1, 0:LANES]))
    for c in range(3):
        for layer in range(2):
            low, high = low_of(ylo[2 * c + layer]), high_of(yhi[2 * c + layer])
            for z in range(Z):
                U[c, z, H - 2 + layer : H - 1 + layer, 0:X] = low[z : z + 1]
                U[c, z, H + Y + layer : H + Y + layer + 1, 0:X] = high[z : z + 1]
        for z in range(Z):
            U[c, z, H - 1 : H, X : X + LANES] = low_corner(c * Z + z)
            U[c, z, H + Y : H + Y + 1, X : X + LANES] = high_corner(c * Z + z)
    low, high = low_of(ylo[6]), high_of(yhi[6])
    for z in range(Z):
        D[z, H - 1 : H, 0:X] = low[z : z + 1]
        D[z, H + Y : H + Y + 1, 0:X] = high[z : z + 1]


def lay_out_face(merged, k, far, near, low_rows, high_rows, columns, F):
    Y, X = near(0).shape
    H = SUB
    low_of, high_of = row_keepers(merged)
    column = column_reader(columns[...])
    for c in range(3):
        F[c, 0, H : H + Y, 0:X] = far(c)
        F[c, 1, H : H + Y, 0:X] = near(c)
        F[c, 1, H : H + Y, X : X + LANES] = column(3 * k + c)
        row = 3 * k + c
        F[c, 1, H - 1 : H, 0:X] = low_of(low_rows[row : row + 1, :])
        F[c, 1, H + Y : H + Y + 1, 0:X] = high_of(high_rows[row : row + 1, :])


def ahead(value):
    return pltpu.roll(value, value.shape[-1] - 1, value.ndim - 1)


def behind(value):
    return pltpu.roll(value, 1, value.ndim - 1)


ZZ, ZY, ZX, YY, YX, XX = range(6)
PAIRS = ((ZZ, ZY, ZX), (ZY, YY, YX), (ZX, YX, XX))


def gradients(at, row, count):
    rows = slice(row, row + count)
    gz, gy, gx = [], [], []
    for c in range(3):
        mid = at(c, 0)
        gz.append(at(c, 1)[rows, :] - at(c, -1)[rows, :])
        gy.append(mid[row + 1 : row + count + 1, :] - mid[row - 1 : row + count - 1, :])
        value = mid[rows, :]
        gx.append(ahead(value) - behind(value))
    return gz, gy, gx


def stiffness(damage):
    keep = 1.0 - damage
    return 0.5 * (keep * keep + RESIDUAL_STIFF)


def energy_of(gz, gy, gx, X):
    cut = lambda value: value[:, 0:X]
    z0, y1, x2 = cut(gz[0]), cut(gy[1]), cut(gx[2])
    mzy = 0.5 * cut(gy[0] + gz[1])
    mzx = 0.5 * cut(gx[0] + gz[2])
    myx = 0.5 * cut(gx[1] + gy[2])
    squares = positive_square_sum(z0, y1, x2, mzy, mzx, myx)
    grow = jnp.maximum(z0 + y1 + x2, 0.0)
    return (0.25 * 0.5 * LAME_FIRST) * (grow * grow) + (0.25 * SHEAR_MODULUS) * squares


def new_damage(mid, below, above, t, energy, tough):
    X = tough.shape[-1]
    r = t * SUB
    value = mid[r : r + SUB, :]
    core = value[:, 0:X]
    lap = (
        below
        + above
        + mid[r + 1 : r + SUB + 1, 0:X]
        + mid[r - 1 : r + SUB - 1, 0:X]
        + (ahead(value) + behind(value))[:, 0:X]
        - 6.0 * core
    )
    return core + TIME_DAMAGE * (2.0 * (1.0 - core) * energy + tough * (lap - core))


def row_stress(at, damage_plane, S, Y, X):
    H = SUB
    for row in (H - 1, H + Y):
        gz, gy, gx = gradients(at, row, 1)
        h = stiffness(damage_plane[row : row + 1, :])
        total = LAME_FIRST * (gz[0] + gy[1] + gx[2])
        for key, value in (
            (ZY, gy[0] + gz[1]),
            (YY, total + 2.0 * gy[1]),
            (YX, gx[1] + gy[2]),
        ):
            S[key, row : row + 1, 0:X] = (h * value)[:, 0:X]


def tile_stress(at, damage_plane, S, t, X):
    rows = slice(t * SUB, t * SUB + SUB)
    gz, gy, gx = gradients(at, t * SUB, SUB)
    h = stiffness(damage_plane[rows, :])
    total = LAME_FIRST * (gz[0] + gy[1] + gx[2])
    S[ZZ, rows, 0:X] = (h * (total + 2.0 * gz[0]))[:, 0:X]
    S[YY, rows, 0:X] = (h * (total + 2.0 * gy[1]))[:, 0:X]
    S[ZY, rows, 0:X] = (h * (gy[0] + gz[1]))[:, 0:X]
    S[ZX, rows, :] = h * (gx[0] + gz[2])
    S[YX, rows, :] = h * (gx[1] + gy[2])
    S[XX, rows, :] = h * (total + 2.0 * gx[2])
    return energy_of(gz, gy, gx, X)


def side_stress(at, damage_plane, S, Y, X):
    turn = LANES
    for t in range(1, Y // SUB + 1):
        r = t * SUB
        rows, out = slice(r, r + SUB), slice(X, X + LANES)
        gz, gy, gx = [], [], []
        for c in range(3):
            mid = at(c, 0)
            gz.append(at(c, 1)[rows, out] - at(c, -1)[rows, out])
            gy.append(mid[r + 1 : r + SUB + 1, out] - mid[r - 1 : r + SUB - 1, out])
            value = mid[rows, :]
            gx.append((ahead(value) - behind(value))[:, out])
        h = stiffness(damage_plane[rows, out])
        total = LAME_FIRST * (gz[0] + gy[1] + gx[2])
        S[ZX, rows, out] = h * (gx[0] + gz[2])
        S[YX, rows, out] = h * (gx[1] + gy[2])
        S[XX, rows, out] = h * (total + 2.0 * gx[2])


def face_stress(at, damage, S, Y, X):
    for t in range(1, Y // SUB + 1):
        rows = slice(t * SUB, t * SUB + SUB)
        gz, gy, gx = gradients(at, t * SUB, SUB)
        h = stiffness(damage(slice((t - 1) * SUB, t * SUB)))
        total = LAME_FIRST * (gz[0] + gy[1] + gx[2])
        for key, value in (
            (ZZ, total + 2.0 * gz[0]),
            (ZY, gy[0] + gz[1]),
            (ZX, gx[0] + gz[2]),
        ):
            S[key, rows, 0:X] = h * value[:, 0:X]


def plane_moved(below, mid, above, u_plane, t, X):
    r = t * SUB
    rows = slice(r, r + SUB)
    out = []
    for c in range(3):
        kz, ky, kx = PAIRS[c]
        value = mid[kx, rows, :]
        force = (
            above[kz, rows, 0:X]
            - below[kz, rows, 0:X]
            + mid[ky, r + 1 : r + SUB + 1, 0:X]
            - mid[ky, r - 1 : r + SUB - 1, 0:X]
            + (ahead(value) - behind(value))[:, 0:X]
        )
        out.append(u_plane(c)[(t - 1) * SUB : t * SUB, :] + (0.5 * TIME_DISP) * force)
    return out


def row_sums(new):
    lane = lax.broadcasted_iota(jnp.int32, (SUB, LANES), 1)
    sums = [jnp.sum(value, axis=-1, keepdims=True) for value in new]
    return jnp.where(lane == 0, sums[0], jnp.where(lane == 1, sums[1], sums[2]))


def means_of(pool, X):
    return (pool * (1.0 / X)).T[0:SUB].astype(jnp.bfloat16)


def inner_tiles(z, tiles, U, D, S, tough, damage):
    X = tough.shape[2]
    for t in tiles:
        energy = tile_stress(lambda c, dz: U.at[c, z + dz], D.at[z], S.at[z - 1], t, X)
        rows = slice(t * SUB, t * SUB + SUB)
        own = slice((t - 1) * SUB, t * SUB)
        damage[z - 1, own, :] = new_damage(
            D.at[z], D[z - 1, rows, 0:X], D[z + 1, rows, 0:X], t, energy, tough[z, own, :]
        )


def middle_kernel(u, d, tough, xh, *rest):
    U, D, S, damage = rest[-4:]
    Z, Y, X = tough.shape
    lay_out_columns(u, d, xh, U, D)

    @pl.loop(1, Z - 1)
    def _(z):
        inner_tiles(z, range(2, Y // SUB), U, D, S, tough, damage)


def inner_kernel(merged, last, *refs):
    rest = list(refs)
    take = lambda k: [rest.pop(0) for _ in range(k)]
    u, tough, ylo, yhi, after = take(5)
    del after
    if last:
        (weight,) = take(1)
    take(4)
    U, D, S, damage, moved = take(5)
    if last:
        part, pool = take(2)
    _, Z, Y, X = u.shape
    count = Y // SUB
    lay_out_rows(merged, ylo, yhi, U, D)

    @pl.loop(1, Z - 1)
    def _(z):
        row_stress(lambda c, dz: U.at[c, z + dz], D.at[z], S.at[z - 1], Y, X)
        inner_tiles(z, (1, count), U, D, S, tough, damage)

    @pl.loop(2, Z - 2)
    def _(z):
        for t in range(1, count + 1):
            own = slice((t - 1) * SUB, t * SUB)
            new = plane_moved(
                S.at[z - 2], S.at[z - 1], S.at[z], lambda c: u.at[c, z], t, X
            )
            for c in range(3):
                moved[c, z - 2, own, :] = new[c]
            if last:
                start = pl.multiple_of((z - 2) * Y + (t - 1) * SUB, SUB)
                pool[pl.ds(start, SUB), :] = row_sums(new)

    if last:
        means = means_of(pool[...], X)
        means = jnp.concatenate([means, means], axis=1)
        chunk = 8 * LANES
        for k in range(weight.shape[1] // chunk):
            cols = slice(k * chunk, (k + 1) * chunk)
            part[:, cols] = jnp.dot(means, weight[:, cols], preferred_element_type=F32)


def weights_kernel(Z, Y, weight, sensor, after, inner, outer):
    del after
    count = lax.axis_size("comp")
    spread = Y * lax.axis_size("pencil")
    index = lax.broadcasted_iota(jnp.int32, (Z * Y, 1), 0)
    plane = lax.axis_index("slab") * Z + index // Y
    row = lax.axis_index("pencil") * Y + index % Y
    ids = (plane * spread + row) * count + lax.axis_index("comp")
    chunk = 8 * LANES
    two, end = 2 * Y, (Z - 2) * Y
    middle = end - two
    inner[0:middle, :] = weight[two:end, :]
    outer[0:two, :] = weight[0:two, :]
    outer[two : 2 * two, :] = weight[end : end + two, :]
    for k in range(sensor.shape[1] // chunk):
        cols = slice(k * chunk, (k + 1) * chunk)
        picks = jnp.where(ids == sensor[:, cols], POINT_GAIN, 0.0).astype(jnp.bfloat16)
        inner[middle : 2 * middle, cols] = picks[two:end]
        outer[2 * two : 3 * two, cols] = picks[0:two]
        outer[3 * two : 4 * two, cols] = picks[end : end + two]


def edge_kernel(U, D, tough, first, second, S, damage):
    Z, Y, X = tough.shape
    low, high = plane_readers(first, second)
    for k, z in enumerate((0, Z - 1)):
        for t in range(1, Y // SUB + 1):
            r = t * SUB
            rows = slice(r, r + SUB)
            own = slice((t - 1) * SUB, t * SUB)
            gz, gy, gx = [], [], []
            for c in range(3):
                below = low(2 * c + 1, own) if z == 0 else U[c, z - 1, rows, 0:X]
                above = U[c, z + 1, rows, 0:X] if z == 0 else high(2 * c, own)
                gz.append(above - below)
                gy.append(U[c, z, r + 1 : r + SUB + 1, 0:X] - U[c, z, r - 1 : r + SUB - 1, 0:X])
                value = U[c, z, rows, :]
                gx.append((ahead(value) - behind(value))[:, 0:X])
            h = stiffness(D[z, rows, 0:X])
            total = LAME_FIRST * (gz[0] + gy[1] + gx[2])
            S[k, ZZ, rows, 0:X] = h * (total + 2.0 * gz[0])
            S[k, YY, rows, 0:X] = h * (total + 2.0 * gy[1])
            S[k, XX, rows, 0:X] = h * (total + 2.0 * gx[2])
            S[k, ZY, rows, 0:X] = h * (gy[0] + gz[1])
            S[k, ZX, rows, 0:X] = h * (gx[0] + gz[2])
            S[k, YX, rows, 0:X] = h * (gx[1] + gy[2])
            energy = energy_of(gz, gy, gx, X)
            below = low(6, own) if z == 0 else D[z - 1, rows, 0:X]
            above = D[z + 1, rows, 0:X] if z == 0 else high(6, own)
            damage[k, own, :] = new_damage(D.at[z], below, above, t, energy, tough[z, own, :])


def outer_kernel(merged, last, *refs):
    rest = list(refs)
    take = lambda k: [rest.pop(0) for _ in range(k)]
    u, first, second, low_rows, high_rows, columns, U, D, S, E_in = take(10)
    if last:
        inner_part, edge_rows = take(2)
        E, moved, part = take(3)
    else:
        inner_moved, inner_damage, edge_damage = take(3)
        E, moved, damage, cols, to_first, to_second = take(6)
    del E_in
    low_face, high_face, faces = take(3)
    if last:
        (pool,) = take(1)
    _, Z, Y, X = u.shape
    tiles = range(1, Y // SUB + 1)
    low, high = plane_readers(first, second)
    lay_out_face(
        merged, 0, lambda c: low(2 * c), lambda c: low(2 * c + 1), low_rows, high_rows, columns, low_face
    )
    lay_out_face(
        merged, 1, lambda c: high(2 * c + 1), lambda c: high(2 * c), low_rows, high_rows, columns, high_face
    )

    def at_plane(z):
        def at(c, dz):
            k = z + dz
            if k < 0:
                return low_face.at[c, 2 + k]
            if k >= Z:
                return high_face.at[c, Z + 1 - k]
            return U.at[c, k]

        return at

    face_stress(at_plane(-1), lambda own: low(6, own), faces.at[0], Y, X)
    face_stress(at_plane(Z), lambda own: high(6, own), faces.at[1], Y, X)
    for k, z in enumerate((0, Z - 1)):
        row_stress(at_plane(z), D.at[z], E.at[k], Y, X)
        side_stress(at_plane(z), D.at[z], E.at[k], Y, X)

    def stress(z):
        if z < 0:
            return faces.at[0]
        if z >= Z:
            return faces.at[1]
        if z == 0:
            return E.at[0]
        if z == Z - 1:
            return E.at[1]
        return S.at[z - 1]

    for k, z in enumerate((0, 1, Z - 2, Z - 1)):
        for t in tiles:
            own = slice((t - 1) * SUB, t * SUB)
            new = plane_moved(stress(z - 1), stress(z), stress(z + 1), lambda c: u.at[c, z], t, X)
            for c in range(3):
                moved[c, k if last else z, own, :] = new[c]
            if last:
                start = k * Y + (t - 1) * SUB
                pool[start : start + SUB, :] = row_sums(new)
    if last:
        means = means_of(pool[...], X)
        means = jnp.concatenate([means, means], axis=1)
        chunk = 8 * LANES
        sub = lax.broadcasted_iota(jnp.int32, (SUB, LANES), 0)
        for k in range(edge_rows.shape[1] // chunk):
            start = slice(k * chunk, (k + 1) * chunk)
            value = inner_part[:, start] + jnp.dot(
                means, edge_rows[:, start], preferred_element_type=F32
            )
            for c in range(3):
                tile = jnp.zeros((SUB, LANES), F32)
                for j in range(SUB):
                    piece = value[c : c + 1, j * LANES : (j + 1) * LANES]
                    tile = jnp.where(sub == j, piece, tile)
                part[c, k] = tile
    else:
        for c in range(3):
            moved[c, 2 : Z - 2] = inner_moved[c]
        damage[0] = edge_damage[0]
        damage[1 : Z - 1] = inner_damage[...]
        damage[Z - 1] = edge_damage[1]
        put_planes(moved, damage, to_first, to_second)
        put_columns(moved, damage, cols)


def fields_kernel(inner_moved, edge_moved, inner_damage, edge_damage, moved, damage):
    Z = damage.shape[0]
    for c in range(3):
        moved[c, 0:2] = edge_moved[c, 0:2]
        moved[c, 2 : Z - 2] = inner_moved[c]
        moved[c, Z - 2 : Z] = edge_moved[c, 2:4]
    damage[0] = edge_damage[0]
    damage[1 : Z - 1] = inner_damage[...]
    damage[Z - 1] = edge_damage[1]


def finish_kernel(count, *refs):
    out = refs[-1]
    total = refs[0][...]
    for ref in refs[1:-1]:
        total = total + ref[...]
    for c in range(3):
        for k in range(total.shape[1]):
            for j in range(SUB):
                start = (k * SUB + j) * LANES
                out[c : c + 1, start : start + LANES] = total[c, k, j : j + 1, :]


def call(kernel, outs, *args, scratch=(), name=None, in_specs=None, micros=1, alias=None):
    many = isinstance(outs, (list, tuple))
    return pl.pallas_call(
        kernel,
        out_shape=outs,
        in_specs=in_specs or [VMEM] * len(args),
        out_specs=[VMEM] * len(outs) if many else VMEM,
        scratch_shapes=list(scratch),
        compiler_params=pltpu.CompilerParams(vmem_limit_bytes=VMEM_LIMIT),
        cost_estimate=pl.CostEstimate(
            flops=0, bytes_accessed=micros * 3_000_000, transcendentals=0
        ),
        input_output_aliases=alias or {},
        name=name,
    )(*args)


def up_pairs(count):
    return [(i, i + 1) for i in range(count - 1)]


def down_pairs(count):
    return [(i + 1, i) for i in range(count - 1)]


def all_sum(value):
    for axis in ("comp", "pencil"):
        count = lax.axis_size(axis)
        bit = 1
        while bit < count:
            value = value + lax.ppermute(value, axis, [(i, i ^ bit) for i in range(count)])
            bit *= 2
    count = lax.axis_size("slab")
    bit = 1
    while count // bit > 4:
        value = value + lax.ppermute(value, "slab", [(i, i ^ bit) for i in range(count)])
        bit *= 2
    terms = [value]
    for k in range(1, count // bit):
        terms.append(lax.ppermute(value, "slab", [(i, i ^ (k * bit)) for i in range(count)]))
    return terms


def local(u_start, toughness, crack_label, obs_weight, sensor_cell):
    Z, Y, X = toughness.shape
    slabs, pencils = lax.axis_size("slab"), lax.axis_size("pencil")
    if lax.axis_size("comp") != 2 or Z < 6 or Z % SUB or 8 * Z > LANES:
        raise ValueError("unsupported block")
    merged = pencils == 2
    n = 1 if merged else 2
    shape = jax.ShapeDtypeStruct
    field, vector = shape((Z, Y, X), F32), shape((3, Z, Y, X), F32)
    columns = shape((Y, LANES), F32)
    sensors = sensor_cell.shape[0]
    rows, lanes = Y + 2 * SUB, X + LANES
    y_up, y_down = up_pairs(pencils), down_pairs(pencils)
    y_pairs = [y_up + y_down] if merged else [y_up, y_down]
    margins = [
        shape((3, Z, rows, lanes), F32),
        shape((Z, rows, lanes), F32),
        shape((Z - 2, 6, rows, lanes), F32),
    ]
    scratch = [
        pltpu.VMEM((3, 2, rows, lanes), F32),
        pltpu.VMEM((3, 2, rows, lanes), F32),
        pltpu.VMEM((2, 3, rows, lanes), F32),
    ]
    edges = shape((2, 6, rows, lanes), F32)
    planes = shape((7, Y, X), F32)
    evens = [pair for pair in up_pairs(slabs) + down_pairs(slabs) if min(pair) % 2 == 0]
    odds = [pair for pair in up_pairs(slabs) + down_pairs(slabs) if min(pair) % 2 == 1]
    swap = [(0, 1), (1, 0)]
    moved, damage, cols, to_first, to_second = call(
        load_kernel,
        [vector, field, columns, planes, planes],
        u_start,
        crack_label,
        scratch=[pltpu.VMEM((Z, Y, X), jnp.int32), pltpu.SemaphoreType.DMA((4,))],
        in_specs=[pl.BlockSpec(memory_space=pltpu.HBM)] * 2,
        name="load",
    )
    for step in range(2):
        last = step == 1
        first = lax.ppermute(to_first, "slab", evens)
        second = lax.ppermute(to_second, "slab", odds)
        xh = lax.ppermute(cols, "comp", swap)
        out = call(
            functools.partial(rows_kernel, merged),
            [shape((8, Z, X), F32)] * n,
            moved,
            damage,
            xh,
            name="rows",
        )
        ys = [lax.ppermute(y, "pencil", pairs) for y, pairs in zip(out, y_pairs)]
        after = [out[0]]
        if not last:
            inner_rows, outer_rows = call(
                functools.partial(weights_kernel, Z, Y),
                [
                    shape((2 * (Z - 4) * Y, sensors), jnp.bfloat16),
                    shape((8 * Y, sensors), jnp.bfloat16),
                ],
                obs_weight.reshape(Z * Y, sensors),
                sensor_cell.reshape(1, sensors),
                out[0],
                name="weights",
            )
            after.append(inner_rows)
        middle = call(
            middle_kernel,
            margins + [shape((Z - 2, Y, X), F32)],
            moved,
            damage,
            toughness,
            xh,
            *after,
            name="middle",
        )
        *corner_rows, corner_columns = call(
            lambda a, b, _, *rest: corners_kernel(merged, a, b, rest[-1], *rest[:-1]),
            [shape((SUB, X), F32)] * n + [columns],
            first,
            second,
            middle[3],
            name="corners",
        )
        args = [moved, toughness, ys[0], ys[-1], corner_columns]
        outs = margins + [shape((Z - 2, Y, X), F32), shape((3, Z - 4, Y, X), F32)]
        inner_scratch = []
        if last:
            args += [inner_rows]
            outs = outs + [shape((SUB, sensors), F32)]
            inner_scratch = [pltpu.VMEM(((Z - 4) * Y, LANES), F32)]
        U, D, S, inner_damage, inner_moved, *more = call(
            functools.partial(inner_kernel, merged, last),
            outs,
            *args,
            *middle,
            scratch=inner_scratch,
            name="inner",
            micros=2,
            alias={len(args) + k: k for k in range(4)},
        )
        if last:
            more.append(outer_rows)
        crows = [lax.ppermute(y, "pencil", pairs) for y, pairs in zip(corner_rows, y_pairs)]
        ccols = lax.ppermute(corner_columns, "comp", swap)
        E, edge_damage = call(
            edge_kernel,
            [edges, shape((2, Y, X), F32)],
            U,
            D,
            toughness,
            first,
            second,
            name="edge",
        )
        args = [moved, first, second, crows[0], crows[-1], ccols, U, D, S, E]
        if last:
            _, edge_moved, part = call(
                functools.partial(outer_kernel, merged, True),
                [
                    edges,
                    shape((3, 4, Y, X), F32),
                    shape((3, sensors // (SUB * LANES), SUB, LANES), F32),
                ],
                *args,
                *more,
                scratch=scratch + [pltpu.VMEM((4 * Y, LANES), F32)],
                name="outer2",
                alias={9: 0},
            )
            moved, damage = call(
                fields_kernel,
                [vector, field],
                inner_moved,
                edge_moved,
                inner_damage,
                edge_damage,
                name="fields",
            )
        else:
            _, moved, damage, cols, to_first, to_second = call(
                functools.partial(outer_kernel, merged, False),
                [edges, vector, field, columns, planes, planes],
                *args,
                inner_moved,
                inner_damage,
                edge_damage,
                scratch=scratch,
                name="outer1",
                alias={9: 0},
            )
    terms = all_sum(part)
    readings = call(
        functools.partial(finish_kernel, len(terms)),
        shape((3, sensors), F32),
        *terms,
        name="finish",
    )
    return moved, damage, readings


def solution(mesh):
    return jax.shard_map(
        local,
        mesh=mesh,
        in_specs=(
            P(None, ("groups", "slab"), "pencil", "comp"),
            P(("groups", "slab"), "pencil", "comp"),
            P(("groups", "slab"), "pencil", "comp"),
            P("slab", "pencil", "comp", None),
            P(),
        ),
        out_specs=(
            P(None, ("groups", "slab"), "pencil", "comp"),
            P(("groups", "slab"), "pencil", "comp"),
            P(None, "groups"),
        ),
        check_vma=False,
    )
```

```python
import functools

import jax
import jax.numpy as jnp
from jax import lax
from jax.experimental import pallas as pl
from jax.experimental.pallas import tpu as pltpu
from jax.sharding import PartitionSpec as P

SHEAR_MODULUS = 1.0
LAME_FIRST = 1.5
RESIDUAL_STIFF = 0.001
TIME_DISP = 0.15
TIME_DAMAGE = 0.08
DAMAGE_LEVEL = 0.45
POINT_GAIN = 8.0
LANES = 128
SUB = 8
COS_THIRD = (
    0.5000000037331834,
    0.5773496613984853,
    -0.11109449276880777,
    0.05327935086024303,
    -0.031925412185213546,
    0.01960032102518762,
    -0.010237508432464154,
    0.003654119632233793,
    -0.0006260453394989179,
)
F32 = jnp.float32
VMEM_LIMIT = 24 * 1024 * 1024
VMEM = pl.BlockSpec(memory_space=pltpu.VMEM)


def positive_square_sum(m00, m11, m22, m01, m02, m12):
    mean = (m00 + m11 + m22) * (1.0 / 3.0)
    b00, b11, b22 = m00 - mean, m11 - mean, m22 - mean
    s01, s02, s12 = m01 * m01, m02 * m02, m12 * m12
    p2 = (b00 * b00 + b11 * b11 + b22 * b22) * (1.0 / 6.0) + (s01 + s02 + s12) * (1.0 / 3.0)
    det = b00 * (b11 * b22 - s12) + 2.0 * (m01 * m02) * m12 - b11 * s02 - b22 * s01
    mean2 = mean * mean
    whole = mean * (mean2 - 3.0 * p2) + det
    up = whole >= 0.0
    safe = jnp.maximum(p2, 1e-24)
    inv = lax.rsqrt(safe)
    p = safe * inv
    half = 0.25 * (det * inv) * (inv * inv)
    half = jnp.where(up, half, -half) + 0.5
    half = jnp.minimum(jnp.maximum(half, 0.0), 1.0)
    t = jnp.sqrt(half)
    c = jnp.full_like(t, COS_THIRD[-1])
    for value in COS_THIRD[-2::-1]:
        c = c * t + value
    pc = p * c
    lead = jnp.where(up, mean, -mean)
    largest = lead + 2.0 * pc
    square = largest * largest
    norm = 6.0 * p2 + 3.0 * mean2
    rest = lead - pc
    return jnp.where(
        up, jnp.where(rest > 0.0, norm, square), jnp.where(rest < 0.0, norm - square, 0.0)
    )


def sides(merged, fn):
    if merged:
        return [jnp.where(lax.axis_index("pencil") == 0, fn(1), fn(-1))]
    return [fn(1), fn(-1)]


def is_left():
    return lax.axis_index("comp") == 0


def pack_columns(tiles, out):
    Y = out.shape[0]
    left = is_left()
    lane = lax.broadcasted_iota(jnp.int32, (Y, LANES), 1)
    slot = jnp.where(left, (lane + 2) // 2 % (LANES // 2), lane // 2)
    acc = jnp.zeros((Y, LANES), F32)
    for entry, plane in enumerate(tiles):
        X = plane.shape[1]
        tile = jnp.where(left, plane[:, X - LANES : X], plane[:, 0:LANES])
        turned = pltpu.roll(tile, 2 * entry, 1) if entry else tile
        acc = jnp.where(slot == entry, turned, acc)
    out[...] = jnp.where(left, pltpu.roll(acc, 2, 1), acc)


def put_columns(u, d, out):
    Z = d.shape[0]
    pack_columns([u.at[c, z] for c in range(3) for z in range(Z)] + [d.at[z] for z in range(Z)], out)


def is_even():
    return lax.axis_index("slab") % 2 == 0


def put_planes(u, d, first, second):
    _, Z, Y, X = u.shape
    even = is_even()
    for c in range(3):
        up, down = u[c, Z - 2 : Z], u[c, 0:2]
        first[2 * c : 2 * c + 2] = jnp.where(even, up, down)
        second[2 * c : 2 * c + 2] = jnp.where(even, down, up)
    up, down = d[Z - 1], d[0]
    first[6] = jnp.where(even, up, down)
    second[6] = jnp.where(even, down, up)


def plane_readers(first, second):
    even = is_even()

    def low(*at):
        return jnp.where(even, second[at], first[at])

    def high(*at):
        return jnp.where(even, first[at], second[at])

    return low, high


def column_reader(packet):
    rows = packet.shape[0]
    left = is_left()
    lane = lax.broadcasted_iota(jnp.int32, (rows, LANES), 1)
    inside = jnp.where(left, lane, LANES - 1 - lane) < 2
    packet = jnp.where(left, packet, pltpu.roll(packet, LANES - 2, 1))

    def column(entry):
        shift = (LANES - 2 * entry) % LANES
        turned = pltpu.roll(packet, shift, 1) if shift else packet
        return jnp.where(inside, turned, 0.0)

    return column


def send_kernel(u, label, first, second, rows, sems):
    Z = label.shape[0]
    parity = lax.axis_index("slab") & 1
    copies = []
    for k, (out, side) in enumerate(((first, 1 - parity), (second, parity))):
        for c in range(3):
            copies.append(
                pltpu.make_async_copy(
                    u.at[c, pl.ds(side * (Z - 2), 2)], out.at[2 * c : 2 * c + 2], sems.at[k, c]
                )
            )
        copies.append(
            pltpu.make_async_copy(label.at[pl.ds(side * (Z - 1), 1)], rows.at[k], sems.at[k, 3])
        )
    for copy in copies:
        copy.start()
    for copy in copies:
        copy.wait()
    first[6] = DAMAGE_LEVEL * rows[0, 0].astype(F32)
    second[6] = DAMAGE_LEVEL * rows[1, 0].astype(F32)


def load_kernel(u_hbm, label_hbm, first, u, d, cols, label, sems):
    del first
    copies = [pltpu.make_async_copy(u_hbm.at[c], u.at[c], sems.at[c]) for c in range(3)]
    copies.append(pltpu.make_async_copy(label_hbm, label, sems.at[3]))
    for copy in copies:
        copy.start()
    copies[3].wait()
    d[...] = DAMAGE_LEVEL * label[...].astype(F32)
    for copy in copies[:3]:
        copy.wait()
    put_columns(u, d, cols)


def rows_kernel(merged, u, d, xh, *outs):
    _, Z, Y, X = u.shape
    for c in range(3):
        for layer in range(2):
            row = lambda s: u[c, :, Y - 2 + layer if s > 0 else layer, :]
            for ref, value in zip(outs, sides(merged, row)):
                ref[2 * c + layer] = value
    for ref, value in zip(outs, sides(merged, lambda s: d[:, Y - 1 if s > 0 else 0, :])):
        ref[6] = value
    corner = lambda s: xh[Y - 1 : Y, :] if s > 0 else xh[0:1, :]
    for ref, value in zip(outs, sides(merged, corner)):
        ref[7, 0:1, 0:LANES] = value


def corners_kernel(merged, first, second, cols, *outs):
    _, Y, X = first.shape
    low, high = plane_readers(first, second)
    near = [low(2 * c + 1) for c in range(3)] + [high(2 * c) for c in range(3)]
    for k, plane in enumerate(near):
        edge = lambda s: plane[Y - 1 : Y, :] if s > 0 else plane[0:1, :]
        for ref, value in zip(outs, sides(merged, edge)):
            ref[k : k + 1, :] = value
    pack_columns(near, cols)


def row_keepers(merged):
    if not merged:
        return (lambda value: value), (lambda value: value)
    py = lax.axis_index("pencil")
    return (
        lambda value: jnp.where(py != 0, value, 0.0),
        lambda value: jnp.where(py == 0, value, 0.0),
    )


def lay_out_columns(u, d, xh, U, D):
    _, Z, Y, X = u.shape
    H = SUB
    column = column_reader(xh[...])
    for c in range(3):
        U[c, :, H : H + Y, 0:X] = u[c]
        for z in range(Z):
            U[c, z, H : H + Y, X : X + LANES] = column(c * Z + z)
    D[:, H : H + Y, 0:X] = d[...]
    for z in range(Z):
        D[z, H : H + Y, X : X + LANES] = column(3 * Z + z)


def lay_out_rows(merged, ylo, yhi, U, D):
    Z, X = D.shape[0], ylo.shape[2]
    Y, H = D.shape[1] - 2 * SUB, SUB
    low_of, high_of = row_keepers(merged)
    low_corner = column_reader(low_of(ylo[7, 0:1, 0:LANES]))
    high_corner = column_reader(high_of(yhi[7, 0:1, 0:LANES]))
    for c in range(3):
        for layer in range(2):
            low, high = low_of(ylo[2 * c + layer]), high_of(yhi[2 * c + layer])
            for z in range(Z):
                U[c, z, H - 2 + layer : H - 1 + layer, 0:X] = low[z : z + 1]
                U[c, z, H + Y + layer : H + Y + layer + 1, 0:X] = high[z : z + 1]
        for z in range(Z):
            U[c, z, H - 1 : H, X : X + LANES] = low_corner(c * Z + z)
            U[c, z, H + Y : H + Y + 1, X : X + LANES] = high_corner(c * Z + z)
    low, high = low_of(ylo[6]), high_of(yhi[6])
    for z in range(Z):
        D[z, H - 1 : H, 0:X] = low[z : z + 1]
        D[z, H + Y : H + Y + 1, 0:X] = high[z : z + 1]


def lay_out_face(merged, k, far, near, low_rows, high_rows, columns, F):
    Y, X = near(0).shape
    H = SUB
    low_of, high_of = row_keepers(merged)
    column = column_reader(columns[...])
    for c in range(3):
        F[c, 0, H : H + Y, 0:X] = far(c)
        F[c, 1, H : H + Y, 0:X] = near(c)
        F[c, 1, H : H + Y, X : X + LANES] = column(3 * k + c)
        row = 3 * k + c
        F[c, 1, H - 1 : H, 0:X] = low_of(low_rows[row : row + 1, :])
        F[c, 1, H + Y : H + Y + 1, 0:X] = high_of(high_rows[row : row + 1, :])


def ahead(value):
    return pltpu.roll(value, value.shape[-1] - 1, value.ndim - 1)


def behind(value):
    return pltpu.roll(value, 1, value.ndim - 1)


ZZ, ZY, ZX, YY, YX, XX = range(6)
PAIRS = ((ZZ, ZY, ZX), (ZY, YY, YX), (ZX, YX, XX))


def gradients(at, row, count):
    rows = slice(row, row + count)
    gz, gy, gx = [], [], []
    for c in range(3):
        mid = at(c, 0)
        gz.append(at(c, 1)[rows, :] - at(c, -1)[rows, :])
        gy.append(mid[row + 1 : row + count + 1, :] - mid[row - 1 : row + count - 1, :])
        value = mid[rows, :]
        gx.append(ahead(value) - behind(value))
    return gz, gy, gx


def stiffness(damage):
    keep = 1.0 - damage
    return 0.5 * (keep * keep + RESIDUAL_STIFF)


def energy_of(gz, gy, gx, X):
    cut = lambda value: value[:, 0:X]
    z0, y1, x2 = cut(gz[0]), cut(gy[1]), cut(gx[2])
    mzy = 0.5 * cut(gy[0] + gz[1])
    mzx = 0.5 * cut(gx[0] + gz[2])
    myx = 0.5 * cut(gx[1] + gy[2])
    squares = positive_square_sum(z0, y1, x2, mzy, mzx, myx)
    grow = jnp.maximum(z0 + y1 + x2, 0.0)
    return (0.25 * 0.5 * LAME_FIRST) * (grow * grow) + (0.25 * SHEAR_MODULUS) * squares


def new_damage(mid, below, above, t, energy, tough):
    X = tough.shape[-1]
    r = t * SUB
    value = mid[r : r + SUB, :]
    core = value[:, 0:X]
    lap = (
        below
        + above
        + mid[r + 1 : r + SUB + 1, 0:X]
        + mid[r - 1 : r + SUB - 1, 0:X]
        + (ahead(value) + behind(value))[:, 0:X]
        - 6.0 * core
    )
    return core + TIME_DAMAGE * (2.0 * (1.0 - core) * energy + tough * (lap - core))


def row_stress(at, damage_plane, S, Y, X):
    H = SUB
    for row in (H - 1, H + Y):
        gz, gy, gx = gradients(at, row, 1)
        h = stiffness(damage_plane[row : row + 1, :])
        total = LAME_FIRST * (gz[0] + gy[1] + gx[2])
        for key, value in (
            (ZY, gy[0] + gz[1]),
            (YY, total + 2.0 * gy[1]),
            (YX, gx[1] + gy[2]),
        ):
            S[key, row : row + 1, 0:X] = (h * value)[:, 0:X]


def tile_stress(at, damage_plane, S, t, X):
    rows = slice(t * SUB, t * SUB + SUB)
    gz, gy, gx = gradients(at, t * SUB, SUB)
    h = stiffness(damage_plane[rows, :])
    total = LAME_FIRST * (gz[0] + gy[1] + gx[2])
    S[ZZ, rows, 0:X] = (h * (total + 2.0 * gz[0]))[:, 0:X]
    S[YY, rows, 0:X] = (h * (total + 2.0 * gy[1]))[:, 0:X]
    S[ZY, rows, 0:X] = (h * (gy[0] + gz[1]))[:, 0:X]
    S[ZX, rows, :] = h * (gx[0] + gz[2])
    S[YX, rows, :] = h * (gx[1] + gy[2])
    S[XX, rows, :] = h * (total + 2.0 * gx[2])
    return energy_of(gz, gy, gx, X)


def side_stress(at, damage_plane, S, Y, X):
    turn = LANES
    for t in range(1, Y // SUB + 1):
        r = t * SUB
        rows, out = slice(r, r + SUB), slice(X, X + LANES)
        gz, gy, gx = [], [], []
        for c in range(3):
            mid = at(c, 0)
            gz.append(at(c, 1)[rows, out] - at(c, -1)[rows, out])
            gy.append(mid[r + 1 : r + SUB + 1, out] - mid[r - 1 : r + SUB - 1, out])
            value = mid[rows, :]
            gx.append((ahead(value) - behind(value))[:, out])
        h = stiffness(damage_plane[rows, out])
        total = LAME_FIRST * (gz[0] + gy[1] + gx[2])
        S[ZX, rows, out] = h * (gx[0] + gz[2])
        S[YX, rows, out] = h * (gx[1] + gy[2])
        S[XX, rows, out] = h * (total + 2.0 * gx[2])


def face_stress(at, damage, S, Y, X):
    for t in range(1, Y // SUB + 1):
        rows = slice(t * SUB, t * SUB + SUB)
        gz, gy, gx = gradients(at, t * SUB, SUB)
        h = stiffness(damage(slice((t - 1) * SUB, t * SUB)))
        total = LAME_FIRST * (gz[0] + gy[1] + gx[2])
        for key, value in (
            (ZZ, total + 2.0 * gz[0]),
            (ZY, gy[0] + gz[1]),
            (ZX, gx[0] + gz[2]),
        ):
            S[key, rows, 0:X] = h * value[:, 0:X]


def plane_moved(below, mid, above, u_plane, t, X):
    r = t * SUB
    rows = slice(r, r + SUB)
    out = []
    for c in range(3):
        kz, ky, kx = PAIRS[c]
        value = mid[kx, rows, :]
        force = (
            above[kz, rows, 0:X]
            - below[kz, rows, 0:X]
            + mid[ky, r + 1 : r + SUB + 1, 0:X]
            - mid[ky, r - 1 : r + SUB - 1, 0:X]
            + (ahead(value) - behind(value))[:, 0:X]
        )
        out.append(u_plane(c)[(t - 1) * SUB : t * SUB, :] + (0.5 * TIME_DISP) * force)
    return out


def row_sums(new):
    lane = lax.broadcasted_iota(jnp.int32, (SUB, LANES), 1)
    sums = [jnp.sum(value, axis=-1, keepdims=True) for value in new]
    return jnp.where(lane == 0, sums[0], jnp.where(lane == 1, sums[1], sums[2]))


def means_of(pool, X):
    return (pool * (1.0 / X)).T[0:SUB].astype(jnp.bfloat16)


def inner_tiles(z, tiles, U, D, S, tough, damage):
    X = tough.shape[2]
    for t in tiles:
        energy = tile_stress(lambda c, dz: U.at[c, z + dz], D.at[z], S.at[z - 1], t, X)
        rows = slice(t * SUB, t * SUB + SUB)
        own = slice((t - 1) * SUB, t * SUB)
        damage[z - 1, own, :] = new_damage(
            D.at[z], D[z - 1, rows, 0:X], D[z + 1, rows, 0:X], t, energy, tough[z, own, :]
        )


def middle_kernel(u, d, tough, xh, *rest):
    U, D, S, damage = rest[-4:]
    Z, Y, X = tough.shape
    lay_out_columns(u, d, xh, U, D)

    @pl.loop(1, Z - 1)
    def _(z):
        inner_tiles(z, range(2, Y // SUB), U, D, S, tough, damage)


def inner_kernel(merged, tough, ylo, yhi, after, *refs):
    del after
    U, D, S, damage = refs[-4:]
    Z, Y, X = tough.shape
    lay_out_rows(merged, ylo, yhi, U, D)

    @pl.loop(1, Z - 1)
    def _(z):
        row_stress(lambda c, dz: U.at[c, z + dz], D.at[z], S.at[z - 1], Y, X)
        inner_tiles(z, (1, Y // SUB), U, D, S, tough, damage)


def moved_kernel(last, u, S, after, *rest):
    del after
    if last:
        weight, moved, part, pool = rest
    else:
        (moved,) = rest
    _, Z, Y, X = u.shape

    @pl.loop(2, Z - 2)
    def _(z):
        for t in range(1, Y // SUB + 1):
            own = slice((t - 1) * SUB, t * SUB)
            new = plane_moved(
                S.at[z - 2], S.at[z - 1], S.at[z], lambda c: u.at[c, z], t, X
            )
            for c in range(3):
                moved[c, z - 2, own, :] = new[c]
            if last:
                start = pl.multiple_of((z - 2) * Y + (t - 1) * SUB, SUB)
                pool[pl.ds(start, SUB), :] = row_sums(new)

    if last:
        means = means_of(pool[...], X)
        means = jnp.concatenate([means, means], axis=1)
        chunk = 8 * LANES
        for k in range(weight.shape[1] // chunk):
            cols = slice(k * chunk, (k + 1) * chunk)
            part[:, cols] = jnp.dot(means, weight[:, cols], preferred_element_type=F32)


def weights_kernel(Z, Y, weight, sensor, after, inner, outer):
    del after
    count = lax.axis_size("comp")
    spread = Y * lax.axis_size("pencil")
    index = lax.broadcasted_iota(jnp.int32, (Z * Y, 1), 0)
    plane = lax.axis_index("slab") * Z + index // Y
    row = lax.axis_index("pencil") * Y + index % Y
    ids = (plane * spread + row) * count + lax.axis_index("comp")
    chunk = 8 * LANES
    two, end = 2 * Y, (Z - 2) * Y
    middle = end - two
    inner[0:middle, :] = weight[two:end, :]
    outer[0:two, :] = weight[0:two, :]
    outer[two : 2 * two, :] = weight[end : end + two, :]
    for k in range(sensor.shape[1] // chunk):
        cols = slice(k * chunk, (k + 1) * chunk)
        picks = jnp.where(ids == sensor[:, cols], POINT_GAIN, 0.0).astype(jnp.bfloat16)
        inner[middle : 2 * middle, cols] = picks[two:end]
        outer[2 * two : 3 * two, cols] = picks[0:two]
        outer[3 * two : 4 * two, cols] = picks[end : end + two]


def edge_kernel(U, D, tough, first, second, S, damage):
    Z, Y, X = tough.shape
    low, high = plane_readers(first, second)
    for k, z in enumerate((0, Z - 1)):
        for t in range(1, Y // SUB + 1):
            r = t * SUB
            rows = slice(r, r + SUB)
            own = slice((t - 1) * SUB, t * SUB)
            gz, gy, gx = [], [], []
            for c in range(3):
                below = low(2 * c + 1, own) if z == 0 else U[c, z - 1, rows, 0:X]
                above = U[c, z + 1, rows, 0:X] if z == 0 else high(2 * c, own)
                gz.append(above - below)
                gy.append(U[c, z, r + 1 : r + SUB + 1, 0:X] - U[c, z, r - 1 : r + SUB - 1, 0:X])
                value = U[c, z, rows, :]
                gx.append((ahead(value) - behind(value))[:, 0:X])
            h = stiffness(D[z, rows, 0:X])
            total = LAME_FIRST * (gz[0] + gy[1] + gx[2])
            S[k, ZZ, rows, 0:X] = h * (total + 2.0 * gz[0])
            S[k, YY, rows, 0:X] = h * (total + 2.0 * gy[1])
            S[k, XX, rows, 0:X] = h * (total + 2.0 * gx[2])
            S[k, ZY, rows, 0:X] = h * (gy[0] + gz[1])
            S[k, ZX, rows, 0:X] = h * (gx[0] + gz[2])
            S[k, YX, rows, 0:X] = h * (gx[1] + gy[2])
            energy = energy_of(gz, gy, gx, X)
            below = low(6, own) if z == 0 else D[z - 1, rows, 0:X]
            above = D[z + 1, rows, 0:X] if z == 0 else high(6, own)
            damage[k, own, :] = new_damage(D.at[z], below, above, t, energy, tough[z, own, :])


def outer_kernel(merged, last, *refs):
    rest = list(refs)
    take = lambda k: [rest.pop(0) for _ in range(k)]
    u, first, second, low_rows, high_rows, columns, U, D, S, E_in = take(10)
    if last:
        inner_part, edge_rows = take(2)
        E, moved, part = take(3)
    else:
        inner_moved, inner_damage, edge_damage = take(3)
        E, moved, damage, cols, to_first, to_second = take(6)
    del E_in
    low_face, high_face, faces = take(3)
    if last:
        (pool,) = take(1)
    _, Z, Y, X = u.shape
    tiles = range(1, Y // SUB + 1)
    low, high = plane_readers(first, second)
    lay_out_face(
        merged, 0, lambda c: low(2 * c), lambda c: low(2 * c + 1), low_rows, high_rows, columns, low_face
    )
    lay_out_face(
        merged, 1, lambda c: high(2 * c + 1), lambda c: high(2 * c), low_rows, high_rows, columns, high_face
    )

    def at_plane(z):
        def at(c, dz):
            k = z + dz
            if k < 0:
                return low_face.at[c, 2 + k]
            if k >= Z:
                return high_face.at[c, Z + 1 - k]
            return U.at[c, k]

        return at

    face_stress(at_plane(-1), lambda own: low(6, own), faces.at[0], Y, X)
    face_stress(at_plane(Z), lambda own: high(6, own), faces.at[1], Y, X)
    for k, z in enumerate((0, Z - 1)):
        row_stress(at_plane(z), D.at[z], E.at[k], Y, X)
        side_stress(at_plane(z), D.at[z], E.at[k], Y, X)

    def stress(z):
        if z < 0:
            return faces.at[0]
        if z >= Z:
            return faces.at[1]
        if z == 0:
            return E.at[0]
        if z == Z - 1:
            return E.at[1]
        return S.at[z - 1]

    for k, z in enumerate((0, 1, Z - 2, Z - 1)):
        for t in tiles:
            own = slice((t - 1) * SUB, t * SUB)
            new = plane_moved(stress(z - 1), stress(z), stress(z + 1), lambda c: u.at[c, z], t, X)
            for c in range(3):
                moved[c, k if last else z, own, :] = new[c]
            if last:
                start = k * Y + (t - 1) * SUB
                pool[start : start + SUB, :] = row_sums(new)
    if last:
        means = means_of(pool[...], X)
        means = jnp.concatenate([means, means], axis=1)
        chunk = 8 * LANES
        sub = lax.broadcasted_iota(jnp.int32, (SUB, LANES), 0)
        for k in range(edge_rows.shape[1] // chunk):
            start = slice(k * chunk, (k + 1) * chunk)
            value = inner_part[:, start] + jnp.dot(
                means, edge_rows[:, start], preferred_element_type=F32
            )
            for c in range(3):
                tile = jnp.zeros((SUB, LANES), F32)
                for j in range(SUB):
                    piece = value[c : c + 1, j * LANES : (j + 1) * LANES]
                    tile = jnp.where(sub == j, piece, tile)
                part[c, k] = tile
    else:
        for c in range(3):
            moved[c, 2 : Z - 2] = inner_moved[c]
        damage[0] = edge_damage[0]
        damage[1 : Z - 1] = inner_damage[...]
        damage[Z - 1] = edge_damage[1]
        put_planes(moved, damage, to_first, to_second)
        put_columns(moved, damage, cols)


def fields_kernel(inner_moved, edge_moved, inner_damage, edge_damage, moved, damage):
    Z = damage.shape[0]
    for c in range(3):
        moved[c, 0:2] = edge_moved[c, 0:2]
        moved[c, 2 : Z - 2] = inner_moved[c]
        moved[c, Z - 2 : Z] = edge_moved[c, 2:4]
    damage[0] = edge_damage[0]
    damage[1 : Z - 1] = inner_damage[...]
    damage[Z - 1] = edge_damage[1]


def finish_kernel(count, *refs):
    out = refs[-1]
    total = refs[0][...]
    for ref in refs[1:-1]:
        total = total + ref[...]
    for c in range(3):
        for k in range(total.shape[1]):
            for j in range(SUB):
                start = (k * SUB + j) * LANES
                out[c : c + 1, start : start + LANES] = total[c, k, j : j + 1, :]


def call(kernel, outs, *args, scratch=(), name=None, in_specs=None, micros=1, alias=None):
    many = isinstance(outs, (list, tuple))
    return pl.pallas_call(
        kernel,
        out_shape=outs,
        in_specs=in_specs or [VMEM] * len(args),
        out_specs=[VMEM] * len(outs) if many else VMEM,
        scratch_shapes=list(scratch),
        compiler_params=pltpu.CompilerParams(vmem_limit_bytes=VMEM_LIMIT),
        cost_estimate=pl.CostEstimate(
            flops=0, bytes_accessed=micros * 3_000_000, transcendentals=0
        ),
        input_output_aliases=alias or {},
        name=name,
    )(*args)


def up_pairs(count):
    return [(i, i + 1) for i in range(count - 1)]


def down_pairs(count):
    return [(i + 1, i) for i in range(count - 1)]


def all_sum(value):
    for axis in ("comp", "pencil"):
        count = lax.axis_size(axis)
        bit = 1
        while bit < count:
            value = value + lax.ppermute(value, axis, [(i, i ^ bit) for i in range(count)])
            bit *= 2
    count = lax.axis_size("slab")
    bit = 1
    while count // bit > 4:
        value = value + lax.ppermute(value, "slab", [(i, i ^ bit) for i in range(count)])
        bit *= 2
    terms = [value]
    for k in range(1, count // bit):
        terms.append(lax.ppermute(value, "slab", [(i, i ^ (k * bit)) for i in range(count)]))
    return terms


def local(u_start, toughness, crack_label, obs_weight, sensor_cell):
    Z, Y, X = toughness.shape
    slabs, pencils = lax.axis_size("slab"), lax.axis_size("pencil")
    if lax.axis_size("comp") != 2 or Z < 6 or Z % SUB or 8 * Z > LANES:
        raise ValueError("unsupported block")
    merged = pencils == 2
    n = 1 if merged else 2
    shape = jax.ShapeDtypeStruct
    field, vector = shape((Z, Y, X), F32), shape((3, Z, Y, X), F32)
    columns = shape((Y, LANES), F32)
    sensors = sensor_cell.shape[0]
    rows, lanes = Y + 2 * SUB, X + LANES
    y_up, y_down = up_pairs(pencils), down_pairs(pencils)
    y_pairs = [y_up + y_down] if merged else [y_up, y_down]
    margins = [
        shape((3, Z, rows, lanes), F32),
        shape((Z, rows, lanes), F32),
        shape((Z - 2, 6, rows, lanes), F32),
    ]
    scratch = [
        pltpu.VMEM((3, 2, rows, lanes), F32),
        pltpu.VMEM((3, 2, rows, lanes), F32),
        pltpu.VMEM((2, 3, rows, lanes), F32),
    ]
    edges = shape((2, 6, rows, lanes), F32)
    planes = shape((7, Y, X), F32)
    evens = [pair for pair in up_pairs(slabs) + down_pairs(slabs) if min(pair) % 2 == 0]
    odds = [pair for pair in up_pairs(slabs) + down_pairs(slabs) if min(pair) % 2 == 1]
    swap = [(0, 1), (1, 0)]
    hbm = pl.BlockSpec(memory_space=pltpu.HBM)
    starts = [
        pltpu.with_memory_space_constraint(value, pltpu.HBM) for value in (u_start, crack_label)
    ]
    to_first, to_second = call(
        send_kernel,
        [planes, planes],
        *starts,
        scratch=[pltpu.VMEM((2, 1, Y, X), jnp.int32), pltpu.SemaphoreType.DMA((2, 4))],
        in_specs=[hbm, hbm],
        name="send",
    )
    moved, damage, cols = call(
        load_kernel,
        [vector, field, columns],
        *starts,
        to_first,
        scratch=[pltpu.VMEM((Z, Y, X), jnp.int32), pltpu.SemaphoreType.DMA((4,))],
        in_specs=[hbm, hbm, VMEM],
        name="load",
    )
    for step in range(2):
        last = step == 1
        first = lax.ppermute(to_first, "slab", evens)
        second = lax.ppermute(to_second, "slab", odds)
        xh = lax.ppermute(cols, "comp", swap)
        out = call(
            functools.partial(rows_kernel, merged),
            [shape((8, Z, X), F32)] * n,
            moved,
            damage,
            xh,
            name="rows",
        )
        ys = [lax.ppermute(y, "pencil", pairs) for y, pairs in zip(out, y_pairs)]
        after = [out[0]]
        if not last:
            inner_rows, outer_rows = call(
                functools.partial(weights_kernel, Z, Y),
                [
                    shape((2 * (Z - 4) * Y, sensors), jnp.bfloat16),
                    shape((8 * Y, sensors), jnp.bfloat16),
                ],
                obs_weight.reshape(Z * Y, sensors),
                sensor_cell.reshape(1, sensors),
                out[0],
                name="weights",
            )
            after.append(inner_rows)
        middle = call(
            middle_kernel,
            margins + [shape((Z - 2, Y, X), F32)],
            moved,
            damage,
            toughness,
            xh,
            *after,
            name="middle",
        )
        def run_inner(after):
            args = [toughness, ys[0], ys[-1], after]
            return call(
                functools.partial(inner_kernel, merged),
                margins + [shape((Z - 2, Y, X), F32)],
                *args,
                *middle,
                name="inner",
                micros=2,
                alias={len(args) + k: k for k in range(4)},
            )

        if last:
            U, D, S, inner_damage = run_inner(xh)
        *corner_rows, corner_columns = call(
            lambda a, b, _, *rest: corners_kernel(merged, a, b, rest[-1], *rest[:-1]),
            [shape((SUB, X), F32)] * n + [columns],
            first,
            second,
            inner_damage if last else middle[3],
            name="corners",
        )
        if not last:
            U, D, S, inner_damage = run_inner(corner_columns)
        args = [moved, S, corner_columns]
        outs = [shape((3, Z - 4, Y, X), F32)]
        if last:
            args.append(inner_rows)
            outs.append(shape((SUB, sensors), F32))
        inner_moved, *more = call(
            functools.partial(moved_kernel, last),
            outs,
            *args,
            scratch=[pltpu.VMEM(((Z - 4) * Y, LANES), F32)] if last else [],
            name="moved",
        )
        if last:
            more.append(outer_rows)
        crows = [lax.ppermute(y, "pencil", pairs) for y, pairs in zip(corner_rows, y_pairs)]
        ccols = lax.ppermute(corner_columns, "comp", swap)
        E, edge_damage = call(
            edge_kernel,
            [edges, shape((2, Y, X), F32)],
            U,
            D,
            toughness,
            first,
            second,
            name="edge",
        )
        args = [moved, first, second, crows[0], crows[-1], ccols, U, D, S, E]
        if last:
            _, edge_moved, part = call(
                functools.partial(outer_kernel, merged, True),
                [
                    edges,
                    shape((3, 4, Y, X), F32),
                    shape((3, sensors // (SUB * LANES), SUB, LANES), F32),
                ],
                *args,
                *more,
                scratch=scratch + [pltpu.VMEM((4 * Y, LANES), F32)],
                name="outer2",
                alias={9: 0},
            )
            moved, damage = call(
                fields_kernel,
                [vector, field],
                inner_moved,
                edge_moved,
                inner_damage,
                edge_damage,
                name="fields",
            )
        else:
            _, moved, damage, cols, to_first, to_second = call(
                functools.partial(outer_kernel, merged, False),
                [edges, vector, field, columns, planes, planes],
                *args,
                inner_moved,
                inner_damage,
                edge_damage,
                scratch=scratch,
                name="outer1",
                alias={9: 0},
            )
    terms = all_sum(part)
    readings = call(
        functools.partial(finish_kernel, len(terms)),
        shape((3, sensors), F32),
        *terms,
        name="finish",
    )
    return moved, damage, readings


def solution(mesh):
    return jax.shard_map(
        local,
        mesh=mesh,
        in_specs=(
            P(None, ("groups", "slab"), "pencil", "comp"),
            P(("groups", "slab"), "pencil", "comp"),
            P(("groups", "slab"), "pencil", "comp"),
            P("slab", "pencil", "comp", None),
            P(),
        ),
        out_specs=(
            P(None, ("groups", "slab"), "pencil", "comp"),
            P(("groups", "slab"), "pencil", "comp"),
            P(None, "groups"),
        ),
        check_vma=False,
    )
```

```python
import functools

import jax
import jax.numpy as jnp
from jax import lax
from jax.experimental import pallas as pl
from jax.experimental.pallas import tpu as pltpu
from jax.sharding import PartitionSpec as P


SHEAR_MODULUS = 1.0
LAME_FIRST = 1.5
RESIDUAL_STIFF = 0.001
TIME_DISP = 0.15
TIME_DAMAGE = 0.08
DAMAGE_LEVEL = 0.45
POINT_GAIN = 8.0
LANES = 128
SUB = 8
COS_THIRD = (
    0.5000000037331834,
    0.5773496613984853,
    -0.11109449276880777,
    0.05327935086024303,
    -0.031925412185213546,
    0.01960032102518762,
    -0.010237508432464154,
    0.003654119632233793,
    -0.0006260453394989179,
)
F32 = jnp.float32
VMEM_LIMIT = 24 * 1024 * 1024
VMEM = pl.BlockSpec(memory_space=pltpu.VMEM)


def positive_square_sum(m00, m11, m22, m01, m02, m12):
    mean = (m00 + m11 + m22) * (1.0 / 3.0)
    b00, b11, b22 = m00 - mean, m11 - mean, m22 - mean
    s01, s02, s12 = m01 * m01, m02 * m02, m12 * m12
    p2 = (b00 * b00 + b11 * b11 + b22 * b22) * (1.0 / 6.0) + (s01 + s02 + s12) * (1.0 / 3.0)
    det = b00 * (b11 * b22 - s12) + 2.0 * (m01 * m02) * m12 - b11 * s02 - b22 * s01
    mean2 = mean * mean
    whole = mean * (mean2 - 3.0 * p2) + det
    up = whole >= 0.0
    safe = jnp.maximum(p2, 1e-24)
    inv = lax.rsqrt(safe)
    p = safe * inv
    half = 0.25 * (det * inv) * (inv * inv)
    half = jnp.where(up, half, -half) + 0.5
    half = jnp.minimum(jnp.maximum(half, 0.0), 1.0)
    t = jnp.sqrt(half)
    c = jnp.full_like(t, COS_THIRD[-1])
    for value in COS_THIRD[-2::-1]:
        c = c * t + value
    pc = p * c
    lead = jnp.where(up, mean, -mean)
    largest = lead + 2.0 * pc
    square = largest * largest
    norm = 6.0 * p2 + 3.0 * mean2
    rest = lead - pc
    return jnp.where(
        up, jnp.where(rest > 0.0, norm, square), jnp.where(rest < 0.0, norm - square, 0.0)
    )


def sides(merged, fn):
    if merged:
        return [jnp.where(lax.axis_index("pencil") == 0, fn(1), fn(-1))]
    return [fn(1), fn(-1)]


def is_left():
    return lax.axis_index("comp") == 0


def pack_columns(tiles, out):
    Y = out.shape[0]
    left = is_left()
    lane = lax.broadcasted_iota(jnp.int32, (Y, LANES), 1)
    slot = jnp.where(left, (lane + 2) // 2 % (LANES // 2), lane // 2)
    acc = jnp.zeros((Y, LANES), F32)
    for entry, plane in enumerate(tiles):
        X = plane.shape[1]
        tile = jnp.where(left, plane[:, X - LANES : X], plane[:, 0:LANES])
        turned = pltpu.roll(tile, 2 * entry, 1) if entry else tile
        acc = jnp.where(slot == entry, turned, acc)
    out[...] = jnp.where(left, pltpu.roll(acc, 2, 1), acc)


def put_columns(u, d, out):
    Z = d.shape[0]
    pack_columns([u.at[c, z] for c in range(3) for z in range(Z)] + [d.at[z] for z in range(Z)], out)


def is_even():
    return lax.axis_index("slab") % 2 == 0


def put_planes(u, d, first, second):
    _, Z, _, _ = u.shape
    even = is_even()
    for c in range(3):
        up, down = u[c, Z - 2 : Z], u[c, 0:2]
        first[2 * c : 2 * c + 2] = jnp.where(even, up, down)
        second[2 * c : 2 * c + 2] = jnp.where(even, down, up)
    up, down = d[Z - 1], d[0]
    first[6] = jnp.where(even, up, down)
    second[6] = jnp.where(even, down, up)


def plane_readers(first, second):
    even = is_even()

    def low(*at):
        return jnp.where(even, second[at], first[at])

    def high(*at):
        return jnp.where(even, first[at], second[at])

    return low, high


def column_reader(packet):
    rows = packet.shape[0]
    left = is_left()
    lane = lax.broadcasted_iota(jnp.int32, (rows, LANES), 1)
    inside = jnp.where(left, lane, LANES - 1 - lane) < 2
    packet = jnp.where(left, packet, pltpu.roll(packet, LANES - 2, 1))

    def column(entry):
        shift = (LANES - 2 * entry) % LANES
        turned = pltpu.roll(packet, shift, 1) if shift else packet
        return jnp.where(inside, turned, 0.0)

    return column


def send_kernel(u, label, first, second, rows, sems):
    Z = label.shape[0]
    parity = lax.axis_index("slab") & 1
    copies = []
    for k, (out, side) in enumerate(((first, 1 - parity), (second, parity))):
        for c in range(3):
            copies.append(
                pltpu.make_async_copy(
                    u.at[c, pl.ds(side * (Z - 2), 2)], out.at[2 * c : 2 * c + 2], sems.at[k, c]
                )
            )
        copies.append(
            pltpu.make_async_copy(label.at[pl.ds(side * (Z - 1), 1)], rows.at[k], sems.at[k, 3])
        )
    for copy in copies:
        copy.start()
    for copy in copies:
        copy.wait()
    first[6] = DAMAGE_LEVEL * rows[0, 0].astype(F32)
    second[6] = DAMAGE_LEVEL * rows[1, 0].astype(F32)


def load_kernel(u_hbm, label_hbm, first, u, d, cols, label, sems):
    del first
    copies = [pltpu.make_async_copy(u_hbm.at[c], u.at[c], sems.at[c]) for c in range(3)]
    copies.append(pltpu.make_async_copy(label_hbm, label, sems.at[3]))
    for copy in copies:
        copy.start()
    copies[3].wait()
    d[...] = DAMAGE_LEVEL * label[...].astype(F32)
    for copy in copies[:3]:
        copy.wait()
    put_columns(u, d, cols)


def rows_kernel(merged, u, d, xh, *outs):
    _, _, Y, _ = u.shape
    for c in range(3):
        for layer in range(2):
            row = lambda s: u[c, :, Y - 2 + layer if s > 0 else layer, :]
            for ref, value in zip(outs, sides(merged, row)):
                ref[2 * c + layer] = value
    for ref, value in zip(outs, sides(merged, lambda s: d[:, Y - 1 if s > 0 else 0, :])):
        ref[6] = value
    corner = lambda s: xh[Y - 1 : Y, :] if s > 0 else xh[0:1, :]
    for ref, value in zip(outs, sides(merged, corner)):
        ref[7, 0:1, 0:LANES] = value


def near_planes(first, second):
    low, high = plane_readers(first, second)
    return [low(2 * c + 1) for c in range(3)] + [high(2 * c) for c in range(3)]


def corner_rows_kernel(merged, first, second, after, *outs):
    del after
    Y = first.shape[1]
    for k, plane in enumerate(near_planes(first, second)):
        edge = lambda s: plane[Y - 1 : Y, :] if s > 0 else plane[0:1, :]
        for ref, value in zip(outs, sides(merged, edge)):
            ref[k : k + 1, :] = value


def corner_columns_kernel(first, second, after, cols):
    del after
    pack_columns(near_planes(first, second), cols)


def row_keepers(merged):
    if not merged:
        return (lambda value: value), (lambda value: value)
    py = lax.axis_index("pencil")
    return (
        lambda value: jnp.where(py != 0, value, 0.0),
        lambda value: jnp.where(py == 0, value, 0.0),
    )


def lay_out_columns(u, d, xh, U, D):
    _, Z, Y, X = u.shape
    H = SUB
    column = column_reader(xh[...])
    for c in range(3):
        U[c, :, H : H + Y, 0:X] = u[c]
        for z in range(Z):
            U[c, z, H : H + Y, X : X + LANES] = column(c * Z + z)
    D[:, H : H + Y, 0:X] = d[...]
    for z in range(Z):
        D[z, H : H + Y, X : X + LANES] = column(3 * Z + z)


def lay_out_rows(merged, ylo, yhi, U, D):
    Z, X = D.shape[0], ylo.shape[2]
    Y, H = D.shape[1] - 2 * SUB, SUB
    low_of, high_of = row_keepers(merged)
    low_corner = column_reader(low_of(ylo[7, 0:1, 0:LANES]))
    high_corner = column_reader(high_of(yhi[7, 0:1, 0:LANES]))
    for c in range(3):
        for layer in range(2):
            low, high = low_of(ylo[2 * c + layer]), high_of(yhi[2 * c + layer])
            for z in range(Z):
                U[c, z, H - 2 + layer : H - 1 + layer, 0:X] = low[z : z + 1]
                U[c, z, H + Y + layer : H + Y + layer + 1, 0:X] = high[z : z + 1]
        for z in range(Z):
            U[c, z, H - 1 : H, X : X + LANES] = low_corner(c * Z + z)
            U[c, z, H + Y : H + Y + 1, X : X + LANES] = high_corner(c * Z + z)
    low, high = low_of(ylo[6]), high_of(yhi[6])
    for z in range(Z):
        D[z, H - 1 : H, 0:X] = low[z : z + 1]
        D[z, H + Y : H + Y + 1, 0:X] = high[z : z + 1]


def lay_out_face(merged, k, far, near, low_rows, high_rows, columns, F):
    Y, X = near(0).shape
    H = SUB
    low_of, high_of = row_keepers(merged)
    column = column_reader(columns[...])
    for c in range(3):
        F[c, 0, H : H + Y, 0:X] = far(c)
        F[c, 1, H : H + Y, 0:X] = near(c)
        F[c, 1, H : H + Y, X : X + LANES] = column(3 * k + c)
        row = 3 * k + c
        F[c, 1, H - 1 : H, 0:X] = low_of(low_rows[row : row + 1, :])
        F[c, 1, H + Y : H + Y + 1, 0:X] = high_of(high_rows[row : row + 1, :])


def ahead(value):
    return pltpu.roll(value, value.shape[-1] - 1, value.ndim - 1)


def behind(value):
    return pltpu.roll(value, 1, value.ndim - 1)


ZZ, ZY, ZX, YY, YX, XX = range(6)
PAIRS = ((ZZ, ZY, ZX), (ZY, YY, YX), (ZX, YX, XX))


def gradients(at, row, count):
    rows = slice(row, row + count)
    gz, gy, gx = [], [], []
    for c in range(3):
        mid = at(c, 0)
        gz.append(at(c, 1)[rows, :] - at(c, -1)[rows, :])
        gy.append(mid[row + 1 : row + count + 1, :] - mid[row - 1 : row + count - 1, :])
        value = mid[rows, :]
        gx.append(ahead(value) - behind(value))
    return gz, gy, gx


def stiffness(damage):
    keep = 1.0 - damage
    return 0.5 * (keep * keep + RESIDUAL_STIFF)


def energy_of(gz, gy, gx, X):
    cut = lambda value: value[:, 0:X]
    z0, y1, x2 = cut(gz[0]), cut(gy[1]), cut(gx[2])
    mzy = 0.5 * cut(gy[0] + gz[1])
    mzx = 0.5 * cut(gx[0] + gz[2])
    myx = 0.5 * cut(gx[1] + gy[2])
    squares = positive_square_sum(z0, y1, x2, mzy, mzx, myx)
    grow = jnp.maximum(z0 + y1 + x2, 0.0)
    return (0.25 * 0.5 * LAME_FIRST) * (grow * grow) + (0.25 * SHEAR_MODULUS) * squares


def new_damage(mid, below, above, t, energy, tough):
    X = tough.shape[-1]
    r = t * SUB
    value = mid[r : r + SUB, :]
    core = value[:, 0:X]
    lap = (
        below
        + above
        + mid[r + 1 : r + SUB + 1, 0:X]
        + mid[r - 1 : r + SUB - 1, 0:X]
        + (ahead(value) + behind(value))[:, 0:X]
        - 6.0 * core
    )
    return core + TIME_DAMAGE * (2.0 * (1.0 - core) * energy + tough * (lap - core))


def row_stress(at, damage_plane, S, Y, X):
    H = SUB
    for row in (H - 1, H + Y):
        gz, gy, gx = gradients(at, row, 1)
        h = stiffness(damage_plane[row : row + 1, :])
        total = LAME_FIRST * (gz[0] + gy[1] + gx[2])
        for key, value in (
            (ZY, gy[0] + gz[1]),
            (YY, total + 2.0 * gy[1]),
            (YX, gx[1] + gy[2]),
        ):
            S[key, row : row + 1, 0:X] = (h * value)[:, 0:X]


def tile_stress(at, damage_plane, S, t, X):
    rows = slice(t * SUB, t * SUB + SUB)
    gz, gy, gx = gradients(at, t * SUB, SUB)
    h = stiffness(damage_plane[rows, :])
    total = LAME_FIRST * (gz[0] + gy[1] + gx[2])
    S[ZZ, rows, 0:X] = (h * (total + 2.0 * gz[0]))[:, 0:X]
    S[YY, rows, 0:X] = (h * (total + 2.0 * gy[1]))[:, 0:X]
    S[ZY, rows, 0:X] = (h * (gy[0] + gz[1]))[:, 0:X]
    S[ZX, rows, :] = h * (gx[0] + gz[2])
    S[YX, rows, :] = h * (gx[1] + gy[2])
    S[XX, rows, :] = h * (total + 2.0 * gx[2])
    return gz, gy, gx


def side_stress(at, damage_plane, S, Y, X):
    for t in range(1, Y // SUB + 1):
        r = t * SUB
        rows, out = slice(r, r + SUB), slice(X, X + LANES)
        gz, gy, gx = [], [], []
        for c in range(3):
            mid = at(c, 0)
            gz.append(at(c, 1)[rows, out] - at(c, -1)[rows, out])
            gy.append(mid[r + 1 : r + SUB + 1, out] - mid[r - 1 : r + SUB - 1, out])
            value = mid[rows, :]
            gx.append((ahead(value) - behind(value))[:, out])
        h = stiffness(damage_plane[rows, out])
        total = LAME_FIRST * (gz[0] + gy[1] + gx[2])
        S[ZX, rows, out] = h * (gx[0] + gz[2])
        S[YX, rows, out] = h * (gx[1] + gy[2])
        S[XX, rows, out] = h * (total + 2.0 * gx[2])


def face_stress(at, damage, S, Y, X):
    for t in range(1, Y // SUB + 1):
        rows = slice(t * SUB, t * SUB + SUB)
        gz, gy, gx = gradients(at, t * SUB, SUB)
        h = stiffness(damage(slice((t - 1) * SUB, t * SUB)))
        total = LAME_FIRST * (gz[0] + gy[1] + gx[2])
        for key, value in (
            (ZZ, total + 2.0 * gz[0]),
            (ZY, gy[0] + gz[1]),
            (ZX, gx[0] + gz[2]),
        ):
            S[key, rows, 0:X] = h * value[:, 0:X]


def plane_moved(below, mid, above, u_plane, t, X):
    r = t * SUB
    rows = slice(r, r + SUB)
    out = []
    for c in range(3):
        kz, ky, kx = PAIRS[c]
        value = mid[kx, rows, :]
        force = (
            above[kz, rows, 0:X]
            - below[kz, rows, 0:X]
            + mid[ky, r + 1 : r + SUB + 1, 0:X]
            - mid[ky, r - 1 : r + SUB - 1, 0:X]
            + (ahead(value) - behind(value))[:, 0:X]
        )
        out.append(u_plane(c)[(t - 1) * SUB : t * SUB, :] + (0.5 * TIME_DISP) * force)
    return out


def row_sums(new):
    lane = lax.broadcasted_iota(jnp.int32, (SUB, LANES), 1)
    sums = [jnp.sum(value, axis=-1, keepdims=True) for value in new]
    return jnp.where(lane == 0, sums[0], jnp.where(lane == 1, sums[1], sums[2]))


def means_of(pool, X):
    return (pool * (1.0 / X)).T[0:SUB].astype(jnp.bfloat16)


def inner_tiles(z, tiles, U, D, S, tough, damage):
    X = tough.shape[2]
    for t in tiles:
        slopes = tile_stress(lambda c, dz: U.at[c, z + dz], D.at[z], S.at[z - 1], t, X)
        if damage:
            rows = slice(t * SUB, t * SUB + SUB)
            own = slice((t - 1) * SUB, t * SUB)
            (out,) = damage
            out[z - 1, own, :] = new_damage(
                D.at[z],
                D[z - 1, rows, 0:X],
                D[z + 1, rows, 0:X],
                t,
                energy_of(*slopes, X),
                tough[z, own, :],
            )


def middle_kernel(last, u, d, tough, xh, *rest):
    U, D, S, *damage = rest[-3 if last else -4 :]
    Z, Y, _ = tough.shape
    lay_out_columns(u, d, xh, U, D)

    @pl.loop(1, Z - 1)
    def _(z):
        inner_tiles(z, range(2, Y // SUB), U, D, S, tough, damage)


def inner_kernel(merged, tough, ylo, yhi, after, *refs):
    del after
    U, D, S, *damage = refs[len(refs) // 2 :]
    Z, Y, X = tough.shape
    lay_out_rows(merged, ylo, yhi, U, D)

    @pl.loop(1, Z - 1)
    def _(z):
        row_stress(lambda c, dz: U.at[c, z + dz], D.at[z], S.at[z - 1], Y, X)
        inner_tiles(z, (1, Y // SUB), U, D, S, tough, damage)


def moved_kernel(last, u, S, after, *rest):
    del after
    if last:
        weight, moved, part, pool = rest
    else:
        (moved,) = rest
    _, Z, Y, X = u.shape

    @pl.loop(2, Z - 2)
    def _(z):
        for t in range(1, Y // SUB + 1):
            own = slice((t - 1) * SUB, t * SUB)
            new = plane_moved(
                S.at[z - 2], S.at[z - 1], S.at[z], lambda c: u.at[c, z], t, X
            )
            for c in range(3):
                moved[c, z - 2, own, :] = new[c]
            if last:
                start = pl.multiple_of((z - 2) * Y + (t - 1) * SUB, SUB)
                pool[pl.ds(start, SUB), :] = row_sums(new)

    if last:
        means = means_of(pool[...], X)
        means = jnp.concatenate([means, means], axis=1)
        chunk = 8 * LANES
        for k in range(weight.shape[1] // chunk):
            cols = slice(k * chunk, (k + 1) * chunk)
            part[:, cols] = jnp.dot(means, weight[:, cols], preferred_element_type=F32)


def weights_kernel(Z, Y, weight, sensor, after, inner, outer):
    del after
    count = lax.axis_size("comp")
    spread = Y * lax.axis_size("pencil")
    index = lax.broadcasted_iota(jnp.int32, (Z * Y, 1), 0)
    plane = lax.axis_index("slab") * Z + index // Y
    row = lax.axis_index("pencil") * Y + index % Y
    ids = (plane * spread + row) * count + lax.axis_index("comp")
    chunk = 8 * LANES
    two, end = 2 * Y, (Z - 2) * Y
    middle = end - two
    inner[0:middle, :] = weight[two:end, :]
    outer[0:two, :] = weight[0:two, :]
    outer[two : 2 * two, :] = weight[end : end + two, :]
    for k in range(sensor.shape[1] // chunk):
        cols = slice(k * chunk, (k + 1) * chunk)
        picks = jnp.where(ids == sensor[:, cols], POINT_GAIN, 0.0).astype(jnp.bfloat16)
        inner[middle : 2 * middle, cols] = picks[two:end]
        outer[2 * two : 3 * two, cols] = picks[0:two]
        outer[3 * two : 4 * two, cols] = picks[end : end + two]


def edge_slopes(U, low, high, z, t, X):
    Z = U.shape[1]
    r = t * SUB
    rows = slice(r, r + SUB)
    own = slice((t - 1) * SUB, t * SUB)
    gz, gy, gx = [], [], []
    for c in range(3):
        below = low(2 * c + 1, own) if z == 0 else U[c, z - 1, rows, 0:X]
        above = high(2 * c, own) if z == Z - 1 else U[c, z + 1, rows, 0:X]
        gz.append(above - below)
        gy.append(U[c, z, r + 1 : r + SUB + 1, 0:X] - U[c, z, r - 1 : r + SUB - 1, 0:X])
        value = U[c, z, rows, :]
        gx.append((ahead(value) - behind(value))[:, 0:X])
    return gz, gy, gx


def edge_damage(D, low, high, z, t, slopes, tough):
    Z, X = D.shape[0], tough.shape[2]
    rows = slice(t * SUB, t * SUB + SUB)
    own = slice((t - 1) * SUB, t * SUB)
    below = low(6, own) if z == 0 else D[z - 1, rows, 0:X]
    above = high(6, own) if z == Z - 1 else D[z + 1, rows, 0:X]
    return new_damage(D.at[z], below, above, t, energy_of(*slopes, X), tough[z, own, :])


def edge_kernel(U, D, tough, first, second, S, *damage):
    Z, Y, X = tough.shape
    low, high = plane_readers(first, second)
    for k, z in enumerate((0, Z - 1)):
        for t in range(1, Y // SUB + 1):
            rows = slice(t * SUB, t * SUB + SUB)
            gz, gy, gx = edge_slopes(U, low, high, z, t, X)
            h = stiffness(D[z, rows, 0:X])
            total = LAME_FIRST * (gz[0] + gy[1] + gx[2])
            S[k, ZZ, rows, 0:X] = h * (total + 2.0 * gz[0])
            S[k, YY, rows, 0:X] = h * (total + 2.0 * gy[1])
            S[k, XX, rows, 0:X] = h * (total + 2.0 * gx[2])
            S[k, ZY, rows, 0:X] = h * (gy[0] + gz[1])
            S[k, ZX, rows, 0:X] = h * (gx[0] + gz[2])
            S[k, YX, rows, 0:X] = h * (gx[1] + gy[2])
            if damage:
                own = slice((t - 1) * SUB, t * SUB)
                damage[0][k, own, :] = edge_damage(D, low, high, z, t, (gz, gy, gx), tough)


def damage_kernel(U, D, tough, first, second, after, damage):
    del after
    Z, Y, X = tough.shape
    low, high = plane_readers(first, second)
    tiles = range(1, Y // SUB + 1)
    for z in (0, Z - 1):
        for t in tiles:
            own = slice((t - 1) * SUB, t * SUB)
            slopes = edge_slopes(U, low, high, z, t, X)
            damage[z, own, :] = edge_damage(D, low, high, z, t, slopes, tough)

    @pl.loop(1, Z - 1)
    def _(z):
        for t in tiles:
            r = t * SUB
            rows = slice(r, r + SUB)
            own = slice((t - 1) * SUB, t * SUB)
            gz, gy, gx = gradients(lambda c, dz: U.at[c, z + dz], r, SUB)
            damage[z, own, :] = new_damage(
                D.at[z],
                D[z - 1, rows, 0:X],
                D[z + 1, rows, 0:X],
                t,
                energy_of(gz, gy, gx, X),
                tough[z, own, :],
            )


def outer_kernel(merged, last, *refs):
    rest = list(refs)
    take = lambda k: [rest.pop(0) for _ in range(k)]
    u, first, second, low_rows, high_rows, columns, U, D, S, E_in = take(10)
    if last:
        inner_part, edge_rows = take(2)
        E, moved, part = take(3)
    else:
        inner_moved, inner_damage, edge_damage = take(3)
        E, moved, damage, cols, to_first, to_second = take(6)
    del E_in
    low_face, high_face, faces = take(3)
    if last:
        (pool,) = take(1)
    _, Z, Y, X = u.shape
    tiles = range(1, Y // SUB + 1)
    low, high = plane_readers(first, second)
    lay_out_face(
        merged, 0, lambda c: low(2 * c), lambda c: low(2 * c + 1), low_rows, high_rows, columns, low_face
    )
    lay_out_face(
        merged, 1, lambda c: high(2 * c + 1), lambda c: high(2 * c), low_rows, high_rows, columns, high_face
    )

    def at_plane(z):
        def at(c, dz):
            k = z + dz
            if k < 0:
                return low_face.at[c, 2 + k]
            if k >= Z:
                return high_face.at[c, Z + 1 - k]
            return U.at[c, k]

        return at

    face_stress(at_plane(-1), lambda own: low(6, own), faces.at[0], Y, X)
    face_stress(at_plane(Z), lambda own: high(6, own), faces.at[1], Y, X)
    for k, z in enumerate((0, Z - 1)):
        row_stress(at_plane(z), D.at[z], E.at[k], Y, X)
        side_stress(at_plane(z), D.at[z], E.at[k], Y, X)

    def stress(z):
        if z < 0:
            return faces.at[0]
        if z >= Z:
            return faces.at[1]
        if z == 0:
            return E.at[0]
        if z == Z - 1:
            return E.at[1]
        return S.at[z - 1]

    for k, z in enumerate((0, 1, Z - 2, Z - 1)):
        for t in tiles:
            own = slice((t - 1) * SUB, t * SUB)
            new = plane_moved(stress(z - 1), stress(z), stress(z + 1), lambda c: u.at[c, z], t, X)
            for c in range(3):
                moved[c, k if last else z, own, :] = new[c]
            if last:
                start = k * Y + (t - 1) * SUB
                pool[start : start + SUB, :] = row_sums(new)
    if last:
        means = means_of(pool[...], X)
        means = jnp.concatenate([means, means], axis=1)
        chunk = 8 * LANES
        sub = lax.broadcasted_iota(jnp.int32, (SUB, LANES), 0)
        for k in range(edge_rows.shape[1] // chunk):
            start = slice(k * chunk, (k + 1) * chunk)
            value = inner_part[:, start] + jnp.dot(
                means, edge_rows[:, start], preferred_element_type=F32
            )
            for c in range(3):
                tile = jnp.zeros((SUB, LANES), F32)
                for j in range(SUB):
                    piece = value[c : c + 1, j * LANES : (j + 1) * LANES]
                    tile = jnp.where(sub == j, piece, tile)
                part[c, k] = tile
    else:
        for c in range(3):
            moved[c, 2 : Z - 2] = inner_moved[c]
        damage[0] = edge_damage[0]
        damage[1 : Z - 1] = inner_damage[...]
        damage[Z - 1] = edge_damage[1]
        put_planes(moved, damage, to_first, to_second)
        put_columns(moved, damage, cols)


def fields_kernel(inner_moved, edge_moved, moved):
    Z = moved.shape[1]
    for c in range(3):
        moved[c, 0:2] = edge_moved[c, 0:2]
        moved[c, 2 : Z - 2] = inner_moved[c]
        moved[c, Z - 2 : Z] = edge_moved[c, 2:4]


def finish_kernel(*refs):
    out = refs[-1]
    total = refs[0][...]
    for ref in refs[1:-1]:
        total = total + ref[...]
    for c in range(3):
        for k in range(total.shape[1]):
            for j in range(SUB):
                start = (k * SUB + j) * LANES
                out[c : c + 1, start : start + LANES] = total[c, k, j : j + 1, :]


def call(kernel, outs, *args, scratch=(), in_specs=None, micros=1, alias=None):
    many = isinstance(outs, (list, tuple))
    return pl.pallas_call(
        kernel,
        out_shape=outs,
        in_specs=in_specs or [VMEM] * len(args),
        out_specs=[VMEM] * len(outs) if many else VMEM,
        scratch_shapes=list(scratch),
        compiler_params=pltpu.CompilerParams(vmem_limit_bytes=VMEM_LIMIT),
        cost_estimate=pl.CostEstimate(
            flops=0, bytes_accessed=micros * 3_000_000, transcendentals=0
        ),
        input_output_aliases=alias or {},
    )(*args)


def up_pairs(count):
    return [(i, i + 1) for i in range(count - 1)]


def down_pairs(count):
    return [(i + 1, i) for i in range(count - 1)]


def all_sum(value):
    for axis in ("comp", "pencil"):
        count = lax.axis_size(axis)
        bit = 1
        while bit < count:
            other = lax.ppermute(value, axis, [(i, i ^ bit) for i in range(count)])
            value = value + other
            bit *= 2
    count = lax.axis_size("slab")
    bit = 1
    while count // bit > 4:
        value = value + lax.ppermute(value, "slab", [(i, i ^ bit) for i in range(count)])
        bit *= 2
    terms = [value]
    for k in range(1, count // bit):
        terms.append(lax.ppermute(value, "slab", [(i, i ^ (k * bit)) for i in range(count)]))
    return terms


def local(u_start, toughness, crack_label, obs_weight, sensor_cell):
    Z, Y, X = toughness.shape
    slabs, pencils = lax.axis_size("slab"), lax.axis_size("pencil")
    if lax.axis_size("comp") != 2 or Z < 6 or Z % SUB or 8 * Z > LANES:
        raise ValueError("unsupported block")
    merged = pencils == 2
    n = 1 if merged else 2
    shape = jax.ShapeDtypeStruct
    field, vector = shape((Z, Y, X), F32), shape((3, Z, Y, X), F32)
    columns = shape((Y, LANES), F32)
    sensors = sensor_cell.shape[0]
    rows, lanes = Y + 2 * SUB, X + LANES
    y_up, y_down = up_pairs(pencils), down_pairs(pencils)
    y_pairs = [y_up + y_down] if merged else [y_up, y_down]
    margins = [
        shape((3, Z, rows, lanes), F32),
        shape((Z, rows, lanes), F32),
        shape((Z - 2, 6, rows, lanes), F32),
    ]
    scratch = [
        pltpu.VMEM((3, 2, rows, lanes), F32),
        pltpu.VMEM((3, 2, rows, lanes), F32),
        pltpu.VMEM((2, 3, rows, lanes), F32),
    ]
    edges = shape((2, 6, rows, lanes), F32)
    planes = shape((7, Y, X), F32)
    evens = [pair for pair in up_pairs(slabs) + down_pairs(slabs) if min(pair) % 2 == 0]
    odds = [pair for pair in up_pairs(slabs) + down_pairs(slabs) if min(pair) % 2 == 1]
    swap = [(0, 1), (1, 0)]
    hbm = pl.BlockSpec(memory_space=pltpu.HBM)
    starts = [
        pltpu.with_memory_space_constraint(value, pltpu.HBM) for value in (u_start, crack_label)
    ]
    to_first, to_second = call(
        send_kernel,
        [planes, planes],
        *starts,
        scratch=[pltpu.VMEM((2, 1, Y, X), jnp.int32), pltpu.SemaphoreType.DMA((2, 4))],
        in_specs=[hbm, hbm],
    )
    moved, damage, cols = call(
        load_kernel,
        [vector, field, columns],
        *starts,
        to_first,
        scratch=[pltpu.VMEM((Z, Y, X), jnp.int32), pltpu.SemaphoreType.DMA((4,))],
        in_specs=[hbm, hbm, VMEM],
    )
    for step in range(2):
        last = step == 1
        first = lax.ppermute(to_first, "slab", evens)
        second = lax.ppermute(to_second, "slab", odds)
        xh = lax.ppermute(cols, "comp", swap)
        out = call(
            functools.partial(rows_kernel, merged), [shape((8, Z, X), F32)] * n, moved, damage, xh
        )
        ys = [lax.ppermute(y, "pencil", pairs) for y, pairs in zip(out, y_pairs)]
        after = [out[0]]
        if not last:
            inner_rows, outer_rows = call(
                functools.partial(weights_kernel, Z, Y),
                [
                    shape((2 * (Z - 4) * Y, sensors), jnp.bfloat16),
                    shape((8 * Y, sensors), jnp.bfloat16),
                ],
                obs_weight.reshape(Z * Y, sensors),
                sensor_cell.reshape(1, sensors),
                out[0],
            )
            after.append(inner_rows)
        inner_outs = margins if last else margins + [shape((Z - 2, Y, X), F32)]
        middle = call(
            functools.partial(middle_kernel, last), inner_outs, moved, damage, toughness, xh, *after
        )

        def run_inner(after):
            args = [toughness, ys[0], ys[-1], after]
            return call(
                functools.partial(inner_kernel, merged),
                inner_outs,
                *args,
                *middle,
                micros=2,
                alias={len(args) + k: k for k in range(len(inner_outs))},
            )

        if last:
            inner = run_inner(xh)
        corner_rows = call(
            functools.partial(corner_rows_kernel, merged),
            [shape((SUB, X), F32)] * n,
            first,
            second,
            inner[2] if last else middle[2],
        )
        corner_columns = call(corner_columns_kernel, columns, first, second, corner_rows[0])
        if not last:
            inner = run_inner(corner_columns)
        U, D, S = inner[:3]
        args = [moved, S, corner_columns]
        outs = [shape((3, Z - 4, Y, X), F32)]
        if last:
            args.append(inner_rows)
            outs.append(shape((SUB, sensors), F32))
        inner_moved, *more = call(
            functools.partial(moved_kernel, last),
            outs,
            *args,
            scratch=[pltpu.VMEM(((Z - 4) * Y, LANES), F32)] if last else [],
        )
        if last:
            more.append(outer_rows)
        crows = [lax.ppermute(y, "pencil", pairs) for y, pairs in zip(corner_rows, y_pairs)]
        ccols = lax.ppermute(corner_columns, "comp", swap)
        E, *more_damage = call(
            edge_kernel,
            [edges] if last else [edges, shape((2, Y, X), F32)],
            U,
            D,
            toughness,
            first,
            second,
        )
        args = [moved, first, second, crows[0], crows[-1], ccols, U, D, S, E]
        if last:
            _, edge_moved, part = call(
                functools.partial(outer_kernel, merged, True),
                [
                    edges,
                    shape((3, 4, Y, X), F32),
                    shape((3, sensors // (SUB * LANES), SUB, LANES), F32),
                ],
                *args,
                *more,
                scratch=scratch + [pltpu.VMEM((4 * Y, LANES), F32)],
                alias={9: 0},
            )
            damage = call(damage_kernel, field, U, D, toughness, first, second, part, micros=2)
            moved = call(fields_kernel, vector, inner_moved, edge_moved)
        else:
            _, moved, damage, cols, to_first, to_second = call(
                functools.partial(outer_kernel, merged, False),
                [edges, vector, field, columns, planes, planes],
                *args,
                inner_moved,
                inner[3],
                *more_damage,
                scratch=scratch,
                alias={9: 0},
            )
    terms = all_sum(part)
    readings = call(finish_kernel, shape((3, sensors), F32), *terms)
    return moved, damage, readings


def solution(mesh):
    return jax.shard_map(
        local,
        mesh=mesh,
        in_specs=(
            P(None, ("groups", "slab"), "pencil", "comp"),
            P(("groups", "slab"), "pencil", "comp"),
            P(("groups", "slab"), "pencil", "comp"),
            P("slab", "pencil", "comp", None),
            P(),
        ),
        out_specs=(
            P(None, ("groups", "slab"), "pencil", "comp"),
            P(("groups", "slab"), "pencil", "comp"),
            P(None, "groups"),
        ),
        check_vma=False,
    )
```

```python
import functools

import jax
import jax.numpy as jnp
from jax import lax
from jax.experimental import pallas as pl
from jax.experimental.pallas import tpu as pltpu
from jax.sharding import PartitionSpec as P


SHEAR_MODULUS = 1.0
LAME_FIRST = 1.5
RESIDUAL_STIFF = 0.001
TIME_DISP = 0.15
TIME_DAMAGE = 0.08
DAMAGE_LEVEL = 0.45
POINT_GAIN = 8.0
LANES = 128
SUB = 8
COS_THIRD = (
    0.5000000037331834,
    0.5773496613984853,
    -0.11109449276880777,
    0.05327935086024303,
    -0.031925412185213546,
    0.01960032102518762,
    -0.010237508432464154,
    0.003654119632233793,
    -0.0006260453394989179,
)
F32 = jnp.float32
VMEM_LIMIT = 24 * 1024 * 1024
VMEM = pl.BlockSpec(memory_space=pltpu.VMEM)


def positive_square_sum(m00, m11, m22, m01, m02, m12):
    mean = (m00 + m11 + m22) * (1.0 / 3.0)
    b00, b11, b22 = m00 - mean, m11 - mean, m22 - mean
    s01, s02, s12 = m01 * m01, m02 * m02, m12 * m12
    p2 = (b00 * b00 + b11 * b11 + b22 * b22) * (1.0 / 6.0) + (s01 + s02 + s12) * (1.0 / 3.0)
    det = b00 * (b11 * b22 - s12) + 2.0 * (m01 * m02) * m12 - b11 * s02 - b22 * s01
    mean2 = mean * mean
    whole = mean * (mean2 - 3.0 * p2) + det
    up = whole >= 0.0
    safe = jnp.maximum(p2, 1e-24)
    inv = lax.rsqrt(safe)
    p = safe * inv
    half = 0.25 * (det * inv) * (inv * inv)
    half = jnp.where(up, half, -half) + 0.5
    half = jnp.minimum(jnp.maximum(half, 0.0), 1.0)
    t = jnp.sqrt(half)
    c = jnp.full_like(t, COS_THIRD[-1])
    for value in COS_THIRD[-2::-1]:
        c = c * t + value
    pc = p * c
    lead = jnp.where(up, mean, -mean)
    largest = lead + 2.0 * pc
    square = largest * largest
    norm = 6.0 * p2 + 3.0 * mean2
    rest = lead - pc
    return jnp.where(
        up, jnp.where(rest > 0.0, norm, square), jnp.where(rest < 0.0, norm - square, 0.0)
    )


def sides(merged, fn):
    if merged:
        return [jnp.where(lax.axis_index("pencil") == 0, fn(1), fn(-1))]
    return [fn(1), fn(-1)]


def is_left():
    return lax.axis_index("comp") == 0


def pack_columns(tiles, out):
    Y = out.shape[0]
    left = is_left()
    lane = lax.broadcasted_iota(jnp.int32, (Y, LANES), 1)
    slot = jnp.where(left, (lane + 2) // 2 % (LANES // 2), lane // 2)
    acc = jnp.zeros((Y, LANES), F32)
    for entry, plane in enumerate(tiles):
        X = plane.shape[1]
        tile = jnp.where(left, plane[:, X - LANES : X], plane[:, 0:LANES])
        turned = pltpu.roll(tile, 2 * entry, 1) if entry else tile
        acc = jnp.where(slot == entry, turned, acc)
    out[...] = jnp.where(left, pltpu.roll(acc, 2, 1), acc)


def put_columns(u, d, out):
    Z = d.shape[0]
    pack_columns([u.at[c, z] for c in range(3) for z in range(Z)] + [d.at[z] for z in range(Z)], out)


def is_even():
    return lax.axis_index("slab") % 2 == 0


def put_planes(u, d, first, second):
    _, Z, _, _ = u.shape
    even = is_even()
    for c in range(3):
        up, down = u[c, Z - 2 : Z], u[c, 0:2]
        first[2 * c : 2 * c + 2] = jnp.where(even, up, down)
        second[2 * c : 2 * c + 2] = jnp.where(even, down, up)
    up, down = d[Z - 1], d[0]
    first[6] = jnp.where(even, up, down)
    second[6] = jnp.where(even, down, up)


def plane_readers(first, second):
    even = is_even()

    def low(*at):
        return jnp.where(even, second[at], first[at])

    def high(*at):
        return jnp.where(even, first[at], second[at])

    return low, high


def column_reader(packet):
    rows = packet.shape[0]
    left = is_left()
    lane = lax.broadcasted_iota(jnp.int32, (rows, LANES), 1)
    inside = jnp.where(left, lane, LANES - 1 - lane) < 2
    packet = jnp.where(left, packet, pltpu.roll(packet, LANES - 2, 1))

    def column(entry):
        shift = (LANES - 2 * entry) % LANES
        turned = pltpu.roll(packet, shift, 1) if shift else packet
        return jnp.where(inside, turned, 0.0)

    return column


def load_kernel(u_hbm, label_hbm, u, d, first, second, label, sems):
    copies = [pltpu.make_async_copy(u_hbm.at[c], u.at[c], sems.at[c]) for c in range(3)]
    copies.append(pltpu.make_async_copy(label_hbm, label, sems.at[3]))
    for copy in copies:
        copy.start()
    copies[3].wait()
    d[...] = DAMAGE_LEVEL * label[...].astype(F32)
    for copy in copies[:3]:
        copy.wait()
    put_planes(u, d, first, second)


def columns_kernel(u, d, first, cols):
    del first
    put_columns(u, d, cols)


def rows_kernel(merged, u, d, xh, *outs):
    _, _, Y, _ = u.shape
    for c in range(3):
        for layer in range(2):
            row = lambda s: u[c, :, Y - 2 + layer if s > 0 else layer, :]
            for ref, value in zip(outs, sides(merged, row)):
                ref[2 * c + layer] = value
    for ref, value in zip(outs, sides(merged, lambda s: d[:, Y - 1 if s > 0 else 0, :])):
        ref[6] = value
    corner = lambda s: xh[Y - 1 : Y, :] if s > 0 else xh[0:1, :]
    for ref, value in zip(outs, sides(merged, corner)):
        ref[7, 0:1, 0:LANES] = value


def near_planes(first, second):
    low, high = plane_readers(first, second)
    return [low(2 * c + 1) for c in range(3)] + [high(2 * c) for c in range(3)]


def corner_rows_kernel(merged, first, second, after, *outs):
    del after
    Y = first.shape[1]
    for k, plane in enumerate(near_planes(first, second)):
        edge = lambda s: plane[Y - 1 : Y, :] if s > 0 else plane[0:1, :]
        for ref, value in zip(outs, sides(merged, edge)):
            ref[k : k + 1, :] = value


def corner_columns_kernel(first, second, after, cols):
    del after
    pack_columns(near_planes(first, second), cols)


def row_keepers(merged):
    if not merged:
        return (lambda value: value), (lambda value: value)
    py = lax.axis_index("pencil")
    return (
        lambda value: jnp.where(py != 0, value, 0.0),
        lambda value: jnp.where(py == 0, value, 0.0),
    )


def lay_out_columns(u, d, xh, U, D):
    _, Z, Y, X = u.shape
    H = SUB
    column = column_reader(xh[...])
    for c in range(3):
        U[c, :, H : H + Y, 0:X] = u[c]
        for z in range(Z):
            U[c, z, H : H + Y, X : X + LANES] = column(c * Z + z)
    D[:, H : H + Y, 0:X] = d[...]
    for z in range(Z):
        D[z, H : H + Y, X : X + LANES] = column(3 * Z + z)


def lay_out_rows(merged, ylo, yhi, U, D):
    Z, X = D.shape[0], ylo.shape[2]
    Y, H = D.shape[1] - 2 * SUB, SUB
    low_of, high_of = row_keepers(merged)
    low_corner = column_reader(low_of(ylo[7, 0:1, 0:LANES]))
    high_corner = column_reader(high_of(yhi[7, 0:1, 0:LANES]))
    for c in range(3):
        for layer in range(2):
            low, high = low_of(ylo[2 * c + layer]), high_of(yhi[2 * c + layer])
            for z in range(Z):
                U[c, z, H - 2 + layer : H - 1 + layer, 0:X] = low[z : z + 1]
                U[c, z, H + Y + layer : H + Y + layer + 1, 0:X] = high[z : z + 1]
        for z in range(Z):
            U[c, z, H - 1 : H, X : X + LANES] = low_corner(c * Z + z)
            U[c, z, H + Y : H + Y + 1, X : X + LANES] = high_corner(c * Z + z)
    low, high = low_of(ylo[6]), high_of(yhi[6])
    for z in range(Z):
        D[z, H - 1 : H, 0:X] = low[z : z + 1]
        D[z, H + Y : H + Y + 1, 0:X] = high[z : z + 1]


def lay_out_face(merged, k, far, near, low_rows, high_rows, columns, F):
    Y, X = near(0).shape
    H = SUB
    low_of, high_of = row_keepers(merged)
    column = column_reader(columns[...])
    for c in range(3):
        F[c, 0, H : H + Y, 0:X] = far(c)
        F[c, 1, H : H + Y, 0:X] = near(c)
        F[c, 1, H : H + Y, X : X + LANES] = column(3 * k + c)
        row = 3 * k + c
        F[c, 1, H - 1 : H, 0:X] = low_of(low_rows[row : row + 1, :])
        F[c, 1, H + Y : H + Y + 1, 0:X] = high_of(high_rows[row : row + 1, :])


def ahead(value):
    return pltpu.roll(value, value.shape[-1] - 1, value.ndim - 1)


def behind(value):
    return pltpu.roll(value, 1, value.ndim - 1)


ZZ, ZY, ZX, YY, YX, XX = range(6)
PAIRS = ((ZZ, ZY, ZX), (ZY, YY, YX), (ZX, YX, XX))


def gradients(at, row, count):
    rows = slice(row, row + count)
    gz, gy, gx = [], [], []
    for c in range(3):
        mid = at(c, 0)
        gz.append(at(c, 1)[rows, :] - at(c, -1)[rows, :])
        gy.append(mid[row + 1 : row + count + 1, :] - mid[row - 1 : row + count - 1, :])
        value = mid[rows, :]
        gx.append(ahead(value) - behind(value))
    return gz, gy, gx


def stiffness(damage):
    keep = 1.0 - damage
    return 0.5 * (keep * keep + RESIDUAL_STIFF)


def energy_of(gz, gy, gx, X):
    cut = lambda value: value[:, 0:X]
    z0, y1, x2 = cut(gz[0]), cut(gy[1]), cut(gx[2])
    mzy = 0.5 * cut(gy[0] + gz[1])
    mzx = 0.5 * cut(gx[0] + gz[2])
    myx = 0.5 * cut(gx[1] + gy[2])
    squares = positive_square_sum(z0, y1, x2, mzy, mzx, myx)
    grow = jnp.maximum(z0 + y1 + x2, 0.0)
    return (0.25 * 0.5 * LAME_FIRST) * (grow * grow) + (0.25 * SHEAR_MODULUS) * squares


def new_damage(mid, below, above, t, energy, tough):
    X = tough.shape[-1]
    r = t * SUB
    value = mid[r : r + SUB, :]
    core = value[:, 0:X]
    lap = (
        below
        + above
        + mid[r + 1 : r + SUB + 1, 0:X]
        + mid[r - 1 : r + SUB - 1, 0:X]
        + (ahead(value) + behind(value))[:, 0:X]
        - 6.0 * core
    )
    return core + TIME_DAMAGE * (2.0 * (1.0 - core) * energy + tough * (lap - core))


def row_stress(at, damage_plane, S, Y, X):
    H = SUB
    for row in (H - 1, H + Y):
        gz, gy, gx = gradients(at, row, 1)
        h = stiffness(damage_plane[row : row + 1, :])
        total = LAME_FIRST * (gz[0] + gy[1] + gx[2])
        for key, value in (
            (ZY, gy[0] + gz[1]),
            (YY, total + 2.0 * gy[1]),
            (YX, gx[1] + gy[2]),
        ):
            S[key, row : row + 1, 0:X] = (h * value)[:, 0:X]


def tile_stress(at, damage_plane, S, t, X):
    rows = slice(t * SUB, t * SUB + SUB)
    gz, gy, gx = gradients(at, t * SUB, SUB)
    h = stiffness(damage_plane[rows, :])
    total = LAME_FIRST * (gz[0] + gy[1] + gx[2])
    S[ZZ, rows, 0:X] = (h * (total + 2.0 * gz[0]))[:, 0:X]
    S[YY, rows, 0:X] = (h * (total + 2.0 * gy[1]))[:, 0:X]
    S[ZY, rows, 0:X] = (h * (gy[0] + gz[1]))[:, 0:X]
    S[ZX, rows, :] = h * (gx[0] + gz[2])
    S[YX, rows, :] = h * (gx[1] + gy[2])
    S[XX, rows, :] = h * (total + 2.0 * gx[2])
    return gz, gy, gx


def side_stress(at, damage_plane, S, Y, X):
    for t in range(1, Y // SUB + 1):
        r = t * SUB
        rows, out = slice(r, r + SUB), slice(X, X + LANES)
        gz, gy, gx = [], [], []
        for c in range(3):
            mid = at(c, 0)
            gz.append(at(c, 1)[rows, out] - at(c, -1)[rows, out])
            gy.append(mid[r + 1 : r + SUB + 1, out] - mid[r - 1 : r + SUB - 1, out])
            value = mid[rows, :]
            gx.append((ahead(value) - behind(value))[:, out])
        h = stiffness(damage_plane[rows, out])
        total = LAME_FIRST * (gz[0] + gy[1] + gx[2])
        S[ZX, rows, out] = h * (gx[0] + gz[2])
        S[YX, rows, out] = h * (gx[1] + gy[2])
        S[XX, rows, out] = h * (total + 2.0 * gx[2])


def face_stress(at, damage, S, Y, X):
    for t in range(1, Y // SUB + 1):
        rows = slice(t * SUB, t * SUB + SUB)
        gz, gy, gx = gradients(at, t * SUB, SUB)
        h = stiffness(damage(slice((t - 1) * SUB, t * SUB)))
        total = LAME_FIRST * (gz[0] + gy[1] + gx[2])
        for key, value in (
            (ZZ, total + 2.0 * gz[0]),
            (ZY, gy[0] + gz[1]),
            (ZX, gx[0] + gz[2]),
        ):
            S[key, rows, 0:X] = h * value[:, 0:X]


def plane_moved(below, mid, above, u_plane, t, X):
    r = t * SUB
    rows = slice(r, r + SUB)
    out = []
    for c in range(3):
        kz, ky, kx = PAIRS[c]
        value = mid[kx, rows, :]
        force = (
            above[kz, rows, 0:X]
            - below[kz, rows, 0:X]
            + mid[ky, r + 1 : r + SUB + 1, 0:X]
            - mid[ky, r - 1 : r + SUB - 1, 0:X]
            + (ahead(value) - behind(value))[:, 0:X]
        )
        out.append(u_plane(c)[(t - 1) * SUB : t * SUB, :] + (0.5 * TIME_DISP) * force)
    return out


def put_folded(pool, start, new):
    for c, value in enumerate(new):
        total = value[:, 0:LANES]
        for k in range(1, value.shape[1] // LANES):
            total = total + value[:, k * LANES : (k + 1) * LANES]
        pool[c, start : start + SUB, :] = total


def sums_of(pool):
    rows = pool.shape[1]
    sub = lax.broadcasted_iota(jnp.int32, (SUB, rows), 0)
    out = jnp.zeros((SUB, rows), F32)
    for c in range(3):
        out = jnp.where(sub == c, jnp.sum(pool[c].T, axis=0, keepdims=True), out)
    return out


def inner_tiles(z, tiles, U, D, S, tough, damage):
    X = tough.shape[2]
    for t in tiles:
        slopes = tile_stress(lambda c, dz: U.at[c, z + dz], D.at[z], S.at[z - 1], t, X)
        if damage:
            rows = slice(t * SUB, t * SUB + SUB)
            own = slice((t - 1) * SUB, t * SUB)
            (out,) = damage
            out[z - 1, own, :] = new_damage(
                D.at[z],
                D[z - 1, rows, 0:X],
                D[z + 1, rows, 0:X],
                t,
                energy_of(*slopes, X),
                tough[z, own, :],
            )


def middle_kernel(last, u, d, tough, xh, *rest):
    U, D, S, *damage = rest[-3 if last else -4 :]
    Z, Y, _ = tough.shape
    lay_out_columns(u, d, xh, U, D)

    @pl.loop(1, Z - 1, unroll=True)
    def _(z):
        inner_tiles(z, range(2, Y // SUB), U, D, S, tough, damage)


def inner_kernel(merged, tough, ylo, yhi, after, *refs):
    del after
    U, D, S, *damage = refs[len(refs) // 2 :]
    Z, Y, X = tough.shape
    lay_out_rows(merged, ylo, yhi, U, D)

    @pl.loop(1, Z - 1, unroll=True)
    def _(z):
        row_stress(lambda c, dz: U.at[c, z + dz], D.at[z], S.at[z - 1], Y, X)
        inner_tiles(z, (1, Y // SUB), U, D, S, tough, damage)


def moved_kernel(last, u, S, after, moved, *more):
    del after
    _, Z, Y, X = u.shape
    for z in range(2, Z - 2):
        for t in range(1, Y // SUB + 1):
            own = slice((t - 1) * SUB, t * SUB)
            new = plane_moved(
                S.at[z - 2], S.at[z - 1], S.at[z], lambda c: u.at[c, z], t, X
            )
            for c in range(3):
                moved[c, z - 2, own, :] = new[c]
            if last:
                put_folded(more[1], (z - 2) * Y + (t - 1) * SUB, new)
    if last:
        sums, pool = more
        sums[...] = sums_of(pool)


def picks_kernel(Z, Y, sensor, weight, after, picks):
    del weight, after
    count = lax.axis_size("comp")
    spread = Y * lax.axis_size("pencil")
    index = lax.broadcasted_iota(jnp.int32, (Z * Y, 1), 0)
    plane = lax.axis_index("slab") * Z + index // Y
    row = lax.axis_index("pencil") * Y + index % Y
    ids = (plane * spread + row) * count + lax.axis_index("comp")
    chunk = 8 * LANES
    for k in range(sensor.shape[1] // chunk):
        cols = slice(k * chunk, (k + 1) * chunk)
        hit = ids == sensor[:, cols]
        picks[:, cols] = jnp.where(hit, POINT_GAIN, 0.0).astype(jnp.bfloat16)


def edge_slopes(U, low, high, z, t, X):
    Z = U.shape[1]
    r = t * SUB
    rows = slice(r, r + SUB)
    own = slice((t - 1) * SUB, t * SUB)
    gz, gy, gx = [], [], []
    for c in range(3):
        below = low(2 * c + 1, own) if z == 0 else U[c, z - 1, rows, 0:X]
        above = high(2 * c, own) if z == Z - 1 else U[c, z + 1, rows, 0:X]
        gz.append(above - below)
        gy.append(U[c, z, r + 1 : r + SUB + 1, 0:X] - U[c, z, r - 1 : r + SUB - 1, 0:X])
        value = U[c, z, rows, :]
        gx.append((ahead(value) - behind(value))[:, 0:X])
    return gz, gy, gx


def edge_damage(D, low, high, z, t, slopes, tough):
    Z, X = D.shape[0], tough.shape[2]
    rows = slice(t * SUB, t * SUB + SUB)
    own = slice((t - 1) * SUB, t * SUB)
    below = low(6, own) if z == 0 else D[z - 1, rows, 0:X]
    above = high(6, own) if z == Z - 1 else D[z + 1, rows, 0:X]
    return new_damage(D.at[z], below, above, t, energy_of(*slopes, X), tough[z, own, :])


def edge_kernel(last, u, inner, U, D, tough, first, second, S, moved, *more):
    Z, Y, X = tough.shape
    pool, damage = (more, ()) if last else ((), more)
    low, high = plane_readers(first, second)
    for k, z in enumerate((0, Z - 1)):
        for t in range(1, Y // SUB + 1):
            rows = slice(t * SUB, t * SUB + SUB)
            gz, gy, gx = edge_slopes(U, low, high, z, t, X)
            h = stiffness(D[z, rows, 0:X])
            total = LAME_FIRST * (gz[0] + gy[1] + gx[2])
            S[k, ZZ, rows, 0:X] = h * (total + 2.0 * gz[0])
            S[k, YY, rows, 0:X] = h * (total + 2.0 * gy[1])
            S[k, XX, rows, 0:X] = h * (total + 2.0 * gx[2])
            S[k, ZY, rows, 0:X] = h * (gy[0] + gz[1])
            S[k, ZX, rows, 0:X] = h * (gx[0] + gz[2])
            S[k, YX, rows, 0:X] = h * (gx[1] + gy[2])
            if damage:
                own = slice((t - 1) * SUB, t * SUB)
                damage[0][k, own, :] = edge_damage(D, low, high, z, t, (gz, gy, gx), tough)
    around = (
        (1, S.at[0], inner.at[0], inner.at[1]),
        (Z - 2, inner.at[Z - 4], inner.at[Z - 3], S.at[1]),
    )
    for k, (z, below, mid, above) in enumerate(around):
        for t in range(1, Y // SUB + 1):
            own = slice((t - 1) * SUB, t * SUB)
            new = plane_moved(below, mid, above, lambda c: u.at[c, z], t, X)
            for c in range(3):
                moved[c, k, own, :] = new[c]
            if last:
                put_folded(pool[0], k * Y + (t - 1) * SUB, new)


def damage_kernel(U, D, tough, first, second, after, damage):
    del after
    Z, Y, X = tough.shape
    low, high = plane_readers(first, second)
    tiles = range(1, Y // SUB + 1)
    for z in (0, Z - 1):
        for t in tiles:
            own = slice((t - 1) * SUB, t * SUB)
            slopes = edge_slopes(U, low, high, z, t, X)
            damage[z, own, :] = edge_damage(D, low, high, z, t, slopes, tough)

    @pl.loop(1, Z - 1, unroll=True)
    def _(z):
        for t in tiles:
            r = t * SUB
            rows = slice(r, r + SUB)
            own = slice((t - 1) * SUB, t * SUB)
            gz, gy, gx = gradients(lambda c, dz: U.at[c, z + dz], r, SUB)
            damage[z, own, :] = new_damage(
                D.at[z],
                D[z - 1, rows, 0:X],
                D[z + 1, rows, 0:X],
                t,
                energy_of(gz, gy, gx, X),
                tough[z, own, :],
            )


def outer_kernel(merged, last, *refs):
    rest = list(refs)
    take = lambda k: [rest.pop(0) for _ in range(k)]
    u, first, second, low_rows, high_rows, columns, U, D, S, E_in = take(10)
    if last:
        inner_sums, near_pool, weight, picks = take(4)
        E, moved, part = take(3)
    else:
        inner_moved, near_moved, inner_damage, edge_damage = take(4)
        E, moved, damage, cols, to_first, to_second = take(6)
    del E_in
    low_face, high_face, faces = take(3)
    if last:
        (pool,) = take(1)
    _, Z, Y, X = u.shape
    tiles = range(1, Y // SUB + 1)
    low, high = plane_readers(first, second)
    lay_out_face(
        merged, 0, lambda c: low(2 * c), lambda c: low(2 * c + 1), low_rows, high_rows, columns, low_face
    )
    lay_out_face(
        merged, 1, lambda c: high(2 * c + 1), lambda c: high(2 * c), low_rows, high_rows, columns, high_face
    )

    def at_plane(z):
        def at(c, dz):
            k = z + dz
            if k < 0:
                return low_face.at[c, 2 + k]
            if k >= Z:
                return high_face.at[c, Z + 1 - k]
            return U.at[c, k]

        return at

    face_stress(at_plane(-1), lambda own: low(6, own), faces.at[0], Y, X)
    face_stress(at_plane(Z), lambda own: high(6, own), faces.at[1], Y, X)
    for k, z in enumerate((0, Z - 1)):
        row_stress(at_plane(z), D.at[z], E.at[k], Y, X)
        side_stress(at_plane(z), D.at[z], E.at[k], Y, X)

    def stress(z):
        if z < 0:
            return faces.at[0]
        if z >= Z:
            return faces.at[1]
        if z == 0:
            return E.at[0]
        if z == Z - 1:
            return E.at[1]
        return S.at[z - 1]

    for k, z in enumerate((0, Z - 1)):
        for t in tiles:
            own = slice((t - 1) * SUB, t * SUB)
            new = plane_moved(stress(z - 1), stress(z), stress(z + 1), lambda c: u.at[c, z], t, X)
            for c in range(3):
                moved[c, k if last else z, own, :] = new[c]
            if last:
                put_folded(pool, 3 * k * Y + (t - 1) * SUB, new)
    if last:
        pool[:, Y : 3 * Y, :] = near_pool[...]
        outer_sums = sums_of(pool)
        means = jnp.concatenate(
            [outer_sums[:, 0 : 2 * Y], inner_sums[...], outer_sums[:, 2 * Y : 4 * Y]], axis=1
        )
        means = (means * (1.0 / X)).astype(jnp.bfloat16)
        chunk = 8 * LANES
        sub = lax.broadcasted_iota(jnp.int32, (SUB, LANES), 0)
        for k in range(weight.shape[1] // chunk):
            start = slice(k * chunk, (k + 1) * chunk)
            value = jnp.dot(means, weight[:, start], preferred_element_type=F32)
            value = value + jnp.dot(means, picks[:, start], preferred_element_type=F32)
            for c in range(3):
                tile = jnp.zeros((SUB, LANES), F32)
                for j in range(SUB):
                    piece = value[c : c + 1, j * LANES : (j + 1) * LANES]
                    tile = jnp.where(sub == j, piece, tile)
                part[c, k] = tile
    else:
        for c in range(3):
            moved[c, 1] = near_moved[c, 0]
            moved[c, 2 : Z - 2] = inner_moved[c]
            moved[c, Z - 2] = near_moved[c, 1]
        damage[0] = edge_damage[0]
        damage[1 : Z - 1] = inner_damage[...]
        damage[Z - 1] = edge_damage[1]
        put_planes(moved, damage, to_first, to_second)
        put_columns(moved, damage, cols)


def fields_kernel(inner_moved, near_moved, edge_moved, moved):
    Z = moved.shape[1]
    for c in range(3):
        moved[c, 0] = edge_moved[c, 0]
        moved[c, 1] = near_moved[c, 0]
        moved[c, 2 : Z - 2] = inner_moved[c]
        moved[c, Z - 2] = near_moved[c, 1]
        moved[c, Z - 1] = edge_moved[c, 1]


def finish_kernel(*refs):
    out = refs[-1]
    total = refs[0][...]
    for ref in refs[1:-1]:
        total = total + ref[...]
    for c in range(3):
        for k in range(total.shape[1]):
            for j in range(SUB):
                start = (k * SUB + j) * LANES
                out[c : c + 1, start : start + LANES] = total[c, k, j : j + 1, :]


def call(kernel, outs, *args, scratch=(), in_specs=None, micros=1, alias=None):
    many = isinstance(outs, (list, tuple))
    return pl.pallas_call(
        kernel,
        out_shape=outs,
        in_specs=in_specs or [VMEM] * len(args),
        out_specs=[VMEM] * len(outs) if many else VMEM,
        scratch_shapes=list(scratch),
        compiler_params=pltpu.CompilerParams(vmem_limit_bytes=VMEM_LIMIT),
        cost_estimate=pl.CostEstimate(
            flops=0, bytes_accessed=micros * 3_000_000, transcendentals=0
        ),
        input_output_aliases=alias or {},
    )(*args)


def up_pairs(count):
    return [(i, i + 1) for i in range(count - 1)]


def down_pairs(count):
    return [(i + 1, i) for i in range(count - 1)]


def all_sum(value):
    for axis in ("comp", "pencil"):
        count = lax.axis_size(axis)
        bit = 1
        while bit < count:
            other = lax.ppermute(value, axis, [(i, i ^ bit) for i in range(count)])
            value = value + other
            bit *= 2
    count = lax.axis_size("slab")
    bit = 1
    while count // bit > 4:
        value = value + lax.ppermute(value, "slab", [(i, i ^ bit) for i in range(count)])
        bit *= 2
    terms = [value]
    for k in range(1, count // bit):
        terms.append(lax.ppermute(value, "slab", [(i, i ^ (k * bit)) for i in range(count)]))
    return terms


def local(u_start, toughness, crack_label, obs_weight, sensor_cell):
    Z, Y, X = toughness.shape
    slabs, pencils = lax.axis_size("slab"), lax.axis_size("pencil")
    if lax.axis_size("comp") != 2 or Z < 6 or Z % SUB or 8 * Z > LANES:
        raise ValueError("unsupported block")
    merged = pencils == 2
    n = 1 if merged else 2
    shape = jax.ShapeDtypeStruct
    field, vector = shape((Z, Y, X), F32), shape((3, Z, Y, X), F32)
    columns = shape((Y, LANES), F32)
    sensors = sensor_cell.shape[0]
    rows, lanes = Y + 2 * SUB, X + LANES
    y_up, y_down = up_pairs(pencils), down_pairs(pencils)
    y_pairs = [y_up + y_down] if merged else [y_up, y_down]
    margins = [
        shape((3, Z, rows, lanes), F32),
        shape((Z, rows, lanes), F32),
        shape((Z - 2, 6, rows, lanes), F32),
    ]
    scratch = [
        pltpu.VMEM((3, 2, rows, lanes), F32),
        pltpu.VMEM((3, 2, rows, lanes), F32),
        pltpu.VMEM((2, 3, rows, lanes), F32),
    ]
    edges = shape((2, 6, rows, lanes), F32)
    planes = shape((7, Y, X), F32)
    evens = [pair for pair in up_pairs(slabs) + down_pairs(slabs) if min(pair) % 2 == 0]
    odds = [pair for pair in up_pairs(slabs) + down_pairs(slabs) if min(pair) % 2 == 1]
    swap = [(0, 1), (1, 0)]
    weight = obs_weight.reshape(Z * Y, sensors)
    hbm = pl.BlockSpec(memory_space=pltpu.HBM)
    starts = [
        pltpu.with_memory_space_constraint(value, pltpu.HBM) for value in (u_start, crack_label)
    ]
    moved, damage, to_first, to_second = call(
        load_kernel,
        [vector, field, planes, planes],
        *starts,
        scratch=[pltpu.VMEM((Z, Y, X), jnp.int32), pltpu.SemaphoreType.DMA((4,))],
        in_specs=[hbm, hbm],
    )
    cols = call(columns_kernel, columns, moved, damage, to_first)
    for step in range(2):
        last = step == 1
        first = lax.ppermute(to_first, "slab", evens)
        second = lax.ppermute(to_second, "slab", odds)
        xh = lax.ppermute(cols, "comp", swap)
        out = call(
            functools.partial(rows_kernel, merged), [shape((8, Z, X), F32)] * n, moved, damage, xh
        )
        ys = [lax.ppermute(y, "pencil", pairs) for y, pairs in zip(out, y_pairs)]
        after = [out[0]]
        if last:
            picks = call(
                functools.partial(picks_kernel, Z, Y),
                shape((Z * Y, sensors), jnp.bfloat16),
                sensor_cell.reshape(1, sensors),
                weight,
                out[0],
            )
            after.append(picks)
        inner_outs = margins if last else margins + [shape((Z - 2, Y, X), F32)]
        middle = call(
            functools.partial(middle_kernel, last), inner_outs, moved, damage, toughness, xh, *after
        )

        def run_inner(after):
            args = [toughness, ys[0], ys[-1], after]
            return call(
                functools.partial(inner_kernel, merged),
                inner_outs,
                *args,
                *middle,
                micros=2,
                alias={len(args) + k: k for k in range(len(inner_outs))},
            )

        if last:
            inner = run_inner(xh)
        corner_rows = call(
            functools.partial(corner_rows_kernel, merged),
            [shape((SUB, X), F32)] * n,
            first,
            second,
            inner[2] if last else middle[2],
        )
        corner_columns = call(corner_columns_kernel, columns, first, second, corner_rows[0])
        if not last:
            inner = run_inner(corner_columns)
        U, D, S = inner[:3]
        inner_moved, *inner_sums = call(
            functools.partial(moved_kernel, last),
            [shape((3, Z - 4, Y, X), F32)] + ([shape((SUB, (Z - 4) * Y), F32)] if last else []),
            moved,
            S,
            corner_columns,
            scratch=[pltpu.VMEM((3, (Z - 4) * Y, LANES), F32)] if last else [],
        )
        crows = [lax.ppermute(y, "pencil", pairs) for y, pairs in zip(corner_rows, y_pairs)]
        ccols = lax.ppermute(corner_columns, "comp", swap)
        extra = shape((3, 2 * Y, LANES), F32) if last else shape((2, Y, X), F32)
        E, near_moved, near = call(
            functools.partial(edge_kernel, last),
            [edges, shape((3, 2, Y, X), F32), extra],
            moved,
            S,
            U,
            D,
            toughness,
            first,
            second,
        )
        args = [moved, first, second, crows[0], crows[-1], ccols, U, D, S, E]
        if last:
            _, edge_moved, part = call(
                functools.partial(outer_kernel, merged, True),
                [
                    edges,
                    shape((3, 2, Y, X), F32),
                    shape((3, sensors // (SUB * LANES), SUB, LANES), F32),
                ],
                *args,
                *inner_sums,
                near,
                weight,
                picks,
                scratch=scratch + [pltpu.VMEM((3, 4 * Y, LANES), F32)],
                alias={9: 0},
            )
            damage = call(damage_kernel, field, U, D, toughness, first, second, part, micros=2)
            moved = call(fields_kernel, vector, inner_moved, near_moved, edge_moved)
        else:
            _, moved, damage, cols, to_first, to_second = call(
                functools.partial(outer_kernel, merged, False),
                [edges, vector, field, columns, planes, planes],
                *args,
                inner_moved,
                near_moved,
                inner[3],
                near,
                scratch=scratch,
                alias={9: 0},
            )
    terms = all_sum(part)
    readings = call(finish_kernel, shape((3, sensors), F32), *terms)
    return moved, damage, readings


def solution(mesh):
    return jax.shard_map(
        local,
        mesh=mesh,
        in_specs=(
            P(None, ("groups", "slab"), "pencil", "comp"),
            P(("groups", "slab"), "pencil", "comp"),
            P(("groups", "slab"), "pencil", "comp"),
            P("slab", "pencil", "comp", None),
            P(),
        ),
        out_specs=(
            P(None, ("groups", "slab"), "pencil", "comp"),
            P(("groups", "slab"), "pencil", "comp"),
            P(None, "groups"),
        ),
        check_vma=False,
    )
```

```python
import functools

import jax
import jax.numpy as jnp
from jax import lax
from jax.experimental import pallas as pl
from jax.experimental.pallas import tpu as pltpu
from jax.sharding import PartitionSpec as P


SHEAR_MODULUS = 1.0
LAME_FIRST = 1.5
RESIDUAL_STIFF = 0.001
TIME_DISP = 0.15
TIME_DAMAGE = 0.08
DAMAGE_LEVEL = 0.45
POINT_GAIN = 8.0
LANES = 128
SUB = 8
COS_THIRD = (
    0.5000000037331834,
    0.5773496613984853,
    -0.11109449276880777,
    0.05327935086024303,
    -0.031925412185213546,
    0.01960032102518762,
    -0.010237508432464154,
    0.003654119632233793,
    -0.0006260453394989179,
)
F32 = jnp.float32
VMEM_LIMIT = 24 * 1024 * 1024
VMEM = pl.BlockSpec(memory_space=pltpu.VMEM)


def positive_square_sum(m00, m11, m22, m01, m02, m12):
    mean = (m00 + m11 + m22) * (1.0 / 3.0)
    b00, b11, b22 = m00 - mean, m11 - mean, m22 - mean
    s01, s02, s12 = m01 * m01, m02 * m02, m12 * m12
    p2 = (b00 * b00 + b11 * b11 + b22 * b22) * (1.0 / 6.0) + (s01 + s02 + s12) * (1.0 / 3.0)
    det = b00 * (b11 * b22 - s12) + 2.0 * (m01 * m02) * m12 - b11 * s02 - b22 * s01
    mean2 = mean * mean
    whole = mean * (mean2 - 3.0 * p2) + det
    up = whole >= 0.0
    safe = jnp.maximum(p2, 1e-24)
    inv = lax.rsqrt(safe)
    p = safe * inv
    half = 0.25 * (det * inv) * (inv * inv)
    half = jnp.where(up, half, -half) + 0.5
    half = jnp.minimum(jnp.maximum(half, 0.0), 1.0)
    t = jnp.sqrt(half)
    c = jnp.full_like(t, COS_THIRD[-1])
    for value in COS_THIRD[-2::-1]:
        c = c * t + value
    pc = p * c
    lead = jnp.where(up, mean, -mean)
    largest = lead + 2.0 * pc
    square = largest * largest
    norm = 6.0 * p2 + 3.0 * mean2
    rest = lead - pc
    return jnp.where(
        up, jnp.where(rest > 0.0, norm, square), jnp.where(rest < 0.0, norm - square, 0.0)
    )


def sides(merged, fn):
    if merged:
        return [jnp.where(lax.axis_index("pencil") == 0, fn(1), fn(-1))]
    return [fn(1), fn(-1)]


def is_left():
    return lax.axis_index("comp") == 0


def pack_columns(tiles, out):
    Y = out.shape[0]
    left = is_left()
    lane = lax.broadcasted_iota(jnp.int32, (Y, LANES), 1)
    slot = jnp.where(left, (lane + 2) // 2 % (LANES // 2), lane // 2)
    acc = jnp.zeros((Y, LANES), F32)
    for entry, plane in enumerate(tiles):
        X = plane.shape[1]
        tile = jnp.where(left, plane[:, X - LANES : X], plane[:, 0:LANES])
        turned = pltpu.roll(tile, 2 * entry, 1) if entry else tile
        acc = jnp.where(slot == entry, turned, acc)
    out[...] = jnp.where(left, pltpu.roll(acc, 2, 1), acc)


def put_columns(u, d, out):
    Z = d.shape[0]
    pack_columns([u.at[c, z] for c in range(3) for z in range(Z)] + [d.at[z] for z in range(Z)], out)


def is_even():
    return lax.axis_index("slab") % 2 == 0


def put_planes(u, d, first, second):
    _, Z, _, _ = u.shape
    even = is_even()
    for c in range(3):
        up, down = u[c, Z - 2 : Z], u[c, 0:2]
        first[2 * c : 2 * c + 2] = jnp.where(even, up, down)
        second[2 * c : 2 * c + 2] = jnp.where(even, down, up)
    up, down = d[Z - 1], d[0]
    first[6] = jnp.where(even, up, down)
    second[6] = jnp.where(even, down, up)


def plane_readers(first, second):
    even = is_even()

    def low(*at):
        return jnp.where(even, second[at], first[at])

    def high(*at):
        return jnp.where(even, first[at], second[at])

    return low, high


def column_reader(packet):
    rows = packet.shape[0]
    left = is_left()
    lane = lax.broadcasted_iota(jnp.int32, (rows, LANES), 1)
    inside = jnp.where(left, lane, LANES - 1 - lane) < 2
    packet = jnp.where(left, packet, pltpu.roll(packet, LANES - 2, 1))

    def column(entry):
        shift = (LANES - 2 * entry) % LANES
        turned = pltpu.roll(packet, shift, 1) if shift else packet
        return jnp.where(inside, turned, 0.0)

    return column


def load_kernel(u_hbm, label_hbm, u, d, first, second, label, sems):
    copies = [pltpu.make_async_copy(u_hbm.at[c], u.at[c], sems.at[c]) for c in range(3)]
    copies.append(pltpu.make_async_copy(label_hbm, label, sems.at[3]))
    for copy in copies:
        copy.start()
    copies[3].wait()
    d[...] = DAMAGE_LEVEL * label[...].astype(F32)
    for copy in copies[:3]:
        copy.wait()
    put_planes(u, d, first, second)


def columns_kernel(u, d, first, cols):
    del first
    put_columns(u, d, cols)


def rows_kernel(merged, u, d, xh, *outs):
    _, _, Y, _ = u.shape
    for c in range(3):
        for layer in range(2):
            row = lambda s: u[c, :, Y - 2 + layer if s > 0 else layer, :]
            for ref, value in zip(outs, sides(merged, row)):
                ref[2 * c + layer] = value
    for ref, value in zip(outs, sides(merged, lambda s: d[:, Y - 1 if s > 0 else 0, :])):
        ref[6] = value
    corner = lambda s: xh[Y - 1 : Y, :] if s > 0 else xh[0:1, :]
    for ref, value in zip(outs, sides(merged, corner)):
        ref[7, 0:1, 0:LANES] = value


def near_planes(first, second):
    low, high = plane_readers(first, second)
    return [low(2 * c + 1) for c in range(3)] + [high(2 * c) for c in range(3)]


def corner_rows_kernel(merged, first, second, after, *outs):
    del after
    Y = first.shape[1]
    for k, plane in enumerate(near_planes(first, second)):
        edge = lambda s: plane[Y - 1 : Y, :] if s > 0 else plane[0:1, :]
        for ref, value in zip(outs, sides(merged, edge)):
            ref[k : k + 1, :] = value


def corner_columns_kernel(first, second, after, cols):
    del after
    pack_columns(near_planes(first, second), cols)


def row_keepers(merged):
    if not merged:
        return (lambda value: value), (lambda value: value)
    py = lax.axis_index("pencil")
    return (
        lambda value: jnp.where(py != 0, value, 0.0),
        lambda value: jnp.where(py == 0, value, 0.0),
    )


def lay_out_columns(u, d, xh, U, D):
    _, Z, Y, X = u.shape
    H = SUB
    column = column_reader(xh[...])
    for c in range(3):
        U[c, :, H : H + Y, 0:X] = u[c]
        for z in range(Z):
            U[c, z, H : H + Y, X : X + LANES] = column(c * Z + z)
    D[:, H : H + Y, 0:X] = d[...]
    for z in range(Z):
        D[z, H : H + Y, X : X + LANES] = column(3 * Z + z)


def lay_out_rows(merged, ylo, yhi, U, D):
    Z, X = D.shape[0], ylo.shape[2]
    Y, H = D.shape[1] - 2 * SUB, SUB
    low_of, high_of = row_keepers(merged)
    low_corner = column_reader(low_of(ylo[7, 0:1, 0:LANES]))
    high_corner = column_reader(high_of(yhi[7, 0:1, 0:LANES]))
    for c in range(3):
        for layer in range(2):
            low, high = low_of(ylo[2 * c + layer]), high_of(yhi[2 * c + layer])
            for z in range(Z):
                U[c, z, H - 2 + layer : H - 1 + layer, 0:X] = low[z : z + 1]
                U[c, z, H + Y + layer : H + Y + layer + 1, 0:X] = high[z : z + 1]
        for z in range(Z):
            U[c, z, H - 1 : H, X : X + LANES] = low_corner(c * Z + z)
            U[c, z, H + Y : H + Y + 1, X : X + LANES] = high_corner(c * Z + z)
    low, high = low_of(ylo[6]), high_of(yhi[6])
    for z in range(Z):
        D[z, H - 1 : H, 0:X] = low[z : z + 1]
        D[z, H + Y : H + Y + 1, 0:X] = high[z : z + 1]


def lay_out_face(k, far, near, columns, F):
    Y, X = near(0).shape
    H = SUB
    column = column_reader(columns[...])
    for c in range(3):
        F[c, 0, H : H + Y, 0:X] = far(c)
        F[c, 1, H : H + Y, 0:X] = near(c)
        F[c, 1, H : H + Y, X : X + LANES] = column(3 * k + c)


def lay_out_face_rows(merged, k, low_rows, high_rows, F):
    X = low_rows.shape[1]
    H = SUB
    Y = F.shape[2] - 2 * SUB
    low_of, high_of = row_keepers(merged)
    for c in range(3):
        row = 3 * k + c
        F[c, 1, H - 1 : H, 0:X] = low_of(low_rows[row : row + 1, :])
        F[c, 1, H + Y : H + Y + 1, 0:X] = high_of(high_rows[row : row + 1, :])


def ahead(value):
    return pltpu.roll(value, value.shape[-1] - 1, value.ndim - 1)


def behind(value):
    return pltpu.roll(value, 1, value.ndim - 1)


ZZ, ZY, ZX, YY, YX, XX = range(6)
PAIRS = ((ZZ, ZY, ZX), (ZY, YY, YX), (ZX, YX, XX))


def gradients(at, row, count):
    rows = slice(row, row + count)
    gz, gy, gx = [], [], []
    for c in range(3):
        mid = at(c, 0)
        gz.append(at(c, 1)[rows, :] - at(c, -1)[rows, :])
        gy.append(mid[row + 1 : row + count + 1, :] - mid[row - 1 : row + count - 1, :])
        value = mid[rows, :]
        gx.append(ahead(value) - behind(value))
    return gz, gy, gx


def stiffness(damage):
    keep = 1.0 - damage
    return 0.5 * (keep * keep + RESIDUAL_STIFF)


def energy_of(gz, gy, gx, X):
    cut = lambda value: value[:, 0:X]
    z0, y1, x2 = cut(gz[0]), cut(gy[1]), cut(gx[2])
    mzy = 0.5 * cut(gy[0] + gz[1])
    mzx = 0.5 * cut(gx[0] + gz[2])
    myx = 0.5 * cut(gx[1] + gy[2])
    squares = positive_square_sum(z0, y1, x2, mzy, mzx, myx)
    grow = jnp.maximum(z0 + y1 + x2, 0.0)
    return (0.25 * 0.5 * LAME_FIRST) * (grow * grow) + (0.25 * SHEAR_MODULUS) * squares


def new_damage(mid, below, above, t, energy, tough):
    X = tough.shape[-1]
    r = t * SUB
    value = mid[r : r + SUB, :]
    core = value[:, 0:X]
    lap = (
        below
        + above
        + mid[r + 1 : r + SUB + 1, 0:X]
        + mid[r - 1 : r + SUB - 1, 0:X]
        + (ahead(value) + behind(value))[:, 0:X]
        - 6.0 * core
    )
    return core + TIME_DAMAGE * (2.0 * (1.0 - core) * energy + tough * (lap - core))


def row_stress(at, damage_plane, S, Y, X):
    H = SUB
    for row in (H - 1, H + Y):
        gz, gy, gx = gradients(at, row, 1)
        h = stiffness(damage_plane[row : row + 1, :])
        total = LAME_FIRST * (gz[0] + gy[1] + gx[2])
        for key, value in (
            (ZY, gy[0] + gz[1]),
            (YY, total + 2.0 * gy[1]),
            (YX, gx[1] + gy[2]),
        ):
            S[key, row : row + 1, 0:X] = (h * value)[:, 0:X]


def tile_stress(at, damage_plane, S, t, X):
    rows = slice(t * SUB, t * SUB + SUB)
    gz, gy, gx = gradients(at, t * SUB, SUB)
    h = stiffness(damage_plane[rows, :])
    total = LAME_FIRST * (gz[0] + gy[1] + gx[2])
    S[ZZ, rows, 0:X] = (h * (total + 2.0 * gz[0]))[:, 0:X]
    S[YY, rows, 0:X] = (h * (total + 2.0 * gy[1]))[:, 0:X]
    S[ZY, rows, 0:X] = (h * (gy[0] + gz[1]))[:, 0:X]
    S[ZX, rows, :] = h * (gx[0] + gz[2])
    S[YX, rows, :] = h * (gx[1] + gy[2])
    S[XX, rows, :] = h * (total + 2.0 * gx[2])
    return gz, gy, gx


def side_stress(at, damage_plane, S, tiles, X):
    for t in tiles:
        r = t * SUB
        rows, out = slice(r, r + SUB), slice(X, X + LANES)
        gz, gy, gx = [], [], []
        for c in range(3):
            mid = at(c, 0)
            gz.append(at(c, 1)[rows, out] - at(c, -1)[rows, out])
            gy.append(mid[r + 1 : r + SUB + 1, out] - mid[r - 1 : r + SUB - 1, out])
            value = mid[rows, :]
            gx.append((ahead(value) - behind(value))[:, out])
        h = stiffness(damage_plane[rows, out])
        total = LAME_FIRST * (gz[0] + gy[1] + gx[2])
        S[ZX, rows, out] = h * (gx[0] + gz[2])
        S[YX, rows, out] = h * (gx[1] + gy[2])
        S[XX, rows, out] = h * (total + 2.0 * gx[2])


def face_stress(at, damage, S, tiles, X):
    for t in tiles:
        rows = slice(t * SUB, t * SUB + SUB)
        gz, gy, gx = gradients(at, t * SUB, SUB)
        h = stiffness(damage(slice((t - 1) * SUB, t * SUB)))
        total = LAME_FIRST * (gz[0] + gy[1] + gx[2])
        for key, value in (
            (ZZ, total + 2.0 * gz[0]),
            (ZY, gy[0] + gz[1]),
            (ZX, gx[0] + gz[2]),
        ):
            S[key, rows, 0:X] = h * value[:, 0:X]


def plane_moved(below, mid, above, u_plane, t, X):
    r = t * SUB
    rows = slice(r, r + SUB)
    out = []
    for c in range(3):
        kz, ky, kx = PAIRS[c]
        value = mid[kx, rows, :]
        force = (
            above[kz, rows, 0:X]
            - below[kz, rows, 0:X]
            + mid[ky, r + 1 : r + SUB + 1, 0:X]
            - mid[ky, r - 1 : r + SUB - 1, 0:X]
            + (ahead(value) - behind(value))[:, 0:X]
        )
        out.append(u_plane(c)[(t - 1) * SUB : t * SUB, :] + (0.5 * TIME_DISP) * force)
    return out


def put_folded(pool, start, new):
    for c, value in enumerate(new):
        total = value[:, 0:LANES]
        for k in range(1, value.shape[1] // LANES):
            total = total + value[:, k * LANES : (k + 1) * LANES]
        pool[c, start : start + SUB, :] = total


def sums_of(pool):
    rows = pool.shape[1]
    sub = lax.broadcasted_iota(jnp.int32, (SUB, rows), 0)
    out = jnp.zeros((SUB, rows), F32)
    for c in range(3):
        out = jnp.where(sub == c, jnp.sum(pool[c].T, axis=0, keepdims=True), out)
    return out


def inner_tiles(z, tiles, U, D, S, tough, damage):
    X = tough.shape[2]
    for t in tiles:
        slopes = tile_stress(lambda c, dz: U.at[c, z + dz], D.at[z], S.at[z - 1], t, X)
        if damage:
            rows = slice(t * SUB, t * SUB + SUB)
            own = slice((t - 1) * SUB, t * SUB)
            (out,) = damage
            out[z - 1, own, :] = new_damage(
                D.at[z],
                D[z - 1, rows, 0:X],
                D[z + 1, rows, 0:X],
                t,
                energy_of(*slopes, X),
                tough[z, own, :],
            )


def middle_kernel(last, u, d, tough, xh, *rest):
    U, D, S, *damage = rest[-3 if last else -4 :]
    Z, Y, _ = tough.shape
    lay_out_columns(u, d, xh, U, D)

    @pl.loop(1, Z - 1, unroll=True)
    def _(z):
        inner_tiles(z, range(2, Y // SUB), U, D, S, tough, damage)


def inner_kernel(merged, tough, ylo, yhi, after, *refs):
    del after
    U, D, S, *damage = refs[len(refs) // 2 :]
    Z, Y, X = tough.shape
    lay_out_rows(merged, ylo, yhi, U, D)

    @pl.loop(1, Z - 1, unroll=True)
    def _(z):
        row_stress(lambda c, dz: U.at[c, z + dz], D.at[z], S.at[z - 1], Y, X)
        inner_tiles(z, (1, Y // SUB), U, D, S, tough, damage)


def moved_kernel(last, u, S, after, moved, *more):
    del after
    _, Z, Y, X = u.shape
    for z in range(2, Z - 2):
        for t in range(1, Y // SUB + 1):
            own = slice((t - 1) * SUB, t * SUB)
            new = plane_moved(
                S.at[z - 2], S.at[z - 1], S.at[z], lambda c: u.at[c, z], t, X
            )
            for c in range(3):
                moved[c, z - 2, own, :] = new[c]
            if last:
                put_folded(more[1], (z - 2) * Y + (t - 1) * SUB, new)
    if last:
        sums, pool = more
        sums[...] = sums_of(pool)


def picks_kernel(Z, Y, sensor, weight, after, picks):
    del weight, after
    count = lax.axis_size("comp")
    spread = Y * lax.axis_size("pencil")
    index = lax.broadcasted_iota(jnp.int32, (Z * Y, 1), 0)
    plane = lax.axis_index("slab") * Z + index // Y
    row = lax.axis_index("pencil") * Y + index % Y
    ids = (plane * spread + row) * count + lax.axis_index("comp")
    chunk = 8 * LANES
    for k in range(sensor.shape[1] // chunk):
        cols = slice(k * chunk, (k + 1) * chunk)
        hit = ids == sensor[:, cols]
        picks[:, cols] = jnp.where(hit, POINT_GAIN, 0.0).astype(jnp.bfloat16)


def edge_slopes(U, low, high, z, t, X):
    Z = U.shape[1]
    r = t * SUB
    rows = slice(r, r + SUB)
    own = slice((t - 1) * SUB, t * SUB)
    gz, gy, gx = [], [], []
    for c in range(3):
        below = low(2 * c + 1, own) if z == 0 else U[c, z - 1, rows, 0:X]
        above = high(2 * c, own) if z == Z - 1 else U[c, z + 1, rows, 0:X]
        gz.append(above - below)
        gy.append(U[c, z, r + 1 : r + SUB + 1, 0:X] - U[c, z, r - 1 : r + SUB - 1, 0:X])
        value = U[c, z, rows, :]
        gx.append((ahead(value) - behind(value))[:, 0:X])
    return gz, gy, gx


def edge_damage(D, low, high, z, t, slopes, tough):
    Z, X = D.shape[0], tough.shape[2]
    rows = slice(t * SUB, t * SUB + SUB)
    own = slice((t - 1) * SUB, t * SUB)
    below = low(6, own) if z == 0 else D[z - 1, rows, 0:X]
    above = high(6, own) if z == Z - 1 else D[z + 1, rows, 0:X]
    return new_damage(D.at[z], below, above, t, energy_of(*slopes, X), tough[z, own, :])


def edge_kernel(last, u, inner, U, D, tough, first, second, S, moved, *more):
    Z, Y, X = tough.shape
    pool, damage = (more, ()) if last else ((), more)
    low, high = plane_readers(first, second)
    for k, z in enumerate((0, Z - 1)):
        for t in range(1, Y // SUB + 1):
            rows = slice(t * SUB, t * SUB + SUB)
            gz, gy, gx = edge_slopes(U, low, high, z, t, X)
            h = stiffness(D[z, rows, 0:X])
            total = LAME_FIRST * (gz[0] + gy[1] + gx[2])
            S[k, ZZ, rows, 0:X] = h * (total + 2.0 * gz[0])
            S[k, YY, rows, 0:X] = h * (total + 2.0 * gy[1])
            S[k, XX, rows, 0:X] = h * (total + 2.0 * gx[2])
            S[k, ZY, rows, 0:X] = h * (gy[0] + gz[1])
            S[k, ZX, rows, 0:X] = h * (gx[0] + gz[2])
            S[k, YX, rows, 0:X] = h * (gx[1] + gy[2])
            if damage:
                own = slice((t - 1) * SUB, t * SUB)
                damage[0][k, own, :] = edge_damage(D, low, high, z, t, (gz, gy, gx), tough)
    around = (
        (1, S.at[0], inner.at[0], inner.at[1]),
        (Z - 2, inner.at[Z - 4], inner.at[Z - 3], S.at[1]),
    )
    for k, (z, below, mid, above) in enumerate(around):
        for t in range(1, Y // SUB + 1):
            own = slice((t - 1) * SUB, t * SUB)
            new = plane_moved(below, mid, above, lambda c: u.at[c, z], t, X)
            for c in range(3):
                moved[c, k, own, :] = new[c]
            if last:
                put_folded(pool[0], k * Y + (t - 1) * SUB, new)


def damage_kernel(U, D, tough, first, second, after, damage):
    del after
    Z, Y, X = tough.shape
    low, high = plane_readers(first, second)
    tiles = range(1, Y // SUB + 1)
    for z in (0, Z - 1):
        for t in tiles:
            own = slice((t - 1) * SUB, t * SUB)
            slopes = edge_slopes(U, low, high, z, t, X)
            damage[z, own, :] = edge_damage(D, low, high, z, t, slopes, tough)

    @pl.loop(1, Z - 1, unroll=True)
    def _(z):
        for t in tiles:
            r = t * SUB
            rows = slice(r, r + SUB)
            own = slice((t - 1) * SUB, t * SUB)
            gz, gy, gx = gradients(lambda c, dz: U.at[c, z + dz], r, SUB)
            damage[z, own, :] = new_damage(
                D.at[z],
                D[z - 1, rows, 0:X],
                D[z + 1, rows, 0:X],
                t,
                energy_of(gz, gy, gx, X),
                tough[z, own, :],
            )


def face_planes(low_face, high_face, U):
    Z = U.shape[1]

    def at_plane(z):
        def at(c, dz):
            k = z + dz
            if k < 0:
                return low_face.at[c, 2 + k]
            if k >= Z:
                return high_face.at[c, Z + 1 - k]
            return U.at[c, k]

        return at

    return at_plane


def face_tiles(tiles, u, first, second, U, D, S, E, low_face, high_face, faces, put):
    _, Z, _, X = u.shape
    low, high = plane_readers(first, second)
    at_plane = face_planes(low_face, high_face, U)
    face_stress(at_plane(-1), lambda own: low(6, own), faces.at[0], tiles, X)
    face_stress(at_plane(Z), lambda own: high(6, own), faces.at[1], tiles, X)
    for k, z in enumerate((0, Z - 1)):
        side_stress(at_plane(z), D.at[z], E.at[k], tiles, X)
    around = (
        (0, faces.at[0], E.at[0], S.at[0]),
        (Z - 1, S.at[Z - 3], E.at[1], faces.at[1]),
    )
    for k, (z, below, mid, above) in enumerate(around):
        for t in tiles:
            put(k, t, plane_moved(below, mid, above, lambda c: u.at[c, z], t, X))


def mid_kernel(last, u, first, second, columns, U, D, S, E_in, E, low_face, high_face, faces, *rest):
    del E_in
    moved, *pool = rest
    Y = u.shape[2]
    low, high = plane_readers(first, second)
    lay_out_face(0, lambda c: low(2 * c), lambda c: low(2 * c + 1), columns, low_face)
    lay_out_face(1, lambda c: high(2 * c + 1), lambda c: high(2 * c), columns, high_face)

    def put(k, t, new):
        for c in range(3):
            moved[c, k, (t - 2) * SUB : (t - 1) * SUB, :] = new[c]
        if last:
            put_folded(pool[0], k * (Y - 2 * SUB) + (t - 2) * SUB, new)

    tiles = range(2, Y // SUB)
    face_tiles(tiles, u, first, second, U, D, S, E, low_face, high_face, faces, put)


def outer_kernel(merged, last, *refs):
    rest = list(refs)
    take = lambda k: [rest.pop(0) for _ in range(k)]
    u, first, second, low_rows, high_rows, U, D, S = take(8)
    take(4)
    if last:
        inner_sums, near_pool, mid_pool, weight, picks = take(5)
        E, low_face, high_face, faces, moved, part, pool = take(7)
    else:
        inner_moved, near_moved, mid_moved, inner_damage, near_damage = take(5)
        E, low_face, high_face, faces, moved, damage, cols, to_first, to_second = take(9)
    _, Z, Y, X = u.shape
    count = Y // SUB
    lay_out_face_rows(merged, 0, low_rows, high_rows, low_face)
    lay_out_face_rows(merged, 1, low_rows, high_rows, high_face)
    at_plane = face_planes(low_face, high_face, U)
    for k, z in enumerate((0, Z - 1)):
        row_stress(at_plane(z), D.at[z], E.at[k], Y, X)

    def put(k, t, new):
        own = slice((t - 1) * SUB, t * SUB)
        for c in range(3):
            if last:
                end = 0 if t == 1 else SUB
                moved[c, k, end : end + SUB, :] = new[c]
            else:
                moved[c, k * (Z - 1), own, :] = new[c]
        if last:
            put_folded(pool, 3 * k * Y + (t - 1) * SUB, new)

    face_tiles((1, count), u, first, second, U, D, S, E, low_face, high_face, faces, put)
    middle = Y - 2 * SUB
    if last:
        pool[:, SUB : SUB + middle, :] = mid_pool[:, 0:middle, :]
        pool[:, Y : 3 * Y, :] = near_pool[...]
        pool[:, 3 * Y + SUB : 3 * Y + SUB + middle, :] = mid_pool[:, middle : 2 * middle, :]
        outer_sums = sums_of(pool)
        means = jnp.concatenate(
            [outer_sums[:, 0 : 2 * Y], inner_sums[...], outer_sums[:, 2 * Y : 4 * Y]], axis=1
        )
        means = (means * (1.0 / X)).astype(jnp.bfloat16)
        chunk = 8 * LANES
        sub = lax.broadcasted_iota(jnp.int32, (SUB, LANES), 0)
        for k in range(weight.shape[1] // chunk):
            start = slice(k * chunk, (k + 1) * chunk)
            value = jnp.dot(means, weight[:, start], preferred_element_type=F32)
            value = value + jnp.dot(means, picks[:, start], preferred_element_type=F32)
            for c in range(3):
                tile = jnp.zeros((SUB, LANES), F32)
                for j in range(SUB):
                    piece = value[c : c + 1, j * LANES : (j + 1) * LANES]
                    tile = jnp.where(sub == j, piece, tile)
                part[c, k] = tile
    else:
        for c in range(3):
            for k in range(2):
                moved[c, k * (Z - 1), SUB : SUB + middle, :] = mid_moved[c, k]
            moved[c, 1] = near_moved[c, 0]
            moved[c, 2 : Z - 2] = inner_moved[c]
            moved[c, Z - 2] = near_moved[c, 1]
        damage[0] = near_damage[0]
        damage[1 : Z - 1] = inner_damage[...]
        damage[Z - 1] = near_damage[1]
        put_planes(moved, damage, to_first, to_second)
        put_columns(moved, damage, cols)


def fields_kernel(inner_moved, near_moved, mid_moved, edge_moved, moved):
    _, Z, Y, _ = moved.shape
    for c in range(3):
        for k, z in enumerate((0, Z - 1)):
            moved[c, z, 0:SUB, :] = edge_moved[c, k, 0:SUB, :]
            moved[c, z, SUB : Y - SUB, :] = mid_moved[c, k]
            moved[c, z, Y - SUB : Y, :] = edge_moved[c, k, SUB : 2 * SUB, :]
        moved[c, 1] = near_moved[c, 0]
        moved[c, 2 : Z - 2] = inner_moved[c]
        moved[c, Z - 2] = near_moved[c, 1]


def finish_kernel(*refs):
    out = refs[-1]
    total = refs[0][...]
    for ref in refs[1:-1]:
        total = total + ref[...]
    for c in range(3):
        for k in range(total.shape[1]):
            for j in range(SUB):
                start = (k * SUB + j) * LANES
                out[c : c + 1, start : start + LANES] = total[c, k, j : j + 1, :]


def call(kernel, outs, *args, scratch=(), in_specs=None, micros=1, alias=None):
    many = isinstance(outs, (list, tuple))
    return pl.pallas_call(
        kernel,
        out_shape=outs,
        in_specs=in_specs or [VMEM] * len(args),
        out_specs=[VMEM] * len(outs) if many else VMEM,
        scratch_shapes=list(scratch),
        compiler_params=pltpu.CompilerParams(vmem_limit_bytes=VMEM_LIMIT),
        cost_estimate=pl.CostEstimate(
            flops=0, bytes_accessed=micros * 3_000_000, transcendentals=0
        ),
        input_output_aliases=alias or {},
    )(*args)


def up_pairs(count):
    return [(i, i + 1) for i in range(count - 1)]


def down_pairs(count):
    return [(i + 1, i) for i in range(count - 1)]


def all_sum(value):
    for axis in ("comp", "pencil"):
        count = lax.axis_size(axis)
        bit = 1
        while bit < count:
            other = lax.ppermute(value, axis, [(i, i ^ bit) for i in range(count)])
            value = value + other
            bit *= 2
    count = lax.axis_size("slab")
    bit = 1
    while count // bit > 4:
        value = value + lax.ppermute(value, "slab", [(i, i ^ bit) for i in range(count)])
        bit *= 2
    terms = [value]
    for k in range(1, count // bit):
        terms.append(lax.ppermute(value, "slab", [(i, i ^ (k * bit)) for i in range(count)]))
    return terms


def local(u_start, toughness, crack_label, obs_weight, sensor_cell):
    Z, Y, X = toughness.shape
    slabs, pencils = lax.axis_size("slab"), lax.axis_size("pencil")
    if lax.axis_size("comp") != 2 or Z < 6 or Z % SUB or 8 * Z > LANES or Y < 3 * SUB:
        raise ValueError("unsupported block")
    merged = pencils == 2
    n = 1 if merged else 2
    shape = jax.ShapeDtypeStruct
    field, vector = shape((Z, Y, X), F32), shape((3, Z, Y, X), F32)
    columns = shape((Y, LANES), F32)
    sensors = sensor_cell.shape[0]
    rows, lanes = Y + 2 * SUB, X + LANES
    y_up, y_down = up_pairs(pencils), down_pairs(pencils)
    y_pairs = [y_up + y_down] if merged else [y_up, y_down]
    margins = [
        shape((3, Z, rows, lanes), F32),
        shape((Z, rows, lanes), F32),
        shape((Z - 2, 6, rows, lanes), F32),
    ]
    face_fields = [shape((3, 2, rows, lanes), F32)] * 2 + [shape((2, 3, rows, lanes), F32)]
    edges = shape((2, 6, rows, lanes), F32)
    planes = shape((7, Y, X), F32)
    evens = [pair for pair in up_pairs(slabs) + down_pairs(slabs) if min(pair) % 2 == 0]
    odds = [pair for pair in up_pairs(slabs) + down_pairs(slabs) if min(pair) % 2 == 1]
    swap = [(0, 1), (1, 0)]
    weight = obs_weight.reshape(Z * Y, sensors)
    hbm = pl.BlockSpec(memory_space=pltpu.HBM)
    starts = [
        pltpu.with_memory_space_constraint(value, pltpu.HBM) for value in (u_start, crack_label)
    ]
    moved, damage, to_first, to_second = call(
        load_kernel,
        [vector, field, planes, planes],
        *starts,
        scratch=[pltpu.VMEM((Z, Y, X), jnp.int32), pltpu.SemaphoreType.DMA((4,))],
        in_specs=[hbm, hbm],
    )
    cols = call(columns_kernel, columns, moved, damage, to_first)
    for step in range(2):
        last = step == 1
        first = lax.ppermute(to_first, "slab", evens)
        second = lax.ppermute(to_second, "slab", odds)
        xh = lax.ppermute(cols, "comp", swap)
        out = call(
            functools.partial(rows_kernel, merged), [shape((8, Z, X), F32)] * n, moved, damage, xh
        )
        ys = [lax.ppermute(y, "pencil", pairs) for y, pairs in zip(out, y_pairs)]
        after = [out[0]]
        if last:
            picks = call(
                functools.partial(picks_kernel, Z, Y),
                shape((Z * Y, sensors), jnp.bfloat16),
                sensor_cell.reshape(1, sensors),
                weight,
                out[0],
            )
            after.append(picks)
        inner_outs = margins if last else margins + [shape((Z - 2, Y, X), F32)]
        middle = call(
            functools.partial(middle_kernel, last), inner_outs, moved, damage, toughness, xh, *after
        )

        def run_inner(after):
            args = [toughness, ys[0], ys[-1], after]
            return call(
                functools.partial(inner_kernel, merged),
                inner_outs,
                *args,
                *middle,
                micros=2,
                alias={len(args) + k: k for k in range(len(inner_outs))},
            )

        corner_rows = call(
            functools.partial(corner_rows_kernel, merged),
            [shape((SUB, X), F32)] * n,
            first,
            second,
            middle[2],
        )
        corner_columns = call(corner_columns_kernel, columns, first, second, corner_rows[0])
        inner = run_inner(corner_columns)
        U, D, S = inner[:3]
        inner_moved, *inner_sums = call(
            functools.partial(moved_kernel, last),
            [shape((3, Z - 4, Y, X), F32)] + ([shape((SUB, (Z - 4) * Y), F32)] if last else []),
            moved,
            S,
            corner_columns,
            scratch=[pltpu.VMEM((3, (Z - 4) * Y, LANES), F32)] if last else [],
        )
        crows = [lax.ppermute(y, "pencil", pairs) for y, pairs in zip(corner_rows, y_pairs)]
        ccols = lax.ppermute(corner_columns, "comp", swap)
        extra = shape((3, 2 * Y, LANES), F32) if last else shape((2, Y, X), F32)
        E, near_moved, near = call(
            functools.partial(edge_kernel, last),
            [edges, shape((3, 2, Y, X), F32), extra],
            moved,
            S,
            U,
            D,
            toughness,
            first,
            second,
        )
        middle_rows = Y - 2 * SUB
        E, low_face, high_face, faces, mid_moved, *mid_pool = call(
            functools.partial(mid_kernel, last),
            [edges, *face_fields, shape((3, 2, middle_rows, X), F32)]
            + ([shape((3, 2 * middle_rows, LANES), F32)] if last else []),
            moved,
            first,
            second,
            ccols,
            U,
            D,
            S,
            E,
            alias={7: 0},
        )
        args = [moved, first, second, crows[0], crows[-1], U, D, S]
        laid = [E, low_face, high_face, faces]
        laid_alias = {len(args) + k: k for k in range(4)}
        if last:
            *_, edge_moved, part = call(
                functools.partial(outer_kernel, merged, True),
                [
                    edges,
                    *face_fields,
                    shape((3, 2, 2 * SUB, X), F32),
                    shape((3, sensors // (SUB * LANES), SUB, LANES), F32),
                ],
                *args,
                *laid,
                *inner_sums,
                near,
                *mid_pool,
                weight,
                picks,
                scratch=[pltpu.VMEM((3, 4 * Y, LANES), F32)],
                alias=laid_alias,
            )
            damage = call(damage_kernel, field, U, D, toughness, first, second, part, micros=2)
            moved = call(fields_kernel, vector, inner_moved, near_moved, mid_moved, edge_moved)
        else:
            *_, moved, damage, cols, to_first, to_second = call(
                functools.partial(outer_kernel, merged, False),
                [edges, *face_fields, vector, field, columns, planes, planes],
                *args,
                *laid,
                inner_moved,
                near_moved,
                mid_moved,
                inner[3],
                near,
                alias=laid_alias,
            )
    terms = all_sum(part)
    readings = call(finish_kernel, shape((3, sensors), F32), *terms)
    return moved, damage, readings


def solution(mesh):
    return jax.shard_map(
        local,
        mesh=mesh,
        in_specs=(
            P(None, ("groups", "slab"), "pencil", "comp"),
            P(("groups", "slab"), "pencil", "comp"),
            P(("groups", "slab"), "pencil", "comp"),
            P("slab", "pencil", "comp", None),
            P(),
        ),
        out_specs=(
            P(None, ("groups", "slab"), "pencil", "comp"),
            P(("groups", "slab"), "pencil", "comp"),
            P(None, "groups"),
        ),
        check_vma=False,
    )
```
